32 devices in a mesh: ctx: 8 (over y, x, core), ch: 4 (over z).
Axes of the slice: x: 2, y: 2, z: 4, core: 2. Of those that a mesh axis runs over, the one named last changes fastest.
Arguments:
- queries: bfloat16 [8192, 2048], P('ch', 'ctx'), may hold values from -6 to 6
- keys: bfloat16 [8192, 2048], P('ch', 'ctx'), may hold values from -6 to 6
- values: bfloat16 [8192, 2048], P('ch', 'ctx'), may hold values from -6 to 6
- short_taps: float32 [3, 7, 8192], P(None, None, 'ch'), may hold values from -2 to 2
- long_filter: bfloat16 [4, 2048, 2048], P('ch', 'ctx'), may hold values from -1.5 to 1.5
- skip_gain: float32 [4, 2048], P('ch', 'ctx'), may hold values from 0.5 to 1.5
Outputs:
- mixed: bfloat16 [8192, 2048], P('ch', 'ctx')
The draws below stay inside these ranges and needn't reach their ends.
All inputs are finite; a program needn't handle non-finite values.
Results may differ from the reference program's by a relative error of at most 0.01.
Values may be sent and summed in bfloat16 or wider, within the bound.
A program may use at most 64 MiB of HBM per device.

```python
import math
import jax
import jax.numpy as jnp
from jax import lax

D = 8192
TAPS = 7
TOKENS = 2048
GROUPS = 4
GROUP_WIDTH = 2048


def draw_long_filter(key, part):
    key_noise, key_rate = jax.random.split(jax.random.fold_in(key, 11))
    noise = jnp.clip(jax.random.normal(key_noise, (GROUPS, GROUP_WIDTH, TOKENS), jnp.float32), -6.0, 6.0)
    low = math.log(0.5 / TOKENS)
    high = math.log(1.0 / 30.0)
    rates = jnp.exp(jax.random.uniform(key_rate, (GROUPS, GROUP_WIDTH, 1), jnp.float32, low, high))
    positions = jnp.arange(TOKENS, dtype=jnp.float32)
    scales = jnp.sqrt(1.0 - jnp.exp(-2.0 * rates))
    return (noise * scales * jnp.exp(-rates * positions)).astype(jnp.bfloat16)


def level_of(own_key, dims, cuts, smallest, high):
    def one(dim, parts):
        steps = jax.random.uniform(jax.random.fold_in(jax.random.fold_in(own_key, 6), dim), (parts,), jnp.float32, smallest / len(cuts), high / len(cuts))
        return jnp.repeat(jnp.exp(steps), dims[dim] // parts).reshape((-1,) + (1,) * (len(dims) - dim - 1))

    loudness = one(*cuts[0])
    for cut in cuts[1:]:
        loudness = loudness * one(*cut)
    return loudness


def gaussian(key, dims, width, most, cuts=(), kind=jnp.bfloat16):
    factor_of = level_of(key, dims, cuts, -0.22, 0.18) if cuts else 1.0
    result = jax.random.normal(key, dims, jnp.float32) * width * factor_of
    return jnp.minimum(jnp.maximum(result, -most), most).astype(kind)


def setup_inputs(seed: int = 0) -> dict:
    splits = jax.random.split(jax.random.key(seed), 7)
    return {
        "queries": gaussian(splits[0], (D, TOKENS), 1.0, 6.0, ((0, 4), (1, 8))),
        "keys": gaussian(splits[1], (D, TOKENS), 1.0, 6.0, ((0, 4), (1, 8))),
        "values": gaussian(splits[2], (D, TOKENS), 1.0, 6.0, ((0, 4), (1, 8))),
        "short_taps": gaussian(splits[3], (3, TAPS, D), TAPS ** -0.5, 2.0, ((2, 4),), jnp.float32),
        "long_filter": draw_long_filter(jax.random.fold_in(splits[6], 71), 0),
        "skip_gain": jnp.clip(0.5 + 1.0 * jax.random.uniform(splits[5], (GROUPS, GROUP_WIDTH), jnp.float32) ** level_of(splits[5], (GROUPS, GROUP_WIDTH), ((0, 4), (1, 8)), -0.2, 0.2), 0.5, 1.5),
    }


def short_conv(source, taps):
    rim = taps.shape[0] - 1
    length = source.shape[1]
    padded = jnp.pad(source.astype(jnp.float32), ((0, 0), (rim, 0)))
    total = jnp.zeros(source.shape, jnp.float32)
    for shift_j in range(taps.shape[0]):
        total = total + taps[shift_j][:, None] * padded[:, rim - shift_j:rim - shift_j + length]
    return total


def reference(queries, keys, values, short_taps, long_filter, skip_gain):
    q_short = short_conv(queries, short_taps[0]).astype(jnp.bfloat16)
    gated = (short_conv(keys, short_taps[1]) * short_conv(values, short_taps[2])).astype(jnp.bfloat16)
    filters = long_filter.reshape(D, TOKENS)
    skips = skip_gain.reshape(D)
    block = math.gcd(D, 512)
    count = D // block
    padded_len = 2 * TOKENS

    def one_block(pair):
        sig, filt = pair
        spec = jnp.fft.rfft(sig.astype(jnp.float32), n=padded_len, axis=1) * jnp.fft.rfft(filt.astype(jnp.float32), n=padded_len, axis=1)
        return jnp.fft.irfft(spec, n=padded_len, axis=1)[:, :TOKENS]

    conv = lax.map(one_block, (gated.reshape(count, block, TOKENS), filters.reshape(count, block, TOKENS)))
    long_out = (conv.reshape(D, TOKENS) + skips[:, None] * gated.astype(jnp.float32)).astype(jnp.bfloat16)
    return (q_short.astype(jnp.float32) * long_out.astype(jnp.float32)).astype(jnp.bfloat16)
```

```python
import functools
import math

import jax
import jax.numpy as jnp
import ml_dtypes
import numpy as np
from jax import lax
from jax.experimental import pallas as pl
from jax.experimental.pallas import tpu as pltpu
from jax.sharding import PartitionSpec as P

MESH = pl.DeviceIdType.MESH
LANES = 128
SLOT = 8
F32 = jnp.float32
BF16 = jnp.bfloat16


def leaf_angles(count, theta):
    if count == 1:
        return [theta]
    return leaf_angles(count // 2, theta / 2) + leaf_angles(count // 2, theta / 2 + math.pi)


def circle_tables():
    place = np.arange(LANES, dtype=np.float64)
    angle = place[:, None] * place[None, :] * (2.0 * math.pi / LANES)
    cos, sin = np.cos(angle), np.sin(angle)
    there = np.block([[cos, -sin], [sin, cos]])
    return np.stack([there, there.T]).astype(ml_dtypes.bfloat16)


def twist_columns(count):
    roots = np.array(leaf_angles(count, 0.0)) + math.pi / (2 * count)
    angle = np.arange(LANES)[:, None] * roots[None, :] / LANES
    return np.concatenate([np.cos(angle), np.sin(angle)], axis=1).astype(np.float32)


def turn(re, im, angle):
    eighth = round(angle / (math.pi / 4))
    if abs(angle - eighth * math.pi / 4) > 1e-9:
        cos, sin = math.cos(angle), math.sin(angle)
        return cos * re - sin * im, cos * im + sin * re
    eighth %= 8
    if eighth % 2:
        re, im = math.sqrt(0.5) * (re - im), math.sqrt(0.5) * (re + im)
    return [(re, im), (-im, re), (-re, -im), (im, -re)][eighth // 2]


def split_forward(coefs, theta, first, emit):
    count = len(coefs)
    if count == 1:
        emit(first, *coefs[0])
        return
    half = count // 2
    plus, minus = [], []
    for (lo_re, lo_im), high in zip(coefs[:half], coefs[half:]):
        hi_re, hi_im = turn(*high, theta / 2)
        plus.append((lo_re + hi_re, lo_im + hi_im))
        minus.append((lo_re - hi_re, lo_im - hi_im))
    split_forward(plus, theta / 2, first, emit)
    split_forward(minus, theta / 2 + math.pi, first + half, emit)


def split_inverse(fetch, count, theta, first):
    if count == 1:
        return [fetch(first)]
    half = count // 2
    plus = split_inverse(fetch, half, theta / 2, first)
    minus = split_inverse(fetch, half, theta / 2 + math.pi, first + half)
    low, high = [], []
    for (p_re, p_im), (m_re, m_im) in zip(plus, minus):
        low.append((p_re + m_re, p_im + m_im))
        high.append(turn(p_re - m_re, p_im - m_im, -theta / 2))
    return low + high


def across(eye, block):
    return lax.dot_general(eye, block, (((1,), (1,)), ((), ())), preferred_element_type=F32)


def crossed(a, b, count):
    total, place = 0, 1
    while place < count:
        total = total + lax.rem(lax.div(a, place) + lax.div(b, place), 2) * place
        place *= 2
    return total


def wide_kernel(
    n,
    q_hbm, k_hbm, v_hbm, taps_hbm, filt_hbm, gain_hbm, table_hbm, twist_hbm,
    out_ref,
    source, taps_ref, filt_ref, gain_ref, table_ref, twist_ref,
    eye, tails, halo, turned, rim, gated, recv, spec, h_spec, ret, filt_rows, twist,
    load_sem, q_sem, side_sem, halo_send, halo_recv,
    rim_send, rim_recv, in_send, in_recv, in_own, out_send, out_recv, out_own,
):
    me = lax.axis_index("ctx")
    width, tok = q_hbm.shape
    chan, length = filt_hbm.shape
    lanes = LANES
    chunks = chan // lanes
    reach = taps_hbm.shape[1]
    blocks = length // LANES
    tiles = tok // LANES
    pairs = n // 2
    step = 16
    edge = 16
    part = 64

    barrier = pltpu.get_barrier_semaphore()
    for d in range(1, n):
        pl.semaphore_signal(
            barrier, inc=1, device_id={"ctx": lax.rem(me + d, n)}, device_id_type=MESH
        )

    def peer_of(j):
        return crossed(me, n - 1 - j, n)

    def peer_rows(peer, c):
        return pl.ds(pl.multiple_of(peer * chan + c * lanes, lanes), lanes)

    def load(w, c, j):
        ref = (q_hbm, k_hbm, v_hbm)[w]
        at = peer_rows(peer_of(j), c)
        return pltpu.make_async_copy(ref.at[at, :], source.at[w, at, :], load_sem.at[w - 1, c, j])

    side = [
        pltpu.make_async_copy(taps_hbm, taps_ref, side_sem.at[0]),
        pltpu.make_async_copy(filt_hbm, filt_ref, side_sem.at[1]),
        pltpu.make_async_copy(gain_hbm, gain_ref, side_sem.at[2]),
        pltpu.make_async_copy(table_hbm, table_ref, side_sem.at[3]),
        pltpu.make_async_copy(twist_hbm, twist_ref, side_sem.at[4]),
    ]
    load_q = pltpu.make_async_copy(q_hbm, source.at[0], q_sem)

    def load_step(j, c):
        load(1, c, j).start()
        load(2, c, j).start()
        return c

    def load_wait(j, c):
        load(1, c, j).wait()
        load(2, c, j).wait()
        return c

    lax.fori_loop(0, 2, load_step, 0)
    side[0].start()
    lax.fori_loop(2, n, load_step, 0)
    for c in range(1, chunks):
        lax.fori_loop(0, n, load_step, c)
    for i in range(1, len(side)):
        side[i].start()
    load_q.start()

    size = eye.shape[0]
    row = lax.broadcasted_iota(jnp.int32, (size, size), 0)
    col = lax.broadcasted_iota(jnp.int32, (size, size), 1)
    eye[...] = (row == col).astype(F32).astype(BF16)
    pick_row = lax.broadcasted_iota(jnp.int32, (SLOT, LANES), 0) + (LANES - SLOT)
    pick = (pick_row == lax.broadcasted_iota(jnp.int32, (SLOT, LANES), 1)).astype(F32).astype(BF16)

    def find_tails(w):
        def one(p, _):
            at = pl.ds(pl.multiple_of(p * chan, chan), chan)
            tails[w, p] = across(pick, source[w, at, tok - LANES :]).astype(BF16)
            return 0

        lax.fori_loop(0, n, one, 0, unroll=4)

    def halo_copy(part_of):
        at = slice(1, 3) if part_of == 0 else slice(0, 1)
        return pltpu.make_async_remote_copy(
            src_ref=tails.at[at], dst_ref=halo.at[at],
            send_sem=halo_send.at[part_of], recv_sem=halo_recv.at[part_of],
            device_id={"ctx": lax.rem(me + 1, n)}, device_id_type=MESH,
        )

    def halo_start(part_of):
        @pl.when(me < n - 1)
        def _():
            halo_copy(part_of).start()

    def halo_wait(part_of):
        @pl.when(me < n - 1)
        def _():
            halo_copy(part_of).wait_send()

        @pl.when(me > 0)
        def _():
            halo_copy(part_of).wait_recv()

    def chunk_lanes(c):
        return slice(c * lanes, (c + 1) * lanes)

    def leaf_lanes(leaf):
        return slice((leaf % 2) * LANES, (leaf % 2) * LANES + lanes)

    def set_halo(w, peer, c, ref, *index):
        ref[(*index, slice(0, SLOT), slice(None))] = jnp.zeros((SLOT, lanes), F32)

        @pl.when(me > 0)
        def _():
            ref[(*index, slice(0, SLOT), slice(None))] = halo[w, peer, :, chunk_lanes(c)].astype(F32)

    def turn_pair(first, pair, c, whole):
        block = jnp.concatenate([source[w, peer_rows(peer, c), :] for w, peer in pair], axis=0)
        both = across(eye[:tok, :tok], block)
        for i, (w, peer) in enumerate(pair):
            rows = both[:, i * lanes : (i + 1) * lanes]
            turned[first + i, SLOT:, :] = rows
            if whole:
                set_halo(w, peer, c, turned, first + i)
            else:
                rim[w - 1, peer, SLOT:, :] = rows[:edge]
        return [taps_ref[w, :, peer_rows(peer, c)] for w, peer in pair]

    def sums_of(ref, index, taps, start, count):
        total = None
        for j in range(reach):
            at = slice(SLOT - j + start, SLOT - j + start + count)
            term = taps[j : j + 1, :] * ref[(*index, at, slice(None))]
            total = term if total is None else total + term
        return total

    def spans(first):
        marks = [first] + list(range((first // part + 1) * part, tok, part)) + [tok]
        return list(zip(marks[:-1], marks[1:]))

    def gate_pair(peers, c, whole):
        taps = [turn_pair(2 * i, [(1, p), (2, p)], c, whole) for i, p in enumerate(peers)]
        for i, p in enumerate(peers):
            for start, stop in spans(0 if whole else edge):
                count = stop - start
                product = sums_of(turned, (2 * i,), taps[i][0], start, count) * sums_of(
                    turned, (2 * i + 1,), taps[i][1], start, count
                )
                gated[c, p, start:stop, :] = product.astype(BF16)

    def in_copy(c, j):
        peer = peer_of(j)
        at = slice(0 if c else edge, tok)
        return pltpu.make_async_remote_copy(
            src_ref=gated.at[c, peer, at, :], dst_ref=recv.at[c, me, at, :],
            send_sem=in_send.at[c, j], recv_sem=in_recv.at[c, j],
            device_id={"ctx": peer}, device_id_type=MESH,
        )

    def rim_copy(j):
        peer = peer_of(j)
        return pltpu.make_async_remote_copy(
            src_ref=gated.at[0, peer, 0:edge, :], dst_ref=recv.at[0, me, 0:edge, :],
            send_sem=rim_send.at[j], recv_sem=rim_recv.at[j],
            device_id={"ctx": peer}, device_id_type=MESH,
        )

    def own_in(c):
        return pltpu.make_async_copy(gated.at[c, me], recv.at[c, me], in_own.at[c])

    def out_copy(c, j):
        peer = peer_of(j)
        return pltpu.make_async_remote_copy(
            src_ref=recv.at[c, peer], dst_ref=ret.at[c, me],
            send_sem=out_send.at[c, j], recv_sem=out_recv.at[c, j],
            device_id={"ctx": peer}, device_id_type=MESH,
        )

    def own_out(c):
        return pltpu.make_async_copy(recv.at[c, me], ret.at[c, me], out_own.at[c])

    def gate_chunk(c):
        def one(i, _):
            if c == 0:
                load_wait(2 * i, c)
                load_wait(2 * i + 1, c)
            gate_pair([peer_of(2 * i), peer_of(2 * i + 1)], c, c > 0)

            @pl.when(i > 0)
            def _():
                in_copy(c, 2 * i - 2).start()
                in_copy(c, 2 * i - 1).start()

            return 0

        if c == 0:
            one_first(one)
        else:
            lax.fori_loop(0, pairs, one, 0)
        in_copy(c, n - 2).start()

    def one_first(one):
        side[0].wait()
        pl.semaphore_wait(barrier, n - 1)
        lax.fori_loop(0, pairs, one, 0)

    gate_chunk(0)
    for c in range(1, chunks):
        lax.fori_loop(0, n, load_wait, c)
    find_tails(1)
    find_tails(2)
    halo_start(0)
    halo_wait(0)

    def rim_step(i, _):
        for p in (peer_of(2 * i), peer_of(2 * i + 1)):
            for w in (1, 2):
                set_halo(w, p, 0, rim, w - 1, p)
            gated[0, p, :edge, :] = (
                sums_of(rim, (0, p), taps_ref[1, :, peer_rows(p, 0)], 0, edge)
                * sums_of(rim, (1, p), taps_ref[2, :, peer_rows(p, 0)], 0, edge)
            ).astype(BF16)
        return 0

    lax.fori_loop(0, pairs, rim_step, 0)

    def rim_start(j, _):
        rim_copy(j).start()
        return 0

    lax.fori_loop(0, n - 1, rim_start, 0)
    own_in(0).start()

    for c in range(1, chunks):
        gate_chunk(c)
        own_in(c).start()

    load_q.wait()
    find_tails(0)
    halo_start(1)

    for i in range(1, len(side)):
        side[i].wait()
    for a in range(blocks):
        filt_rows[a // tiles, (a % tiles) * LANES : (a % tiles + 1) * LANES, :] = across(
            eye[:LANES, :LANES], filt_ref[:, a * LANES : (a + 1) * LANES]
        ).astype(BF16)

    def short_stage(fetch_rows, first=False):
        def one(r, _):
            re_at = pl.ds(pl.multiple_of(r * step, step), step)
            im_at = pl.ds(pl.multiple_of(LANES + r * step, step), step)

            def emit(leaf, re, im):
                if first:
                    for which in range(2):
                        column = twist_ref[re_at, which * blocks + leaf : which * blocks + leaf + 1]
                        twist[leaf, which, re_at, :] = jnp.broadcast_to(column, (step, lanes))
                cos, sin = twist[leaf, 0, re_at, :], twist[leaf, 1, re_at, :]
                spec[leaf // 2, re_at, leaf_lanes(leaf)] = (re * cos - im * sin).astype(BF16)
                spec[leaf // 2, im_at, leaf_lanes(leaf)] = (re * sin + im * cos).astype(BF16)

            coefs = []
            for a in range(blocks):
                at = pl.ds(pl.multiple_of((a % tiles) * LANES + r * step, step), step)
                x, lean = fetch_rows(a // tiles, at).astype(F32), a * math.pi / (2 * blocks)
                coefs.append((x * math.cos(lean), x * math.sin(lean)))
            split_forward(coefs, 0.0, 0, emit)
            return 0

        lax.fori_loop(0, LANES // step, one, 0)

    def filter_chunk(c):
        short_stage(lambda a, at: filt_rows[a, at, chunk_lanes(c)], c == 0)

        def filt_pair(pair, _):
            h_spec[c, pair] = jnp.dot(table_ref[0], spec[pair], preferred_element_type=F32).astype(h_spec.dtype)
            return 0

        lax.fori_loop(0, blocks // 2, filt_pair, 0, unroll=2)

    for c in range(chunks):
        filter_chunk(c)

    def rim_wait(j, _):
        rim_copy(j).wait()
        return 0

    for c in range(chunks):
        def wait_in(j, _):
            in_copy(c, j).wait()
            return 0

        lax.fori_loop(0, n - 1, wait_in, 0)
        if c == 0:
            lax.fori_loop(0, n - 1, rim_wait, 0)
        own_in(c).wait()
        short_stage(lambda a, at: recv[c, a, at, :])

        def pair_step(pair, _):
            sig = jnp.dot(table_ref[0], spec[pair], preferred_element_type=F32)
            h_re, h_im = h_spec[c, pair, :LANES, :].astype(F32), h_spec[c, pair, LANES:, :].astype(F32)
            s_re, s_im = sig[:LANES], sig[LANES:]
            prod = jnp.concatenate([s_re * h_re - s_im * h_im, s_re * h_im + s_im * h_re], axis=0).astype(BF16)
            h_spec[c, pair] = jnp.dot(table_ref[1], prod, preferred_element_type=F32).astype(h_spec.dtype)
            return 0

        lax.fori_loop(0, blocks // 2, pair_step, 0, unroll=4)
        gain = gain_ref[:, chunk_lanes(c)]

        def back_step(r, _):
            re_at = pl.ds(pl.multiple_of(r * step, step), step)
            im_at = pl.ds(pl.multiple_of(LANES + r * step, step), step)

            def fetch(leaf):
                re = h_spec[c, leaf // 2, re_at, leaf_lanes(leaf)].astype(F32)
                im = h_spec[c, leaf // 2, im_at, leaf_lanes(leaf)].astype(F32)
                cos, sin = twist[leaf, 0, re_at, :], twist[leaf, 1, re_at, :]
                return re * cos + im * sin, im * cos - re * sin

            parts = split_inverse(fetch, blocks, 0.0, 0)
            for a, (re, im) in enumerate(parts):
                lean = a * math.pi / (2 * blocks)
                cos, sin = math.cos(lean) / length, math.sin(lean) / length
                at = pl.ds(pl.multiple_of((a % tiles) * LANES + r * step, step), step)
                sig = recv[c, a // tiles, at, :].astype(F32)
                recv[c, a // tiles, at, :] = (cos * re + sin * im + gain * sig).astype(BF16)
            return 0

        lax.fori_loop(0, LANES // step, back_step, 0)

        def return_step(j, _):
            out_copy(c, j).start()
            return 0

        lax.fori_loop(0, n - 1, return_step, 0)
        own_out(c).start()

    halo_wait(1)
    for c in range(chunks):
        def q_step(i, _):
            peers = (2 * i, 2 * i + 1)
            taps = turn_pair(0, [(0, p) for p in peers], c, True)
            for slot, p in enumerate(peers):
                parts = [sums_of(turned, (slot,), taps[slot], start, part).astype(BF16) for start in range(0, tok, part)]
                out_ref[peer_rows(p, c), :] = across(eye[:lanes, :lanes], jnp.concatenate(parts, axis=0)).astype(BF16)
            return 0

        lax.fori_loop(0, pairs, q_step, 0)

    def mix(peer, c):
        at = peer_rows(peer, c)
        long = across(eye[:lanes, :lanes], ret[c, peer])
        out_ref[at, :] = (out_ref[at, :].astype(F32) * long).astype(BF16)

    for c in range(chunks):
        own_out(c).wait()
        mix(me, c)

        def mix_step(j, _):
            out_copy(c, j).wait()
            mix(peer_of(j), c)
            return 0

        lax.fori_loop(0, n - 1, mix_step, 0)


def kernel(
    n, lanes,
    q_ref, k_ref, v_ref, taps_ref, filt_hbm, gain_ref, table_ref, twist_ref,
    out_hbm,
    out_ref, eye, tails, halo, turned, gated, recv, spec, h_spec, ret, filt_ref, filt_rows, twist,
    filt_sem, halo_sem, in_send, in_recv, in_own, out_send, out_recv, out_own, put,
):
    me = lax.axis_index("ctx")
    width, tok = q_ref.shape
    chan, length = filt_ref.shape
    chunks = chan // lanes
    rim = taps_ref.shape[-2]
    blocks = length // LANES
    tiles = tok // LANES
    sources = (q_ref, k_ref, v_ref)
    step = 16
    filt_copy = pltpu.make_async_copy(filt_hbm, filt_ref, filt_sem)
    filt_copy.start()

    barrier = pltpu.get_barrier_semaphore()
    for d in range(1, n):
        pl.semaphore_signal(barrier, inc=1, device_id={"ctx": lax.rem(me + d, n)}, device_id_type=MESH)

    side = eye.shape[0]
    row = lax.broadcasted_iota(jnp.int32, (side, side), 0)
    col = lax.broadcasted_iota(jnp.int32, (side, side), 1)
    eye[...] = (row == col).astype(F32).astype(BF16)

    pick_row = lax.broadcasted_iota(jnp.int32, (SLOT, LANES), 0) + (LANES - SLOT)
    pick = (pick_row == lax.broadcasted_iota(jnp.int32, (SLOT, LANES), 1)).astype(F32).astype(BF16)

    def tail_step(p, _):
        at = pl.ds(pl.multiple_of(p * chan, chan), chan)
        for w in range(3):
            tails[w, p] = across(pick, sources[w][at, tok - LANES :]).astype(BF16)
        return 0

    lax.fori_loop(0, n, tail_step, 0, unroll=4)

    pl.semaphore_wait(barrier, n - 1)
    halo_copy = pltpu.make_async_remote_copy(
        src_ref=tails, dst_ref=halo, send_sem=halo_sem.at[0], recv_sem=halo_sem.at[1],
        device_id={"ctx": lax.rem(me + 1, n)}, device_id_type=MESH,
    )

    halo_copy.start()
    if lanes < LANES:
        spec[...] = jnp.zeros_like(spec)

    filt_copy.wait()
    for a in range(blocks):
        filt_rows[a // tiles, (a % tiles) * LANES : (a % tiles + 1) * LANES, :] = across(
            eye[:LANES, :LANES], filt_ref[:, a * LANES : (a + 1) * LANES]
        ).astype(BF16)

    def chunk_lanes(c):
        return slice(c * lanes, (c + 1) * lanes)

    def leaf_lanes(leaf):
        return slice((leaf % 2) * LANES, (leaf % 2) * LANES + lanes)

    def short_stage(ref, c, first=False):
        at_lanes = chunk_lanes(c)

        def one(r, _):
            re_at = pl.ds(pl.multiple_of(r * step, step), step)
            im_at = pl.ds(pl.multiple_of(LANES + r * step, step), step)

            def emit(leaf, re, im):
                if first:
                    for which in range(2):
                        column = twist_ref[re_at, which * blocks + leaf : which * blocks + leaf + 1]
                        twist[leaf, which, re_at, :] = jnp.broadcast_to(column, (step, lanes))
                cos, sin = twist[leaf, 0, re_at, :], twist[leaf, 1, re_at, :]
                spec[leaf // 2, re_at, leaf_lanes(leaf)] = (re * cos - im * sin).astype(BF16)
                spec[leaf // 2, im_at, leaf_lanes(leaf)] = (re * sin + im * cos).astype(BF16)

            coefs = []
            for a in range(blocks):
                at = pl.ds(pl.multiple_of((a % tiles) * LANES + r * step, step), step)
                x, lean = ref[a // tiles, at, at_lanes].astype(F32), a * math.pi / (2 * blocks)
                coefs.append((x * math.cos(lean), x * math.sin(lean)))
            split_forward(coefs, 0.0, 0, emit)
            return 0

        lax.fori_loop(0, LANES // step, one, 0)

    def filter_chunk(c):
        short_stage(filt_rows, c, c == 0)

        def filt_pair(pair, _):
            h_spec[c, pair] = jnp.dot(table_ref[0], spec[pair], preferred_element_type=F32).astype(h_spec.dtype)
            return 0

        lax.fori_loop(0, blocks // 2, filt_pair, 0, unroll=2)

    filter_chunk(0)
    halo_copy.wait()

    def peer_rows(peer, c):
        return pl.ds(pl.multiple_of(peer * chan + c * lanes, lanes), lanes)

    def short(first, pair, c):
        block = jnp.concatenate([sources[w][peer_rows(peer, c), :] for w, peer in pair], axis=0)
        both = across(eye[:tok, :tok], block)
        taps = []
        for i, (w, peer) in enumerate(pair):
            turned[first + i, :SLOT, :] = jnp.where(me > 0, halo[w, peer, :, chunk_lanes(c)].astype(F32), 0.0)
            turned[first + i, SLOT:, :] = both[:, i * lanes : (i + 1) * lanes]
            if len(taps_ref.shape) == 3:
                taps.append(taps_ref[w, :, peer_rows(peer, c)])
            else:
                taps.append(taps_ref[peer, w, :, chunk_lanes(c)])
        return taps

    def sums_of(slot, taps, start, count):
        total = None
        for j in range(rim):
            term = taps[j : j + 1, :] * turned[slot, SLOT - j + start : SLOT - j + start + count, :]
            total = term if total is None else total + term
        return total

    part = 64

    def gate_pair(peers, c):
        taps = [short(2 * i, [(1, p), (2, p)], c) for i, p in enumerate(peers)]
        for i, p in enumerate(peers):
            for start in range(0, tok, part):
                product = sums_of(2 * i, taps[i][0], start, part) * sums_of(2 * i + 1, taps[i][1], start, part)
                gated[p, start : start + part, chunk_lanes(c)] = product.astype(BF16)

    def in_copy(c, d):
        peer = lax.rem(me + d, n)
        return pltpu.make_async_remote_copy(
            src_ref=gated.at[peer, :, chunk_lanes(c)], dst_ref=recv.at[me, :, chunk_lanes(c)],
            send_sem=in_send.at[c, d], recv_sem=in_recv.at[c, d],
            device_id={"ctx": peer}, device_id_type=MESH,
        )

    def own_in(c):
        return pltpu.make_async_copy(gated.at[me, :, chunk_lanes(c)], recv.at[me, :, chunk_lanes(c)], in_own.at[c])

    def out_copy(c, d):
        peer = lax.rem(me + d, n)
        return pltpu.make_async_remote_copy(
            src_ref=recv.at[peer, :, chunk_lanes(c)], dst_ref=ret.at[me, :, chunk_lanes(c)],
            send_sem=out_send.at[c, d], recv_sem=out_recv.at[c, d],
            device_id={"ctx": peer}, device_id_type=MESH,
        )

    def own_out(c):
        return pltpu.make_async_copy(recv.at[me, :, chunk_lanes(c)], ret.at[me, :, chunk_lanes(c)], out_own.at[c])

    for c in range(chunks):
        def send_step(i, _):
            gate_pair([lax.rem(me + 2 * i + 1, n), lax.rem(me + 2 * i + 2, n)], c)

            @pl.when(i > 0)
            def _():
                in_copy(c, 2 * i - 1).start()
                in_copy(c, 2 * i).start()

            return 0

        lax.fori_loop(0, n // 2, send_step, 0)
        in_copy(c, n - 1).start()
        own_in(c).start()

    for c in range(1, chunks):
        filter_chunk(c)

    for c in range(chunks):
        def wait_in(d, _):
            in_copy(c, d).wait()
            return 0

        lax.fori_loop(1, n, wait_in, 0)
        own_in(c).wait()
        at_lanes = chunk_lanes(c)
        short_stage(recv, c)

        def pair_step(pair, _):
            sig = jnp.dot(table_ref[0], spec[pair], preferred_element_type=F32)
            h_re, h_im = h_spec[c, pair, :LANES, :].astype(F32), h_spec[c, pair, LANES:, :].astype(F32)
            s_re, s_im = sig[:LANES], sig[LANES:]
            prod = jnp.concatenate([s_re * h_re - s_im * h_im, s_re * h_im + s_im * h_re], axis=0).astype(BF16)
            h_spec[c, pair] = jnp.dot(table_ref[1], prod, preferred_element_type=F32).astype(h_spec.dtype)
            return 0

        lax.fori_loop(0, blocks // 2, pair_step, 0, unroll=4)
        gain = gain_ref[:, at_lanes]

        def back_step(r, _):
            re_at = pl.ds(pl.multiple_of(r * step, step), step)
            im_at = pl.ds(pl.multiple_of(LANES + r * step, step), step)
            def fetch(leaf):
                re = h_spec[c, leaf // 2, re_at, leaf_lanes(leaf)].astype(F32)
                im = h_spec[c, leaf // 2, im_at, leaf_lanes(leaf)].astype(F32)
                cos, sin = twist[leaf, 0, re_at, :], twist[leaf, 1, re_at, :]
                return re * cos + im * sin, im * cos - re * sin

            parts = split_inverse(fetch, blocks, 0.0, 0)
            for a, (re, im) in enumerate(parts):
                lean = a * math.pi / (2 * blocks)
                cos, sin = math.cos(lean) / length, math.sin(lean) / length
                at = pl.ds(pl.multiple_of((a % tiles) * LANES + r * step, step), step)
                sig = recv[a // tiles, at, at_lanes].astype(F32)
                recv[a // tiles, at, at_lanes] = (cos * re + sin * im + gain * sig).astype(BF16)
            return 0

        lax.fori_loop(0, LANES // step, back_step, 0)

        def return_step(d, _):
            out_copy(c, d).start()
            return 0

        lax.fori_loop(1, n, return_step, 0)
        own_out(c).start()

    for c in range(chunks):
        def q_step(i, _):
            peers = (2 * i, 2 * i + 1)
            taps = short(0, [(0, p) for p in peers], c)
            for slot, p in enumerate(peers):
                parts = [sums_of(slot, taps[slot], start, part).astype(BF16) for start in range(0, tok, part)]
                out_ref[peer_rows(p, c), :] = across(eye[:lanes, :lanes], jnp.concatenate(parts, axis=0)).astype(BF16)
            return 0

        lax.fori_loop(0, n // 2, q_step, 0)

    def mix(peer, c):
        at = peer_rows(peer, c)
        long = across(eye[:lanes, :lanes], ret[peer, :, chunk_lanes(c)])
        out_ref[at, :] = (out_ref[at, :].astype(F32) * long).astype(BF16)
        put_copy(peer, c).start()

    def put_copy(peer, c):
        at = peer_rows(peer, c)
        return pltpu.make_async_copy(out_ref.at[at, :], out_hbm.at[at, :], put.at[c, peer])

    for c in range(chunks):
        own_out(c).wait()
        mix(me, c)

        def mix_step(d, _):
            out_copy(c, d).wait()
            mix(lax.rem(me + n - d, n), c)
            return 0

        lax.fori_loop(1, n, mix_step, 0)

    for c in range(chunks):
        def put_step(p, _):
            put_copy(p, c).wait()
            return 0

        lax.fori_loop(0, n, put_step, 0)


def wide_call(n, queries, keys, values, taps, filters, gain):
    width, tok = queries.shape
    chan, length = filters.shape
    blocks = length // LANES
    chunks = chan // LANES
    reach = taps.shape[1]
    dma = pltpu.SemaphoreType.DMA
    two = 2 * LANES
    table = circle_tables()
    columns = twist_columns(blocks)
    held = [
        pltpu.with_memory_space_constraint(x, pltpu.HBM)
        for x in (queries, keys, values, taps, filters, gain, jnp.asarray(table), jnp.asarray(columns))
    ]
    return pl.pallas_call(
        functools.partial(wide_kernel, n),
        out_shape=pltpu.VMEM((width, tok), BF16),
        in_specs=[pl.BlockSpec(memory_space=pltpu.HBM)] * 8,
        out_specs=pl.BlockSpec(memory_space=pltpu.VMEM),
        scratch_shapes=[
            pltpu.VMEM((3, width, tok), BF16),
            pltpu.VMEM((3, reach, width), F32),
            pltpu.VMEM((chan, length), BF16),
            pltpu.VMEM((1, chan), F32),
            pltpu.VMEM(table.shape, BF16),
            pltpu.VMEM(columns.shape, F32),
            pltpu.VMEM((tok, tok), BF16),
            pltpu.VMEM((3, n, SLOT, chan), BF16),
            pltpu.VMEM((3, n, SLOT, chan), BF16),
            pltpu.VMEM((4, SLOT + tok, LANES), F32),
            pltpu.VMEM((2, n, SLOT + 16, LANES), F32),
            pltpu.VMEM((chunks, n, tok, LANES), BF16),
            pltpu.VMEM((chunks, n, tok, LANES), BF16),
            pltpu.VMEM((blocks // 2, two, two), BF16),
            pltpu.VMEM((chunks, blocks // 2, two, two), F32),
            pltpu.VMEM((chunks, n, tok, LANES), BF16),
            pltpu.VMEM((n, tok, chan), BF16),
            pltpu.VMEM((blocks, 2, LANES, LANES), F32),
            dma((2, chunks, n)),
            dma,
            dma((5,)),
            dma((2,)),
            dma((2,)),
            dma((n,)),
            dma((n,)),
            dma((chunks, n)),
            dma((chunks, n)),
            dma((chunks,)),
            dma((chunks, n)),
            dma((chunks, n)),
            dma((chunks,)),
        ],
        compiler_params=pltpu.CompilerParams(
            collective_id=0, has_side_effects=True, vmem_limit_bytes=40 * 2**20
        ),
        name="hyena",
    )(*held)


def solution(mesh):
    n = mesh.shape["ctx"]

    def local(queries, keys, values, short_taps, long_filter, skip_gain):
        width, tok = queries.shape
        chan, length = long_filter.shape[1:]
        blocks = length // LANES
        lanes = min(chan, LANES)
        chunks = chan // lanes
        small_work = length * chan <= 2**20
        if n >= 2 and n & (n - 1) == 0 and chan % LANES == 0 and tok % LANES == 0 and small_work:
            return wide_call(n, queries, keys, values, short_taps, long_filter[0], skip_gain)
        table = jnp.asarray(circle_tables())
        twist = jnp.asarray(twist_columns(blocks))
        dma = pltpu.SemaphoreType.DMA
        two = 2 * LANES
        small = blocks * two * max(chan, LANES) * 4 <= 8 * 2**20
        side = max(tok, LANES)
        any_space = pl.BlockSpec(memory_space=pl.ANY)
        taps = short_taps
        if lanes < LANES:
            taps = jnp.moveaxis(short_taps.reshape(3, -1, n, chan), 2, 0)
        return pl.pallas_call(
            functools.partial(kernel, n, lanes),
            out_shape=jax.ShapeDtypeStruct((width, tok), BF16),
            in_specs=[any_space if i == 4 else pl.BlockSpec(memory_space=pltpu.VMEM) for i in range(8)],
            out_specs=any_space,
            scratch_shapes=[
                pltpu.VMEM((width, tok), BF16),
                pltpu.VMEM((side, side), BF16),
                pltpu.VMEM((3, n, SLOT, chan), BF16),
                pltpu.VMEM((3, n, SLOT, chan), BF16),
                pltpu.VMEM((4, SLOT + tok, lanes), F32),
                pltpu.VMEM((n, tok, chan), BF16),
                pltpu.VMEM((n, tok, chan), BF16),
                pltpu.VMEM((blocks // 2, two, two), BF16),
                pltpu.VMEM((chunks, blocks // 2, two, two), F32 if small else BF16),
                pltpu.VMEM((n, tok, chan), BF16),
                pltpu.VMEM((chan, length), BF16),
                pltpu.VMEM((n, tok, chan), BF16),
                pltpu.VMEM((blocks, 2, LANES, lanes), F32),
                dma,
                dma((2,)),
                dma((chunks, n)),
                dma((chunks, n)),
                dma((chunks,)),
                dma((chunks, n)),
                dma((chunks, n)),
                dma((chunks,)),
                dma((chunks, n)),
            ],
            compiler_params=pltpu.CompilerParams(
                collective_id=0, has_side_effects=True, vmem_limit_bytes=67043328
            ),
            name="hyena",
        )(queries, keys, values, taps, long_filter[0], skip_gain, table, twist)

    placed = (
        P("ch", "ctx"),
        P("ch", "ctx"),
        P("ch", "ctx"),
        P(None, None, "ch"),
        P("ch", "ctx", None),
        P("ch", "ctx"),
    )
    return jax.shard_map(local, mesh=mesh, in_specs=placed, out_specs=P("ch", "ctx"), check_vma=False)
```

```python
import functools
import math

import jax
import jax.numpy as jnp
import ml_dtypes
import numpy as np
from jax import lax
from jax.experimental import pallas as pl
from jax.experimental.pallas import tpu as pltpu
from jax.sharding import PartitionSpec as P

MESH = pl.DeviceIdType.MESH
LANES = 128
SLOT = 8
F32 = jnp.float32
BF16 = jnp.bfloat16


def leaf_angles(count, theta):
    if count == 1:
        return [theta]
    return leaf_angles(count // 2, theta / 2) + leaf_angles(count // 2, theta / 2 + math.pi)


def circle_tables():
    place = np.arange(LANES, dtype=np.float64)
    angle = place[:, None] * place[None, :] * (2.0 * math.pi / LANES)
    cos, sin = np.cos(angle), np.sin(angle)
    there = np.block([[cos, -sin], [sin, cos]])
    return np.stack([there, there.T]).astype(ml_dtypes.bfloat16)


def twist_columns(count):
    roots = np.array(leaf_angles(count, 0.0)) + math.pi / (2 * count)
    angle = np.arange(LANES)[:, None] * roots[None, :] / LANES
    return np.concatenate([np.cos(angle), np.sin(angle)], axis=1).astype(np.float32)


def turn(re, im, angle):
    eighth = round(angle / (math.pi / 4))
    if abs(angle - eighth * math.pi / 4) > 1e-9:
        cos, sin = math.cos(angle), math.sin(angle)
        return cos * re - sin * im, cos * im + sin * re
    eighth %= 8
    if eighth % 2:
        re, im = math.sqrt(0.5) * (re - im), math.sqrt(0.5) * (re + im)
    return [(re, im), (-im, re), (-re, -im), (im, -re)][eighth // 2]


def split_forward(coefs, theta, first, emit):
    count = len(coefs)
    if count == 1:
        emit(first, *coefs[0])
        return
    half = count // 2
    plus, minus = [], []
    for (lo_re, lo_im), high in zip(coefs[:half], coefs[half:]):
        hi_re, hi_im = turn(*high, theta / 2)
        plus.append((lo_re + hi_re, lo_im + hi_im))
        minus.append((lo_re - hi_re, lo_im - hi_im))
    split_forward(plus, theta / 2, first, emit)
    split_forward(minus, theta / 2 + math.pi, first + half, emit)


def split_inverse(fetch, count, theta, first):
    if count == 1:
        return [fetch(first)]
    half = count // 2
    plus = split_inverse(fetch, half, theta / 2, first)
    minus = split_inverse(fetch, half, theta / 2 + math.pi, first + half)
    low, high = [], []
    for (p_re, p_im), (m_re, m_im) in zip(plus, minus):
        low.append((p_re + m_re, p_im + m_im))
        high.append(turn(p_re - m_re, p_im - m_im, -theta / 2))
    return low + high


def across(eye, block):
    return lax.dot_general(eye, block, (((1,), (1,)), ((), ())), preferred_element_type=F32)


def wave_tables(tok):
    bins = np.concatenate([np.arange(0, tok, 2), np.arange(1, tok, 2)])
    angle = (2 * bins + 1)[:, None] * np.arange(tok)[None, :] * (math.pi / (2 * tok))
    there = np.concatenate([np.cos(angle), np.sin(angle)], axis=0)
    return there.astype(ml_dtypes.bfloat16), (there.T / tok).astype(ml_dtypes.bfloat16)


def crossed(a, b, count):
    total, place = 0, 1
    while place < count:
        total = total + lax.rem(lax.div(a, place) + lax.div(b, place), 2) * place
        place *= 2
    return total


def wide_kernel(
    n,
    q_hbm, k_hbm, v_hbm, taps_hbm, filt_hbm, gain_hbm, there_hbm, back_hbm,
    out_ref,
    source, taps_ref, filt_ref, gain_ref, there_ref, back_ref,
    eye, tails, halo, turned, rim, gated, recv, ret, q_rows, wave, filt_wave, sig_wave, out_wave,
    load_sem, q_sem, side_sem, halo_send, halo_recv,
    rim_send, rim_recv, in_send, in_recv, in_own, out_send, out_recv, out_own,
):
    me = lax.axis_index("ctx")
    width, tok = q_hbm.shape
    chan, length = filt_hbm.shape
    lanes = LANES
    chunks = chan // lanes
    reach = taps_hbm.shape[1]
    pairs = n // 2
    step = 16
    half = step // 2
    edge = 16
    part = 64

    barrier = pltpu.get_barrier_semaphore()
    for d in range(1, n):
        pl.semaphore_signal(
            barrier, inc=1, device_id={"ctx": lax.rem(me + d, n)}, device_id_type=MESH
        )

    def peer_of(j):
        return crossed(me, n - 1 - j, n)

    def peer_rows(peer, c):
        return pl.ds(pl.multiple_of(peer * chan + c * lanes, lanes), lanes)

    def load(w, c, j):
        ref = (q_hbm, k_hbm, v_hbm)[w]
        at = peer_rows(peer_of(j), c)
        return pltpu.make_async_copy(ref.at[at, :], source.at[w, at, :], load_sem.at[w - 1, c, j])

    side = [
        pltpu.make_async_copy(taps_hbm, taps_ref, side_sem.at[0]),
        pltpu.make_async_copy(filt_hbm, filt_ref, side_sem.at[1]),
        pltpu.make_async_copy(gain_hbm, gain_ref, side_sem.at[2]),
        pltpu.make_async_copy(there_hbm, there_ref, side_sem.at[3]),
        pltpu.make_async_copy(back_hbm, back_ref, side_sem.at[4]),
    ]
    load_q = pltpu.make_async_copy(q_hbm, source.at[0], q_sem)

    def load_step(j, c):
        load(1, c, j).start()
        load(2, c, j).start()
        return c

    def load_wait(j, c):
        load(1, c, j).wait()
        load(2, c, j).wait()
        return c

    lax.fori_loop(0, 2, load_step, 0)
    side[0].start()
    lax.fori_loop(2, n, load_step, 0)
    for c in range(1, chunks):
        lax.fori_loop(0, n, load_step, c)
    for i in range(1, len(side)):
        side[i].start()
    load_q.start()

    size = eye.shape[0]
    row = lax.broadcasted_iota(jnp.int32, (size, size), 0)
    col = lax.broadcasted_iota(jnp.int32, (size, size), 1)
    eye[...] = (row == col).astype(F32).astype(BF16)
    pick_row = lax.broadcasted_iota(jnp.int32, (SLOT, LANES), 0) + (LANES - SLOT)
    pick = (pick_row == lax.broadcasted_iota(jnp.int32, (SLOT, LANES), 1)).astype(F32).astype(BF16)

    def find_tails(w):
        def one(p, _):
            at = pl.ds(pl.multiple_of(p * chan, chan), chan)
            tails[w, p] = across(pick, source[w, at, tok - LANES :]).astype(BF16)
            return 0

        lax.fori_loop(0, n, one, 0, unroll=4)

    def halo_copy(part_of):
        at = slice(1, 3) if part_of == 0 else slice(0, 1)
        return pltpu.make_async_remote_copy(
            src_ref=tails.at[at], dst_ref=halo.at[at],
            send_sem=halo_send.at[part_of], recv_sem=halo_recv.at[part_of],
            device_id={"ctx": lax.rem(me + 1, n)}, device_id_type=MESH,
        )

    def halo_start(part_of):
        @pl.when(me < n - 1)
        def _():
            halo_copy(part_of).start()

    def halo_wait(part_of):
        @pl.when(me < n - 1)
        def _():
            halo_copy(part_of).wait_send()

        @pl.when(me > 0)
        def _():
            halo_copy(part_of).wait_recv()

    def chunk_lanes(c):
        return slice(c * lanes, (c + 1) * lanes)

    def set_halo(w, peer, c, ref, *index):
        ref[(*index, slice(0, SLOT), slice(None))] = jnp.zeros((SLOT, lanes), F32)

        @pl.when(me > 0)
        def _():
            ref[(*index, slice(0, SLOT), slice(None))] = halo[w, peer, :, chunk_lanes(c)].astype(F32)

    def turn_pair(first, pair, c, whole):
        block = jnp.concatenate([source[w, peer_rows(peer, c), :] for w, peer in pair], axis=0)
        both = across(eye[:tok, :tok], block)
        for i, (w, peer) in enumerate(pair):
            rows = both[:, i * lanes : (i + 1) * lanes]
            turned[first + i, SLOT:, :] = rows
            if whole:
                set_halo(w, peer, c, turned, first + i)
            else:
                rim[w - 1, peer, SLOT:, :] = rows[:edge]
        return [taps_ref[w, :, peer_rows(peer, c)] for w, peer in pair]

    def sums_of(ref, index, taps, start, count):
        total = None
        for j in range(reach):
            at = slice(SLOT - j + start, SLOT - j + start + count)
            term = taps[j : j + 1, :] * ref[(*index, at, slice(None))]
            total = term if total is None else total + term
        return total

    def spans(first):
        marks = [first] + list(range((first // part + 1) * part, tok, part)) + [tok]
        return list(zip(marks[:-1], marks[1:]))

    def gate_pair(peers, c, whole):
        taps = [turn_pair(2 * i, [(1, p), (2, p)], c, whole) for i, p in enumerate(peers)]
        for i, p in enumerate(peers):
            for start, stop in spans(0 if whole else edge):
                count = stop - start
                product = sums_of(turned, (2 * i,), taps[i][0], start, count) * sums_of(
                    turned, (2 * i + 1,), taps[i][1], start, count
                )
                gated[c, p, start:stop, :] = product.astype(BF16)

    def in_copy(c, j):
        peer = peer_of(j)
        at = slice(0 if c else edge, tok)
        return pltpu.make_async_remote_copy(
            src_ref=gated.at[c, peer, at, :], dst_ref=recv.at[c, me, at, :],
            send_sem=in_send.at[c, j], recv_sem=in_recv.at[c, j],
            device_id={"ctx": peer}, device_id_type=MESH,
        )

    def rim_copy(j):
        peer = peer_of(j)
        return pltpu.make_async_remote_copy(
            src_ref=gated.at[0, peer, 0:edge, :], dst_ref=recv.at[0, me, 0:edge, :],
            send_sem=rim_send.at[j], recv_sem=rim_recv.at[j],
            device_id={"ctx": peer}, device_id_type=MESH,
        )

    def own_in(c):
        return pltpu.make_async_copy(gated.at[c, me], recv.at[c, me], in_own.at[c])

    def out_copy(c, j):
        peer = peer_of(j)
        return pltpu.make_async_remote_copy(
            src_ref=recv.at[c, peer], dst_ref=ret.at[c, me],
            send_sem=out_send.at[c, j], recv_sem=out_recv.at[c, j],
            device_id={"ctx": peer}, device_id_type=MESH,
        )

    def own_out(c):
        return pltpu.make_async_copy(recv.at[c, me], ret.at[c, me], out_own.at[c])

    def gate_chunk(c):
        def one(i, _):
            if c == 0:
                load_wait(2 * i, c)
                load_wait(2 * i + 1, c)
            gate_pair([peer_of(2 * i), peer_of(2 * i + 1)], c, c > 0)

            @pl.when(i > 0)
            def _():
                in_copy(c, 2 * i - 2).start()
                in_copy(c, 2 * i - 1).start()

            return 0

        if c == 0:
            one_first(one)
        else:
            lax.fori_loop(0, pairs, one, 0)
        in_copy(c, n - 2).start()

    def one_first(one):
        side[0].wait()
        pl.semaphore_wait(barrier, n - 1)
        lax.fori_loop(0, pairs, one, 0)

    gate_chunk(0)
    for c in range(1, chunks):
        lax.fori_loop(0, n, load_wait, c)
    find_tails(1)
    find_tails(2)
    halo_start(0)

    for i in range(1, len(side)):
        side[i].wait()

    mid = tok // 2
    signs = ((0, 1.0), (mid, -1.0))

    def filter_wave(d):
        wave[d % 2] = across(there_ref[...], filt_ref[:, d * tok : (d + 1) * tok])
        now, before = wave.at[d % 2], wave.at[1 - d % 2]

        def one(r, _):
            for first, sign in signs:
                re_at = pl.ds(pl.multiple_of(first + r * step, step), step)
                im_at = pl.ds(pl.multiple_of(tok + first + r * step, step), step)
                re, im = now[re_at, :], now[im_at, :]
                if d > 0:
                    re, im = re + sign * before[im_at, :], im - sign * before[re_at, :]
                for c in range(chunks):
                    filt_wave[c, d, re_at, :] = re[:, chunk_lanes(c)]
                    filt_wave[c, d, im_at, :] = im[:, chunk_lanes(c)]
            return 0

        lax.fori_loop(0, mid // step, one, 0, unroll=2)

    for d in range(n):
        filter_wave(d)
    halo_wait(0)

    def rim_step(i, _):
        for p in (peer_of(2 * i), peer_of(2 * i + 1)):
            for w in (1, 2):
                set_halo(w, p, 0, rim, w - 1, p)
            gated[0, p, :edge, :] = (
                sums_of(rim, (0, p), taps_ref[1, :, peer_rows(p, 0)], 0, edge)
                * sums_of(rim, (1, p), taps_ref[2, :, peer_rows(p, 0)], 0, edge)
            ).astype(BF16)
        return 0

    lax.fori_loop(0, pairs, rim_step, 0)

    def rim_start(j, _):
        rim_copy(j).start()
        return 0

    lax.fori_loop(0, n - 1, rim_start, 0)
    own_in(0).start()

    for c in range(1, chunks):
        gate_chunk(c)
        own_in(c).start()

    load_q.wait()
    find_tails(0)
    halo_start(1)

    def sig_step(c):
        def one(i, _):
            in_copy(c, 2 * i).wait()
            if c == 0:
                rim_copy(2 * i).wait()

            @pl.when(i < pairs - 1)
            def _():
                in_copy(c, 2 * i + 1).wait()
                if c == 0:
                    rim_copy(2 * i + 1).wait()

            @pl.when(i == pairs - 1)
            def _():
                own_in(c).wait()

            first = lax.div(peer_of(2 * i), 2) * 2
            both = jnp.concatenate([recv[c, first], recv[c, first + 1]], axis=1)
            both = jnp.dot(there_ref[...], both, preferred_element_type=F32)
            sig_wave[first] = both[:, :lanes]
            sig_wave[first + 1] = both[:, lanes:]
            return 0

        lax.fori_loop(0, pairs, one, 0)

    def blend(c):
        def one(r, _):
            done = []
            for part_of in range(2):
                start = r * step + part_of * half
                re_at = pl.ds(pl.multiple_of(start, half), half)
                im_at = pl.ds(pl.multiple_of(tok + start, half), half)
                f_re = [filt_wave[c, d, re_at, :] for d in range(n)]
                f_im = [filt_wave[c, d, im_at, :] for d in range(n)]
                s_re = [sig_wave[d, re_at, :] for d in range(n)]
                s_im = [sig_wave[d, im_at, :] for d in range(n)]
                rows = []
                for i in range(n):
                    re = im = None
                    for j in range(i + 1):
                        a, b, x, y = f_re[i - j], f_im[i - j], s_re[j], s_im[j]
                        re = a * x - b * y if re is None else re + a * x - b * y
                        im = a * y + b * x if im is None else im + a * y + b * x
                    rows.append((re, im))
                done.append(rows)
            re_at = pl.ds(pl.multiple_of(r * step, step), step)
            im_at = pl.ds(pl.multiple_of(tok + r * step, step), step)
            for i in range(n):
                at = slice((i % 2) * lanes, (i % 2 + 1) * lanes)
                for which, rows_at in enumerate((re_at, im_at)):
                    whole = jnp.concatenate([done[0][i][which], done[1][i][which]], axis=0)
                    out_wave[i // 2, rows_at, at] = whole.astype(BF16)
            return 0

        lax.fori_loop(0, tok // step, one, 0)

    def return_step(c):
        gain = gain_ref[:, chunk_lanes(c)]

        def one(i, _):
            couple = lax.div(peer_of(2 * i), 2)
            both = jnp.dot(back_ref[...], out_wave[couple], preferred_element_type=F32)
            for k in range(2):
                sig = recv[c, 2 * couple + k].astype(F32)
                recv[c, 2 * couple + k] = (both[:, k * lanes : (k + 1) * lanes] + gain * sig).astype(BF16)

            @pl.when(i > 0)
            def _():
                out_copy(c, 2 * i - 2).start()
                out_copy(c, 2 * i - 1).start()

            return 0

        lax.fori_loop(0, pairs, one, 0)
        out_copy(c, n - 2).start()
        own_out(c).start()

    def q_chunk(c):
        def one(i, _):
            peers = (2 * i, 2 * i + 1)
            taps = turn_pair(0, [(0, p) for p in peers], c, True)
            for slot, p in enumerate(peers):
                for start in range(0, tok, part):
                    q_rows[c, p, start : start + part, :] = sums_of(
                        turned, (slot,), taps[slot], start, part
                    ).astype(BF16)
            return 0

        lax.fori_loop(0, pairs, one, 0)

    for c in range(chunks):
        sig_step(c)
        blend(c)
        return_step(c)
        if c == 0:
            halo_wait(1)
        q_chunk(c)

    def mix(peer, c):
        long = ret[c, peer].astype(F32)
        mixed = (q_rows[c, peer].astype(F32) * long).astype(BF16)
        out_ref[peer_rows(peer, c), :] = across(eye[:lanes, :lanes], mixed).astype(BF16)

    for c in range(chunks):
        own_out(c).wait()
        mix(me, c)

        def mix_step(j, _):
            out_copy(c, n - 2 - j).wait()
            mix(peer_of(n - 2 - j), c)
            return 0

        lax.fori_loop(0, n - 1, mix_step, 0)


def kernel(
    n, lanes,
    q_ref, k_ref, v_ref, taps_ref, filt_hbm, gain_ref, table_ref, twist_ref,
    out_hbm,
    out_ref, eye, tails, halo, turned, gated, recv, spec, h_spec, ret, filt_ref, filt_rows, twist,
    filt_sem, halo_sem, in_send, in_recv, in_own, out_send, out_recv, out_own, put,
):
    me = lax.axis_index("ctx")
    width, tok = q_ref.shape
    chan, length = filt_ref.shape
    chunks = chan // lanes
    rim = taps_ref.shape[-2]
    blocks = length // LANES
    tiles = tok // LANES
    sources = (q_ref, k_ref, v_ref)
    step = 16
    filt_copy = pltpu.make_async_copy(filt_hbm, filt_ref, filt_sem)
    filt_copy.start()

    barrier = pltpu.get_barrier_semaphore()
    for d in range(1, n):
        pl.semaphore_signal(barrier, inc=1, device_id={"ctx": lax.rem(me + d, n)}, device_id_type=MESH)

    side = eye.shape[0]
    row = lax.broadcasted_iota(jnp.int32, (side, side), 0)
    col = lax.broadcasted_iota(jnp.int32, (side, side), 1)
    eye[...] = (row == col).astype(F32).astype(BF16)

    pick_row = lax.broadcasted_iota(jnp.int32, (SLOT, LANES), 0) + (LANES - SLOT)
    pick = (pick_row == lax.broadcasted_iota(jnp.int32, (SLOT, LANES), 1)).astype(F32).astype(BF16)

    def tail_step(p, _):
        at = pl.ds(pl.multiple_of(p * chan, chan), chan)
        for w in range(3):
            tails[w, p] = across(pick, sources[w][at, tok - LANES :]).astype(BF16)
        return 0

    lax.fori_loop(0, n, tail_step, 0, unroll=4)

    pl.semaphore_wait(barrier, n - 1)
    halo_copy = pltpu.make_async_remote_copy(
        src_ref=tails, dst_ref=halo, send_sem=halo_sem.at[0], recv_sem=halo_sem.at[1],
        device_id={"ctx": lax.rem(me + 1, n)}, device_id_type=MESH,
    )

    halo_copy.start()
    if lanes < LANES:
        spec[...] = jnp.zeros_like(spec)

    filt_copy.wait()
    for a in range(blocks):
        filt_rows[a // tiles, (a % tiles) * LANES : (a % tiles + 1) * LANES, :] = across(
            eye[:LANES, :LANES], filt_ref[:, a * LANES : (a + 1) * LANES]
        ).astype(BF16)

    def chunk_lanes(c):
        return slice(c * lanes, (c + 1) * lanes)

    def leaf_lanes(leaf):
        return slice((leaf % 2) * LANES, (leaf % 2) * LANES + lanes)

    def short_stage(ref, c, first=False):
        at_lanes = chunk_lanes(c)

        def one(r, _):
            re_at = pl.ds(pl.multiple_of(r * step, step), step)
            im_at = pl.ds(pl.multiple_of(LANES + r * step, step), step)

            def emit(leaf, re, im):
                if first:
                    for which in range(2):
                        column = twist_ref[re_at, which * blocks + leaf : which * blocks + leaf + 1]
                        twist[leaf, which, re_at, :] = jnp.broadcast_to(column, (step, lanes))
                cos, sin = twist[leaf, 0, re_at, :], twist[leaf, 1, re_at, :]
                spec[leaf // 2, re_at, leaf_lanes(leaf)] = (re * cos - im * sin).astype(BF16)
                spec[leaf // 2, im_at, leaf_lanes(leaf)] = (re * sin + im * cos).astype(BF16)

            coefs = []
            for a in range(blocks):
                at = pl.ds(pl.multiple_of((a % tiles) * LANES + r * step, step), step)
                x, lean = ref[a // tiles, at, at_lanes].astype(F32), a * math.pi / (2 * blocks)
                coefs.append((x * math.cos(lean), x * math.sin(lean)))
            split_forward(coefs, 0.0, 0, emit)
            return 0

        lax.fori_loop(0, LANES // step, one, 0)

    def filter_chunk(c):
        short_stage(filt_rows, c, c == 0)

        def filt_pair(pair, _):
            h_spec[c, pair] = jnp.dot(table_ref[0], spec[pair], preferred_element_type=F32).astype(h_spec.dtype)
            return 0

        lax.fori_loop(0, blocks // 2, filt_pair, 0, unroll=2)

    filter_chunk(0)
    halo_copy.wait()

    def peer_rows(peer, c):
        return pl.ds(pl.multiple_of(peer * chan + c * lanes, lanes), lanes)

    def short(first, pair, c):
        block = jnp.concatenate([sources[w][peer_rows(peer, c), :] for w, peer in pair], axis=0)
        both = across(eye[:tok, :tok], block)
        taps = []
        for i, (w, peer) in enumerate(pair):
            turned[first + i, :SLOT, :] = jnp.where(me > 0, halo[w, peer, :, chunk_lanes(c)].astype(F32), 0.0)
            turned[first + i, SLOT:, :] = both[:, i * lanes : (i + 1) * lanes]
            if len(taps_ref.shape) == 3:
                taps.append(taps_ref[w, :, peer_rows(peer, c)])
            else:
                taps.append(taps_ref[peer, w, :, chunk_lanes(c)])
        return taps

    def sums_of(slot, taps, start, count):
        total = None
        for j in range(rim):
            term = taps[j : j + 1, :] * turned[slot, SLOT - j + start : SLOT - j + start + count, :]
            total = term if total is None else total + term
        return total

    part = 64

    def gate_pair(peers, c):
        taps = [short(2 * i, [(1, p), (2, p)], c) for i, p in enumerate(peers)]
        for i, p in enumerate(peers):
            for start in range(0, tok, part):
                product = sums_of(2 * i, taps[i][0], start, part) * sums_of(2 * i + 1, taps[i][1], start, part)
                gated[p, start : start + part, chunk_lanes(c)] = product.astype(BF16)

    def in_copy(c, d):
        peer = lax.rem(me + d, n)
        return pltpu.make_async_remote_copy(
            src_ref=gated.at[peer, :, chunk_lanes(c)], dst_ref=recv.at[me, :, chunk_lanes(c)],
            send_sem=in_send.at[c, d], recv_sem=in_recv.at[c, d],
            device_id={"ctx": peer}, device_id_type=MESH,
        )

    def own_in(c):
        return pltpu.make_async_copy(gated.at[me, :, chunk_lanes(c)], recv.at[me, :, chunk_lanes(c)], in_own.at[c])

    def out_copy(c, d):
        peer = lax.rem(me + d, n)
        return pltpu.make_async_remote_copy(
            src_ref=recv.at[peer, :, chunk_lanes(c)], dst_ref=ret.at[me, :, chunk_lanes(c)],
            send_sem=out_send.at[c, d], recv_sem=out_recv.at[c, d],
            device_id={"ctx": peer}, device_id_type=MESH,
        )

    def own_out(c):
        return pltpu.make_async_copy(recv.at[me, :, chunk_lanes(c)], ret.at[me, :, chunk_lanes(c)], out_own.at[c])

    for c in range(chunks):
        def send_step(i, _):
            gate_pair([lax.rem(me + 2 * i + 1, n), lax.rem(me + 2 * i + 2, n)], c)

            @pl.when(i > 0)
            def _():
                in_copy(c, 2 * i - 1).start()
                in_copy(c, 2 * i).start()

            return 0

        lax.fori_loop(0, n // 2, send_step, 0)
        in_copy(c, n - 1).start()
        own_in(c).start()

    for c in range(1, chunks):
        filter_chunk(c)

    for c in range(chunks):
        def wait_in(d, _):
            in_copy(c, d).wait()
            return 0

        lax.fori_loop(1, n, wait_in, 0)
        own_in(c).wait()
        at_lanes = chunk_lanes(c)
        short_stage(recv, c)

        def pair_step(pair, _):
            sig = jnp.dot(table_ref[0], spec[pair], preferred_element_type=F32)
            h_re, h_im = h_spec[c, pair, :LANES, :].astype(F32), h_spec[c, pair, LANES:, :].astype(F32)
            s_re, s_im = sig[:LANES], sig[LANES:]
            prod = jnp.concatenate([s_re * h_re - s_im * h_im, s_re * h_im + s_im * h_re], axis=0).astype(BF16)
            h_spec[c, pair] = jnp.dot(table_ref[1], prod, preferred_element_type=F32).astype(h_spec.dtype)
            return 0

        lax.fori_loop(0, blocks // 2, pair_step, 0, unroll=4)
        gain = gain_ref[:, at_lanes]

        def back_step(r, _):
            re_at = pl.ds(pl.multiple_of(r * step, step), step)
            im_at = pl.ds(pl.multiple_of(LANES + r * step, step), step)
            def fetch(leaf):
                re = h_spec[c, leaf // 2, re_at, leaf_lanes(leaf)].astype(F32)
                im = h_spec[c, leaf // 2, im_at, leaf_lanes(leaf)].astype(F32)
                cos, sin = twist[leaf, 0, re_at, :], twist[leaf, 1, re_at, :]
                return re * cos + im * sin, im * cos - re * sin

            parts = split_inverse(fetch, blocks, 0.0, 0)
            for a, (re, im) in enumerate(parts):
                lean = a * math.pi / (2 * blocks)
                cos, sin = math.cos(lean) / length, math.sin(lean) / length
                at = pl.ds(pl.multiple_of((a % tiles) * LANES + r * step, step), step)
                sig = recv[a // tiles, at, at_lanes].astype(F32)
                recv[a // tiles, at, at_lanes] = (cos * re + sin * im + gain * sig).astype(BF16)
            return 0

        lax.fori_loop(0, LANES // step, back_step, 0)

        def return_step(d, _):
            out_copy(c, d).start()
            return 0

        lax.fori_loop(1, n, return_step, 0)
        own_out(c).start()

    for c in range(chunks):
        def q_step(i, _):
            peers = (2 * i, 2 * i + 1)
            taps = short(0, [(0, p) for p in peers], c)
            for slot, p in enumerate(peers):
                parts = [sums_of(slot, taps[slot], start, part).astype(BF16) for start in range(0, tok, part)]
                out_ref[peer_rows(p, c), :] = across(eye[:lanes, :lanes], jnp.concatenate(parts, axis=0)).astype(BF16)
            return 0

        lax.fori_loop(0, n // 2, q_step, 0)

    def mix(peer, c):
        at = peer_rows(peer, c)
        long = across(eye[:lanes, :lanes], ret[peer, :, chunk_lanes(c)])
        out_ref[at, :] = (out_ref[at, :].astype(F32) * long).astype(BF16)
        put_copy(peer, c).start()

    def put_copy(peer, c):
        at = peer_rows(peer, c)
        return pltpu.make_async_copy(out_ref.at[at, :], out_hbm.at[at, :], put.at[c, peer])

    for c in range(chunks):
        own_out(c).wait()
        mix(me, c)

        def mix_step(d, _):
            out_copy(c, d).wait()
            mix(lax.rem(me + n - d, n), c)
            return 0

        lax.fori_loop(1, n, mix_step, 0)

    for c in range(chunks):
        def put_step(p, _):
            put_copy(p, c).wait()
            return 0

        lax.fori_loop(0, n, put_step, 0)


def wide_call(n, queries, keys, values, taps, filters, gain):
    width, tok = queries.shape
    chan, length = filters.shape
    chunks = chan // LANES
    reach = taps.shape[1]
    dma = pltpu.SemaphoreType.DMA
    there, back = wave_tables(tok)
    held = [
        pltpu.with_memory_space_constraint(x, pltpu.HBM)
        for x in (queries, keys, values, taps, filters, gain, jnp.asarray(there), jnp.asarray(back))
    ]
    return pl.pallas_call(
        functools.partial(wide_kernel, n),
        out_shape=pltpu.VMEM((width, tok), BF16),
        in_specs=[pl.BlockSpec(memory_space=pltpu.HBM)] * 8,
        out_specs=pl.BlockSpec(memory_space=pltpu.VMEM),
        scratch_shapes=[
            pltpu.VMEM((3, width, tok), BF16),
            pltpu.VMEM((3, reach, width), F32),
            pltpu.VMEM((chan, length), BF16),
            pltpu.VMEM((1, chan), F32),
            pltpu.VMEM(there.shape, BF16),
            pltpu.VMEM(back.shape, BF16),
            pltpu.VMEM((tok, tok), BF16),
            pltpu.VMEM((3, n, SLOT, chan), BF16),
            pltpu.VMEM((3, n, SLOT, chan), BF16),
            pltpu.VMEM((4, SLOT + tok, LANES), F32),
            pltpu.VMEM((2, n, SLOT + 16, LANES), F32),
            pltpu.VMEM((chunks, n, tok, LANES), BF16),
            pltpu.VMEM((chunks, n, tok, LANES), BF16),
            pltpu.VMEM((chunks, n, tok, LANES), BF16),
            pltpu.VMEM((chunks, n, tok, LANES), BF16),
            pltpu.VMEM((2, 2 * tok, chan), F32),
            pltpu.VMEM((chunks, n, 2 * tok, LANES), F32),
            pltpu.VMEM((n, 2 * tok, LANES), F32),
            pltpu.VMEM((n // 2, 2 * tok, 2 * LANES), BF16),
            dma((2, chunks, n)),
            dma,
            dma((5,)),
            dma((2,)),
            dma((2,)),
            dma((n,)),
            dma((n,)),
            dma((chunks, n)),
            dma((chunks, n)),
            dma((chunks,)),
            dma((chunks, n)),
            dma((chunks, n)),
            dma((chunks,)),
        ],
        compiler_params=pltpu.CompilerParams(
            collective_id=0, has_side_effects=True, vmem_limit_bytes=40 * 2**20
        ),
        name="hyena",
    )(*held)


def solution(mesh):
    n = mesh.shape["ctx"]

    def local(queries, keys, values, short_taps, long_filter, skip_gain):
        width, tok = queries.shape
        chan, length = long_filter.shape[1:]
        blocks = length // LANES
        lanes = min(chan, LANES)
        chunks = chan // lanes
        small_work = length * chan <= 2**20
        if n >= 2 and n & (n - 1) == 0 and chan % LANES == 0 and tok % LANES == 0 and length == n * tok and small_work:
            return wide_call(n, queries, keys, values, short_taps, long_filter[0], skip_gain)
        table = jnp.asarray(circle_tables())
        twist = jnp.asarray(twist_columns(blocks))
        dma = pltpu.SemaphoreType.DMA
        two = 2 * LANES
        small = blocks * two * max(chan, LANES) * 4 <= 8 * 2**20
        side = max(tok, LANES)
        any_space = pl.BlockSpec(memory_space=pl.ANY)
        taps = short_taps
        if lanes < LANES:
            taps = jnp.moveaxis(short_taps.reshape(3, -1, n, chan), 2, 0)
        return pl.pallas_call(
            functools.partial(kernel, n, lanes),
            out_shape=jax.ShapeDtypeStruct((width, tok), BF16),
            in_specs=[any_space if i == 4 else pl.BlockSpec(memory_space=pltpu.VMEM) for i in range(8)],
            out_specs=any_space,
            scratch_shapes=[
                pltpu.VMEM((width, tok), BF16),
                pltpu.VMEM((side, side), BF16),
                pltpu.VMEM((3, n, SLOT, chan), BF16),
                pltpu.VMEM((3, n, SLOT, chan), BF16),
                pltpu.VMEM((4, SLOT + tok, lanes), F32),
                pltpu.VMEM((n, tok, chan), BF16),
                pltpu.VMEM((n, tok, chan), BF16),
                pltpu.VMEM((blocks // 2, two, two), BF16),
                pltpu.VMEM((chunks, blocks // 2, two, two), F32 if small else BF16),
                pltpu.VMEM((n, tok, chan), BF16),
                pltpu.VMEM((chan, length), BF16),
                pltpu.VMEM((n, tok, chan), BF16),
                pltpu.VMEM((blocks, 2, LANES, lanes), F32),
                dma,
                dma((2,)),
                dma((chunks, n)),
                dma((chunks, n)),
                dma((chunks,)),
                dma((chunks, n)),
                dma((chunks, n)),
                dma((chunks,)),
                dma((chunks, n)),
            ],
            compiler_params=pltpu.CompilerParams(
                collective_id=0, has_side_effects=True, vmem_limit_bytes=67043328
            ),
            name="hyena",
        )(queries, keys, values, taps, long_filter[0], skip_gain, table, twist)

    placed = (
        P("ch", "ctx"),
        P("ch", "ctx"),
        P("ch", "ctx"),
        P(None, None, "ch"),
        P("ch", "ctx", None),
        P("ch", "ctx"),
    )
    return jax.shard_map(local, mesh=mesh, in_specs=placed, out_specs=P("ch", "ctx"), check_vma=False)
```

```python
import functools
import math

import jax
import jax.numpy as jnp
import ml_dtypes
import numpy as np
from jax import lax
from jax.experimental import pallas as pl
from jax.experimental.pallas import tpu as pltpu
from jax.sharding import PartitionSpec as P

MESH = pl.DeviceIdType.MESH
LANES = 128
SLOT = 8
F32 = jnp.float32
BF16 = jnp.bfloat16


def leaf_angles(count, theta):
    if count == 1:
        return [theta]
    return leaf_angles(count // 2, theta / 2) + leaf_angles(count // 2, theta / 2 + math.pi)


def circle_tables():
    place = np.arange(LANES, dtype=np.float64)
    angle = place[:, None] * place[None, :] * (2.0 * math.pi / LANES)
    cos, sin = np.cos(angle), np.sin(angle)
    there = np.block([[cos, -sin], [sin, cos]])
    return np.stack([there, there.T]).astype(ml_dtypes.bfloat16)


def twist_columns(count):
    roots = np.array(leaf_angles(count, 0.0)) + math.pi / (2 * count)
    angle = np.arange(LANES)[:, None] * roots[None, :] / LANES
    return np.concatenate([np.cos(angle), np.sin(angle)], axis=1).astype(np.float32)


def turn(re, im, angle):
    eighth = round(angle / (math.pi / 4))
    if abs(angle - eighth * math.pi / 4) > 1e-9:
        cos, sin = math.cos(angle), math.sin(angle)
        return cos * re - sin * im, cos * im + sin * re
    eighth %= 8
    if eighth % 2:
        re, im = math.sqrt(0.5) * (re - im), math.sqrt(0.5) * (re + im)
    return [(re, im), (-im, re), (-re, -im), (im, -re)][eighth // 2]


def split_forward(coefs, theta, first, emit):
    count = len(coefs)
    if count == 1:
        emit(first, *coefs[0])
        return
    half = count // 2
    plus, minus = [], []
    for (lo_re, lo_im), high in zip(coefs[:half], coefs[half:]):
        hi_re, hi_im = turn(*high, theta / 2)
        plus.append((lo_re + hi_re, lo_im + hi_im))
        minus.append((lo_re - hi_re, lo_im - hi_im))
    split_forward(plus, theta / 2, first, emit)
    split_forward(minus, theta / 2 + math.pi, first + half, emit)


def split_inverse(fetch, count, theta, first):
    if count == 1:
        return [fetch(first)]
    half = count // 2
    plus = split_inverse(fetch, half, theta / 2, first)
    minus = split_inverse(fetch, half, theta / 2 + math.pi, first + half)
    low, high = [], []
    for (p_re, p_im), (m_re, m_im) in zip(plus, minus):
        low.append((p_re + m_re, p_im + m_im))
        high.append(turn(p_re - m_re, p_im - m_im, -theta / 2))
    return low + high


def across(eye, block):
    return lax.dot_general(eye, block, (((1,), (1,)), ((), ())), preferred_element_type=F32)


def crossed(a, b, count):
    total, place = 0, 1
    while place < count:
        total = total + lax.rem(lax.div(a, place) + lax.div(b, place), 2) * place
        place *= 2
    return total


def wave_tables(tok):
    bins = np.concatenate([np.arange(0, tok, 2), np.arange(1, tok, 2)])
    angle = (2 * bins + 1)[:, None] * np.arange(tok)[None, :] * (math.pi / (2 * tok))
    there = np.concatenate([np.cos(angle), np.sin(angle)], axis=0)
    return there.astype(ml_dtypes.bfloat16), (there.T / tok).astype(ml_dtypes.bfloat16)


def send_order(n):
    pairs = [(m, m - 1) for m in range(n - 1, 0, -2)]
    return [(4, 2), (5, 3), (6, 7), (1, 0)] if n == 8 else pairs


def wide_kernel(
    n,
    q_hbm, k_hbm, v_hbm, taps_hbm, filt_hbm, gain_hbm, there_hbm, back_hbm,
    out_ref,
    q_ref, source, taps_ref, filt_ref, gain_ref, there_ref, back_ref,
    eye, tails, halo, q_tails, q_halo, turned_a, turned_b, rim, gated, recv, ret, q_rows,
    wave, filt_wave, sig_wave, out_wave,
    load_sem, rest_sem, q_sem, side_sem, halo_send, halo_recv,
    rim_recv, in_send, in_recv, in_own, out_send, out_recv,
):
    me = lax.axis_index("ctx")
    chunks, lanes, tok = q_hbm.shape[1:]
    reach = taps_hbm.shape[1]
    pairs = n // 2
    step = 16
    half = step // 2
    edge = 16
    part = 64
    order = send_order(n)
    first_code = sum(a * n**i for i, (a, _) in enumerate(order))
    second_code = sum(b * n**i for i, (_, b) in enumerate(order))

    barrier = pltpu.get_barrier_semaphore()
    for d in range(1, n):
        pl.semaphore_signal(
            barrier, inc=1, device_id={"ctx": lax.rem(me + d, n)}, device_id_type=MESH
        )

    def met(m):
        return crossed(me, m, n)

    def load_start(m):
        p = met(m)
        for w, ref in enumerate((k_hbm, v_hbm)):
            pltpu.make_async_copy(ref.at[p, 0], source.at[0, p, w], load_sem.at[m]).start()

    def load_wait(m):
        p = met(m)
        pltpu.make_async_copy(source.at[0, p], source.at[0, p], load_sem.at[m]).wait()

    def rest(c):
        return [
            pltpu.make_async_copy(ref.at[:, c], source.at[c, :, w], rest_sem.at[c, w])
            for w, ref in enumerate((k_hbm, v_hbm))
        ]

    side = [
        pltpu.make_async_copy(taps_hbm, taps_ref, side_sem.at[0]),
        pltpu.make_async_copy(filt_hbm, filt_ref, side_sem.at[1]),
        pltpu.make_async_copy(gain_hbm, gain_ref, side_sem.at[2]),
        pltpu.make_async_copy(there_hbm, there_ref, side_sem.at[3]),
        pltpu.make_async_copy(back_hbm, back_ref, side_sem.at[4]),
    ]
    load_q = pltpu.make_async_copy(q_hbm, q_ref, q_sem)

    for i, (a, b) in enumerate(order):
        load_start(jnp.int32(a))
        load_start(jnp.int32(b))
        if i == 0:
            side[0].start()
    for c in range(1, chunks):
        for copy in rest(c):
            copy.start()
    for i in (1, 3, 2, 4):
        side[i].start()
    load_q.start()

    size = eye.shape[0]
    row = lax.broadcasted_iota(jnp.int32, (size, size), 0)
    col = lax.broadcasted_iota(jnp.int32, (size, size), 1)
    eye[...] = (row == col).astype(F32).astype(BF16)
    pick_row = lax.broadcasted_iota(jnp.int32, (SLOT, LANES), 0) + (LANES - SLOT)
    pick = (pick_row == lax.broadcasted_iota(jnp.int32, (SLOT, LANES), 1)).astype(F32).astype(BF16)

    def peer_rows(peer, c):
        return pl.ds(pl.multiple_of((peer * chunks + c) * lanes, lanes), lanes)

    def chunk_lanes(c):
        return slice(c * lanes, (c + 1) * lanes)

    @pl.when(me == 0)
    def _():
        halo[...] = jnp.zeros_like(halo)
        q_halo[...] = jnp.zeros_like(q_halo)

    def halo_copy(which):
        mine, theirs = ((tails, halo), (q_tails, q_halo))[which]
        return pltpu.make_async_remote_copy(
            src_ref=mine, dst_ref=theirs, send_sem=halo_send.at[which], recv_sem=halo_recv.at[which],
            device_id={"ctx": lax.rem(me + 1, n)}, device_id_type=MESH,
        )

    def halo_start(which):
        @pl.when(me < n - 1)
        def _():
            halo_copy(which).start()

    def halo_wait(which):
        @pl.when(me < n - 1)
        def _():
            halo_copy(which).wait_send()

        @pl.when(me > 0)
        def _():
            halo_copy(which).wait_recv()

    def find_tails():
        for c in range(chunks):
            def one(p, _):
                block = source[c, p].reshape(2 * lanes, tok)
                tails[c, p] = across(pick, block[:, tok - LANES :]).astype(BF16)
                return 0

            lax.fori_loop(0, n, one, 0, unroll=4)

    def find_q_tails():
        def one(p, _):
            block = q_ref[p].reshape(chunks * lanes, tok)
            q_tails[p] = across(pick, block[:, tok - LANES :]).astype(BF16)
            return 0

        lax.fori_loop(0, n, one, 0, unroll=4)

    def turn(c, m, turned):
        p = met(m)
        both = across(eye[:tok, :tok], source[c, p].reshape(2 * lanes, tok))
        for w in range(2):
            rows = both[:, w * lanes : (w + 1) * lanes]
            turned[w, SLOT:, :] = rows
            if c > 0:
                turned[w, :SLOT, :] = halo[c, p, :, w * lanes : (w + 1) * lanes].astype(F32)
            else:
                rim[w, p, SLOT:, :] = rows[:edge]

    def sums_of(ref, index, taps, start, count):
        total = None
        for j in range(reach):
            at = slice(SLOT - j + start, SLOT - j + start + count)
            term = taps[j : j + 1, :] * ref[(*index, at, slice(None))]
            total = term if total is None else total + term
        return total

    def spans(first):
        marks = [first] + list(range((first // part + 1) * part, tok, part)) + [tok]
        return list(zip(marks[:-1], marks[1:]))

    def gate(c, m, turned):
        p = met(m)
        k_taps, v_taps = (taps_ref[w, :, peer_rows(p, c)] for w in (1, 2))
        for start, stop in spans(0 if c else edge):
            count = stop - start
            product = sums_of(turned, (0,), k_taps, start, count) * sums_of(turned, (1,), v_taps, start, count)
            gated[c, p, start:stop, :] = product.astype(BF16)

    def in_start(c, m):
        peer = met(m)
        at = slice(0 if c else edge, tok)
        pltpu.make_async_remote_copy(
            src_ref=gated.at[c, peer, at, :], dst_ref=recv.at[c, me, at, :],
            send_sem=in_send, recv_sem=in_recv.at[c, lax.div(m, 2)],
            device_id={"ctx": peer}, device_id_type=MESH,
        ).start()

    def rim_start(m):
        peer = met(m)
        pltpu.make_async_remote_copy(
            src_ref=gated.at[0, peer, 0:edge, :], dst_ref=recv.at[0, me, 0:edge, :],
            send_sem=in_send, recv_sem=rim_recv,
            device_id={"ctx": peer}, device_id_type=MESH,
        ).start()

    def own_in(c):
        return pltpu.make_async_copy(gated.at[c, me], recv.at[c, me], in_own.at[c])

    def out_copy(c, m):
        peer = met(m)
        return pltpu.make_async_remote_copy(
            src_ref=recv.at[c, peer], dst_ref=ret.at[c, me],
            send_sem=out_send, recv_sem=out_recv.at[c, m],
            device_id={"ctx": peer}, device_id_type=MESH,
        )

    def await_bytes(ref, sem):
        pltpu.make_async_copy(ref, ref, sem).wait()

    def gate_chunk(c):
        if c == 0:
            for m in (*order[0], order[1][0]):
                load_wait(jnp.int32(m))
            side[0].wait()
        turn(c, jnp.int32(order[0][0]), turned_a)
        if c == 0:
            pl.semaphore_wait(barrier, n - 1)

        def one(i, codes):
            a, b = lax.rem(codes[0], n), lax.rem(codes[1], n)
            codes = (lax.div(codes[0], n), lax.div(codes[1], n))
            after = lax.rem(codes[0], n)
            if c == 0:
                @pl.when(i == 1)
                def _():
                    for m in (order[1][1], *(m for pair in order[2:] for m in pair)):
                        load_wait(jnp.int32(m))
                    for k in range(1, chunks):
                        for copy in rest(k):
                            copy.wait()
                    find_tails()
                    halo_start(0)

            turn(c, b, turned_b)
            gate(c, a, turned_a)
            in_start(c, a)
            turn(c, after, turned_a)
            gate(c, b, turned_b)

            @pl.when(i < pairs - 1)
            def _():
                in_start(c, b)

            return codes

        lax.fori_loop(0, pairs, one, (jnp.int32(first_code), jnp.int32(second_code)))

    def filter_wave(d):
        wave[d % 2] = across(there_ref[...], filt_ref[:, d * tok : (d + 1) * tok])
        now, before = wave.at[d % 2], wave.at[1 - d % 2]

        def one(r, _):
            for first, sign in ((0, 1.0), (tok // 2, -1.0)):
                re_at = pl.ds(pl.multiple_of(first + r * step, step), step)
                im_at = pl.ds(pl.multiple_of(tok + first + r * step, step), step)
                re, im = now[re_at, :], now[im_at, :]
                if d > 0:
                    re, im = re + sign * before[im_at, :], im - sign * before[re_at, :]
                for c in range(chunks):
                    filt_wave[c, d, re_at, :] = re[:, chunk_lanes(c)]
                    filt_wave[c, d, im_at, :] = im[:, chunk_lanes(c)]
            return 0

        lax.fori_loop(0, tok // 2 // step, one, 0, unroll=2)

    def rim_step(p, _):
        sums = []
        for w in range(2):
            rim[w, p, :SLOT, :] = halo[0, p, :, w * lanes : (w + 1) * lanes].astype(F32)
            sums.append(sums_of(rim, (w, p), taps_ref[1 + w, :, peer_rows(p, 0)], 0, edge))
        gated[0, p, :edge, :] = (sums[0] * sums[1]).astype(BF16)
        return 0

    def sig_couple(c, first):
        both = jnp.concatenate([recv[c, first], recv[c, first + 1]], axis=1)
        both = jnp.dot(there_ref[...], both, preferred_element_type=F32)
        sig_wave[first] = both[:, :lanes]
        sig_wave[first + 1] = both[:, lanes:]

    def sig_chunk(c):
        at = slice(0 if c else edge, tok)
        if c == 0:
            await_bytes(recv.at[0, 0 : n - 1, 0:edge, :], rim_recv)
        own_in(c).wait()
        await_bytes(recv.at[c, met(jnp.int32(1)), at, :], in_recv.at[c, 0])
        sig_couple(c, 2 * lax.div(me, 2))

        def one(x, _):
            first = 2 * lax.div(met(2 * x), 2)
            await_bytes(recv.at[c, pl.ds(first, 2), at, :], in_recv.at[c, x])
            sig_couple(c, first)
            return 0

        lax.fori_loop(1, pairs, one, 0)

    def blend(c):
        def one(r, _):
            done = []
            for part_of in range(2):
                start = r * step + part_of * half
                re_at = pl.ds(pl.multiple_of(start, half), half)
                im_at = pl.ds(pl.multiple_of(tok + start, half), half)
                f_re = [filt_wave[c, d, re_at, :] for d in range(n)]
                f_im = [filt_wave[c, d, im_at, :] for d in range(n)]
                s_re = [sig_wave[d, re_at, :] for d in range(n)]
                s_im = [sig_wave[d, im_at, :] for d in range(n)]
                rows = []
                for i in range(n):
                    re = im = None
                    for j in range(i + 1):
                        a, b, x, y = f_re[i - j], f_im[i - j], s_re[j], s_im[j]
                        re = a * x - b * y if re is None else re + a * x - b * y
                        im = a * y + b * x if im is None else im + a * y + b * x
                    rows.append((re, im))
                done.append(rows)
            re_at = pl.ds(pl.multiple_of(r * step, step), step)
            im_at = pl.ds(pl.multiple_of(tok + r * step, step), step)
            for i in range(n):
                at = slice((i % 2) * lanes, (i % 2 + 1) * lanes)
                for which, rows_at in enumerate((re_at, im_at)):
                    whole = jnp.concatenate([done[0][i][which], done[1][i][which]], axis=0)
                    out_wave[i // 2, rows_at, at] = whole.astype(BF16)
            return 0

        lax.fori_loop(0, tok // step, one, 0)

    def return_chunk(c):
        gain = gain_ref[:, chunk_lanes(c)]

        def one(i, _):
            x = pairs - 1 - i
            couple = lax.div(met(2 * x), 2)
            both = jnp.dot(back_ref[...], out_wave[couple], preferred_element_type=F32)
            for k in range(2):
                sig = recv[c, 2 * couple + k].astype(F32)
                recv[c, 2 * couple + k] = (both[:, k * lanes : (k + 1) * lanes] + gain * sig).astype(BF16)

            @pl.when(x > 0)
            def _():
                out_copy(c, 2 * x).start()

            out_copy(c, 2 * x + 1).start()
            return 0

        lax.fori_loop(0, pairs, one, 0)

    def q_turn(p, turned):
        both = across(eye[:tok, :tok], q_ref[p].reshape(chunks * lanes, tok))
        for c in range(chunks):
            turned[c, SLOT:, :] = both[:, chunk_lanes(c)]
            turned[c, :SLOT, :] = q_halo[p, :, chunk_lanes(c)].astype(F32)

    def q_sums(p, turned):
        for c in range(chunks):
            taps = taps_ref[0, :, peer_rows(p, c)]
            for start in range(0, tok, part):
                q_rows[c, p, start : start + part, :] = sums_of(turned, (c,), taps, start, part).astype(BF16)

    def q_range(first, last):
        q_turn(first, turned_a)

        def one(i, _):
            p = first + 2 * i
            q_turn(p + 1, turned_b)
            q_sums(p, turned_a)
            q_turn(lax.rem(p + 2, n), turned_a)
            q_sums(p + 1, turned_b)
            return 0

        lax.fori_loop(0, (last - first) // 2, one, 0)

    def mix(ref, peer, c):
        mixed = (q_rows[c, peer].astype(F32) * ref[c, peer].astype(F32)).astype(BF16)
        out_ref[peer_rows(peer, c), :] = across(eye[:lanes, :lanes], mixed).astype(BF16)

    def mix_arrived(c, m):
        out_copy(c, m).wait_recv()
        mix(ret, met(m), c)

    def mix_chunk(c):
        mix(recv, me, c)
        mix_arrived(c, jnp.int32(1))

        def one(i, _):
            x = pairs - 1 - i
            mix_arrived(c, 2 * x)
            mix_arrived(c, 2 * x + 1)
            return 0

        lax.fori_loop(0, pairs - 1, one, 0)

    gate_chunk(0)
    for i in range(1, len(side)):
        side[i].wait()
    for d in range(n):
        filter_wave(d)
    halo_wait(0)
    lax.fori_loop(0, n, rim_step, 0, unroll=2)

    def rim_starts(m, _):
        rim_start(m)
        return 0

    lax.fori_loop(1, n, rim_starts, 0)
    own_in(0).start()
    for c in range(1, chunks):
        gate_chunk(c)
        own_in(c).start()
    load_q.wait()
    find_q_tails()
    halo_start(1)
    for c in range(chunks):
        sig_chunk(c)
        blend(c)
        return_chunk(c)
        if c == 0:
            halo_wait(1)
        q_range(c * n // chunks, (c + 1) * n // chunks)
    for c in range(chunks):
        mix_chunk(c)
    await_bytes(gated.at[:, 0 : n - 1], in_send)
    await_bytes(recv.at[:, 0 : n - 1], out_send)


def kernel(
    n, lanes,
    q_ref, k_ref, v_ref, taps_ref, filt_hbm, gain_ref, table_ref, twist_ref,
    out_hbm,
    out_ref, eye, tails, halo, turned, gated, recv, spec, h_spec, ret, filt_ref, filt_rows, twist,
    filt_sem, halo_sem, in_send, in_recv, in_own, out_send, out_recv, out_own, put,
):
    me = lax.axis_index("ctx")
    width, tok = q_ref.shape
    chan, length = filt_ref.shape
    chunks = chan // lanes
    rim = taps_ref.shape[-2]
    blocks = length // LANES
    tiles = tok // LANES
    sources = (q_ref, k_ref, v_ref)
    step = 16
    filt_copy = pltpu.make_async_copy(filt_hbm, filt_ref, filt_sem)
    filt_copy.start()

    barrier = pltpu.get_barrier_semaphore()
    for d in range(1, n):
        pl.semaphore_signal(barrier, inc=1, device_id={"ctx": lax.rem(me + d, n)}, device_id_type=MESH)

    side = eye.shape[0]
    row = lax.broadcasted_iota(jnp.int32, (side, side), 0)
    col = lax.broadcasted_iota(jnp.int32, (side, side), 1)
    eye[...] = (row == col).astype(F32).astype(BF16)

    pick_row = lax.broadcasted_iota(jnp.int32, (SLOT, LANES), 0) + (LANES - SLOT)
    pick = (pick_row == lax.broadcasted_iota(jnp.int32, (SLOT, LANES), 1)).astype(F32).astype(BF16)

    def tail_step(p, _):
        at = pl.ds(pl.multiple_of(p * chan, chan), chan)
        for w in range(3):
            tails[w, p] = across(pick, sources[w][at, tok - LANES :]).astype(BF16)
        return 0

    lax.fori_loop(0, n, tail_step, 0, unroll=4)

    pl.semaphore_wait(barrier, n - 1)
    halo_copy = pltpu.make_async_remote_copy(
        src_ref=tails, dst_ref=halo, send_sem=halo_sem.at[0], recv_sem=halo_sem.at[1],
        device_id={"ctx": lax.rem(me + 1, n)}, device_id_type=MESH,
    )

    halo_copy.start()
    if lanes < LANES:
        spec[...] = jnp.zeros_like(spec)

    filt_copy.wait()
    for a in range(blocks):
        filt_rows[a // tiles, (a % tiles) * LANES : (a % tiles + 1) * LANES, :] = across(
            eye[:LANES, :LANES], filt_ref[:, a * LANES : (a + 1) * LANES]
        ).astype(BF16)

    def chunk_lanes(c):
        return slice(c * lanes, (c + 1) * lanes)

    def leaf_lanes(leaf):
        return slice((leaf % 2) * LANES, (leaf % 2) * LANES + lanes)

    def short_stage(ref, c, first=False):
        at_lanes = chunk_lanes(c)

        def one(r, _):
            re_at = pl.ds(pl.multiple_of(r * step, step), step)
            im_at = pl.ds(pl.multiple_of(LANES + r * step, step), step)

            def emit(leaf, re, im):
                if first:
                    for which in range(2):
                        column = twist_ref[re_at, which * blocks + leaf : which * blocks + leaf + 1]
                        twist[leaf, which, re_at, :] = jnp.broadcast_to(column, (step, lanes))
                cos, sin = twist[leaf, 0, re_at, :], twist[leaf, 1, re_at, :]
                spec[leaf // 2, re_at, leaf_lanes(leaf)] = (re * cos - im * sin).astype(BF16)
                spec[leaf // 2, im_at, leaf_lanes(leaf)] = (re * sin + im * cos).astype(BF16)

            coefs = []
            for a in range(blocks):
                at = pl.ds(pl.multiple_of((a % tiles) * LANES + r * step, step), step)
                x, lean = ref[a // tiles, at, at_lanes].astype(F32), a * math.pi / (2 * blocks)
                coefs.append((x * math.cos(lean), x * math.sin(lean)))
            split_forward(coefs, 0.0, 0, emit)
            return 0

        lax.fori_loop(0, LANES // step, one, 0)

    def filter_chunk(c):
        short_stage(filt_rows, c, c == 0)

        def filt_pair(pair, _):
            h_spec[c, pair] = jnp.dot(table_ref[0], spec[pair], preferred_element_type=F32).astype(h_spec.dtype)
            return 0

        lax.fori_loop(0, blocks // 2, filt_pair, 0, unroll=2)

    filter_chunk(0)
    halo_copy.wait()

    def peer_rows(peer, c):
        return pl.ds(pl.multiple_of(peer * chan + c * lanes, lanes), lanes)

    def short(first, pair, c):
        block = jnp.concatenate([sources[w][peer_rows(peer, c), :] for w, peer in pair], axis=0)
        both = across(eye[:tok, :tok], block)
        taps = []
        for i, (w, peer) in enumerate(pair):
            turned[first + i, :SLOT, :] = jnp.where(me > 0, halo[w, peer, :, chunk_lanes(c)].astype(F32), 0.0)
            turned[first + i, SLOT:, :] = both[:, i * lanes : (i + 1) * lanes]
            if len(taps_ref.shape) == 3:
                taps.append(taps_ref[w, :, peer_rows(peer, c)])
            else:
                taps.append(taps_ref[peer, w, :, chunk_lanes(c)])
        return taps

    def sums_of(slot, taps, start, count):
        total = None
        for j in range(rim):
            term = taps[j : j + 1, :] * turned[slot, SLOT - j + start : SLOT - j + start + count, :]
            total = term if total is None else total + term
        return total

    part = 64

    def gate_pair(peers, c):
        taps = [short(2 * i, [(1, p), (2, p)], c) for i, p in enumerate(peers)]
        for i, p in enumerate(peers):
            for start in range(0, tok, part):
                product = sums_of(2 * i, taps[i][0], start, part) * sums_of(2 * i + 1, taps[i][1], start, part)
                gated[p, start : start + part, chunk_lanes(c)] = product.astype(BF16)

    def in_copy(c, d):
        peer = lax.rem(me + d, n)
        return pltpu.make_async_remote_copy(
            src_ref=gated.at[peer, :, chunk_lanes(c)], dst_ref=recv.at[me, :, chunk_lanes(c)],
            send_sem=in_send.at[c, d], recv_sem=in_recv.at[c, d],
            device_id={"ctx": peer}, device_id_type=MESH,
        )

    def own_in(c):
        return pltpu.make_async_copy(gated.at[me, :, chunk_lanes(c)], recv.at[me, :, chunk_lanes(c)], in_own.at[c])

    def out_copy(c, d):
        peer = lax.rem(me + d, n)
        return pltpu.make_async_remote_copy(
            src_ref=recv.at[peer, :, chunk_lanes(c)], dst_ref=ret.at[me, :, chunk_lanes(c)],
            send_sem=out_send.at[c, d], recv_sem=out_recv.at[c, d],
            device_id={"ctx": peer}, device_id_type=MESH,
        )

    def own_out(c):
        return pltpu.make_async_copy(recv.at[me, :, chunk_lanes(c)], ret.at[me, :, chunk_lanes(c)], out_own.at[c])

    for c in range(chunks):
        def send_step(i, _):
            gate_pair([lax.rem(me + 2 * i + 1, n), lax.rem(me + 2 * i + 2, n)], c)

            @pl.when(i > 0)
            def _():
                in_copy(c, 2 * i - 1).start()
                in_copy(c, 2 * i).start()

            return 0

        lax.fori_loop(0, n // 2, send_step, 0)
        in_copy(c, n - 1).start()
        own_in(c).start()

    for c in range(1, chunks):
        filter_chunk(c)

    for c in range(chunks):
        def wait_in(d, _):
            in_copy(c, d).wait()
            return 0

        lax.fori_loop(1, n, wait_in, 0)
        own_in(c).wait()
        at_lanes = chunk_lanes(c)
        short_stage(recv, c)

        def pair_step(pair, _):
            sig = jnp.dot(table_ref[0], spec[pair], preferred_element_type=F32)
            h_re, h_im = h_spec[c, pair, :LANES, :].astype(F32), h_spec[c, pair, LANES:, :].astype(F32)
            s_re, s_im = sig[:LANES], sig[LANES:]
            prod = jnp.concatenate([s_re * h_re - s_im * h_im, s_re * h_im + s_im * h_re], axis=0).astype(BF16)
            h_spec[c, pair] = jnp.dot(table_ref[1], prod, preferred_element_type=F32).astype(h_spec.dtype)
            return 0

        lax.fori_loop(0, blocks // 2, pair_step, 0, unroll=4)
        gain = gain_ref[:, at_lanes]

        def back_step(r, _):
            re_at = pl.ds(pl.multiple_of(r * step, step), step)
            im_at = pl.ds(pl.multiple_of(LANES + r * step, step), step)
            def fetch(leaf):
                re = h_spec[c, leaf // 2, re_at, leaf_lanes(leaf)].astype(F32)
                im = h_spec[c, leaf // 2, im_at, leaf_lanes(leaf)].astype(F32)
                cos, sin = twist[leaf, 0, re_at, :], twist[leaf, 1, re_at, :]
                return re * cos + im * sin, im * cos - re * sin

            parts = split_inverse(fetch, blocks, 0.0, 0)
            for a, (re, im) in enumerate(parts):
                lean = a * math.pi / (2 * blocks)
                cos, sin = math.cos(lean) / length, math.sin(lean) / length
                at = pl.ds(pl.multiple_of((a % tiles) * LANES + r * step, step), step)
                sig = recv[a // tiles, at, at_lanes].astype(F32)
                recv[a // tiles, at, at_lanes] = (cos * re + sin * im + gain * sig).astype(BF16)
            return 0

        lax.fori_loop(0, LANES // step, back_step, 0)

        def return_step(d, _):
            out_copy(c, d).start()
            return 0

        lax.fori_loop(1, n, return_step, 0)
        own_out(c).start()

    for c in range(chunks):
        def q_step(i, _):
            peers = (2 * i, 2 * i + 1)
            taps = short(0, [(0, p) for p in peers], c)
            for slot, p in enumerate(peers):
                parts = [sums_of(slot, taps[slot], start, part).astype(BF16) for start in range(0, tok, part)]
                out_ref[peer_rows(p, c), :] = across(eye[:lanes, :lanes], jnp.concatenate(parts, axis=0)).astype(BF16)
            return 0

        lax.fori_loop(0, n // 2, q_step, 0)

    def mix(peer, c):
        at = peer_rows(peer, c)
        long = across(eye[:lanes, :lanes], ret[peer, :, chunk_lanes(c)])
        out_ref[at, :] = (out_ref[at, :].astype(F32) * long).astype(BF16)
        put_copy(peer, c).start()

    def put_copy(peer, c):
        at = peer_rows(peer, c)
        return pltpu.make_async_copy(out_ref.at[at, :], out_hbm.at[at, :], put.at[c, peer])

    for c in range(chunks):
        own_out(c).wait()
        mix(me, c)

        def mix_step(d, _):
            out_copy(c, d).wait()
            mix(lax.rem(me + n - d, n), c)
            return 0

        lax.fori_loop(1, n, mix_step, 0)

    for c in range(chunks):
        def put_step(p, _):
            put_copy(p, c).wait()
            return 0

        lax.fori_loop(0, n, put_step, 0)


def wide_call(n, queries, keys, values, taps, filters, gain):
    width, tok = queries.shape
    chan, length = filters.shape
    chunks = chan // LANES
    reach = taps.shape[1]
    dma = pltpu.SemaphoreType.DMA
    there, back = wave_tables(tok)
    cut = [x.reshape(n, chunks, LANES, tok) for x in (queries, keys, values)]
    held = [
        pltpu.with_memory_space_constraint(x, pltpu.HBM)
        for x in (*cut, taps, filters, gain, jnp.asarray(there), jnp.asarray(back))
    ]
    return pl.pallas_call(
        functools.partial(wide_kernel, n),
        out_shape=pltpu.VMEM((width, tok), BF16),
        in_specs=[pl.BlockSpec(memory_space=pltpu.HBM)] * 8,
        out_specs=pl.BlockSpec(memory_space=pltpu.VMEM),
        scratch_shapes=[
            pltpu.VMEM((n, chunks, LANES, tok), BF16),
            pltpu.VMEM((chunks, n, 2, LANES, tok), BF16),
            pltpu.VMEM((3, reach, width), F32),
            pltpu.VMEM((chan, length), BF16),
            pltpu.VMEM((1, chan), F32),
            pltpu.VMEM(there.shape, BF16),
            pltpu.VMEM(back.shape, BF16),
            pltpu.VMEM((tok, tok), BF16),
            pltpu.VMEM((chunks, n, SLOT, 2 * LANES), BF16),
            pltpu.VMEM((chunks, n, SLOT, 2 * LANES), BF16),
            pltpu.VMEM((n, SLOT, chan), BF16),
            pltpu.VMEM((n, SLOT, chan), BF16),
            pltpu.VMEM((2, SLOT + tok, LANES), F32),
            pltpu.VMEM((2, SLOT + tok, LANES), F32),
            pltpu.VMEM((2, n, SLOT + 16, LANES), F32),
            pltpu.VMEM((chunks, n, tok, LANES), BF16),
            pltpu.VMEM((chunks, n, tok, LANES), BF16),
            pltpu.VMEM((chunks, n, tok, LANES), BF16),
            pltpu.VMEM((chunks, n, tok, LANES), BF16),
            pltpu.VMEM((2, 2 * tok, chan), F32),
            pltpu.VMEM((chunks, n, 2 * tok, LANES), F32),
            pltpu.VMEM((n, 2 * tok, LANES), F32),
            pltpu.VMEM((n // 2, 2 * tok, 2 * LANES), BF16),
            dma((n,)),
            dma((chunks, 2)),
            dma,
            dma((5,)),
            dma((2,)),
            dma((2,)),
            dma,
            dma,
            dma((chunks, n // 2)),
            dma((chunks,)),
            dma,
            dma((chunks, n)),
        ],
        compiler_params=pltpu.CompilerParams(
            collective_id=0, has_side_effects=True, vmem_limit_bytes=40 * 2**20
        ),
        name="hyena",
    )(*held)


def solution(mesh):
    n = mesh.shape["ctx"]

    def local(queries, keys, values, short_taps, long_filter, skip_gain):
        width, tok = queries.shape
        chan, length = long_filter.shape[1:]
        blocks = length // LANES
        lanes = min(chan, LANES)
        chunks = chan // lanes
        if n in (4, 8) and chan == 2 * LANES and tok == 2 * LANES and length == n * tok and width == n * chan:
            return wide_call(n, queries, keys, values, short_taps, long_filter[0], skip_gain)
        table = jnp.asarray(circle_tables())
        twist = jnp.asarray(twist_columns(blocks))
        dma = pltpu.SemaphoreType.DMA
        two = 2 * LANES
        small = blocks * two * max(chan, LANES) * 4 <= 8 * 2**20
        side = max(tok, LANES)
        any_space = pl.BlockSpec(memory_space=pl.ANY)
        taps = short_taps
        if lanes < LANES:
            taps = jnp.moveaxis(short_taps.reshape(3, -1, n, chan), 2, 0)
        return pl.pallas_call(
            functools.partial(kernel, n, lanes),
            out_shape=jax.ShapeDtypeStruct((width, tok), BF16),
            in_specs=[any_space if i == 4 else pl.BlockSpec(memory_space=pltpu.VMEM) for i in range(8)],
            out_specs=any_space,
            scratch_shapes=[
                pltpu.VMEM((width, tok), BF16),
                pltpu.VMEM((side, side), BF16),
                pltpu.VMEM((3, n, SLOT, chan), BF16),
                pltpu.VMEM((3, n, SLOT, chan), BF16),
                pltpu.VMEM((4, SLOT + tok, lanes), F32),
                pltpu.VMEM((n, tok, chan), BF16),
                pltpu.VMEM((n, tok, chan), BF16),
                pltpu.VMEM((blocks // 2, two, two), BF16),
                pltpu.VMEM((chunks, blocks // 2, two, two), F32 if small else BF16),
                pltpu.VMEM((n, tok, chan), BF16),
                pltpu.VMEM((chan, length), BF16),
                pltpu.VMEM((n, tok, chan), BF16),
                pltpu.VMEM((blocks, 2, LANES, lanes), F32),
                dma,
                dma((2,)),
                dma((chunks, n)),
                dma((chunks, n)),
                dma((chunks,)),
                dma((chunks, n)),
                dma((chunks, n)),
                dma((chunks,)),
                dma((chunks, n)),
            ],
            compiler_params=pltpu.CompilerParams(
                collective_id=0, has_side_effects=True, vmem_limit_bytes=67043328
            ),
            name="hyena",
        )(queries, keys, values, taps, long_filter[0], skip_gain, table, twist)

    placed = (
        P("ch", "ctx"),
        P("ch", "ctx"),
        P("ch", "ctx"),
        P(None, None, "ch"),
        P("ch", "ctx", None),
        P("ch", "ctx"),
    )
    return jax.shard_map(local, mesh=mesh, in_specs=placed, out_specs=P("ch", "ctx"), check_vma=False)
```

```python
import functools
import math

import jax
import jax.numpy as jnp
import ml_dtypes
import numpy as np
from jax import lax
from jax.experimental import pallas as pl
from jax.experimental.pallas import tpu as pltpu
from jax.sharding import PartitionSpec as P

MESH = pl.DeviceIdType.MESH
LANES = 128
SLOT = 8
F32 = jnp.float32
BF16 = jnp.bfloat16


def leaf_angles(count, theta):
    if count == 1:
        return [theta]
    return leaf_angles(count // 2, theta / 2) + leaf_angles(count // 2, theta / 2 + math.pi)


def circle_tables():
    place = np.arange(LANES, dtype=np.float64)
    angle = place[:, None] * place[None, :] * (2.0 * math.pi / LANES)
    cos, sin = np.cos(angle), np.sin(angle)
    there = np.block([[cos, -sin], [sin, cos]])
    return np.stack([there, there.T]).astype(ml_dtypes.bfloat16)


def twist_columns(count):
    roots = np.array(leaf_angles(count, 0.0)) + math.pi / (2 * count)
    angle = np.arange(LANES)[:, None] * roots[None, :] / LANES
    return np.concatenate([np.cos(angle), np.sin(angle)], axis=1).astype(np.float32)


def turn(re, im, angle):
    eighth = round(angle / (math.pi / 4))
    if abs(angle - eighth * math.pi / 4) > 1e-9:
        cos, sin = math.cos(angle), math.sin(angle)
        return cos * re - sin * im, cos * im + sin * re
    eighth %= 8
    if eighth % 2:
        re, im = math.sqrt(0.5) * (re - im), math.sqrt(0.5) * (re + im)
    return [(re, im), (-im, re), (-re, -im), (im, -re)][eighth // 2]


def split_forward(coefs, theta, first, emit):
    count = len(coefs)
    if count == 1:
        emit(first, *coefs[0])
        return
    half = count // 2
    plus, minus = [], []
    for (lo_re, lo_im), high in zip(coefs[:half], coefs[half:]):
        hi_re, hi_im = turn(*high, theta / 2)
        plus.append((lo_re + hi_re, lo_im + hi_im))
        minus.append((lo_re - hi_re, lo_im - hi_im))
    split_forward(plus, theta / 2, first, emit)
    split_forward(minus, theta / 2 + math.pi, first + half, emit)


def split_inverse(fetch, count, theta, first):
    if count == 1:
        return [fetch(first)]
    half = count // 2
    plus = split_inverse(fetch, half, theta / 2, first)
    minus = split_inverse(fetch, half, theta / 2 + math.pi, first + half)
    low, high = [], []
    for (p_re, p_im), (m_re, m_im) in zip(plus, minus):
        low.append((p_re + m_re, p_im + m_im))
        high.append(turn(p_re - m_re, p_im - m_im, -theta / 2))
    return low + high


def across(eye, block):
    return lax.dot_general(eye, block, (((1,), (1,)), ((), ())), preferred_element_type=F32)


def crossed(a, b, count):
    total, place = 0, 1
    while place < count:
        total = total + lax.rem(lax.div(a, place) + lax.div(b, place), 2) * place
        place *= 2
    return total


def wave_tables(tok):
    bins = np.arange(tok).reshape(-1, SLOT, 2).transpose(0, 2, 1).reshape(-1)
    angle = (2 * bins + 1)[:, None] * np.arange(tok)[None, :] * (math.pi / (2 * tok))
    there = np.concatenate([np.cos(angle), np.sin(angle)], axis=0)
    return there.astype(ml_dtypes.bfloat16), (there.T / tok).astype(ml_dtypes.bfloat16)


def send_order(n):
    pairs = [(m, m - 1) for m in range(n - 1, 0, -2)]
    return [(4, 6), (2, 7), (5, 3), (1, 0)] if n == 8 else pairs


def wide_kernel(
    n,
    q_hbm, k_hbm, v_hbm, taps_hbm, filt_hbm, gain_hbm, there_hbm, back_hbm,
    out_ref,
    q_ref, source, taps_ref, filt_ref, gain_ref, there_ref, back_ref,
    eye, tails, halo, q_tails, q_halo, turned_a, turned_b, rim, gated, recv, ret, q_rows,
    wave, filt_wave, sig_wave, out_wave,
    load_sem, rest_sem, q_sem, side_sem, halo_send, halo_recv,
    rim_recv, in_send, in_recv, in_own, out_send, out_recv,
):
    me = lax.axis_index("ctx")
    chunks, lanes, tok = q_hbm.shape[1:]
    reach = taps_hbm.shape[1]
    pairs = n // 2
    step = 16
    half = step // 2
    edge = 16
    part = 64
    order = send_order(n)
    first_code = sum(a * n**i for i, (a, _) in enumerate(order))
    second_code = sum(b * n**i for i, (_, b) in enumerate(order))

    barrier = pltpu.get_barrier_semaphore()
    for d in range(1, n):
        pl.semaphore_signal(
            barrier, inc=1, device_id={"ctx": lax.rem(me + d, n)}, device_id_type=MESH
        )

    def met(m):
        return crossed(me, m, n)

    def load_start(m):
        p = met(m)
        for w, ref in enumerate((k_hbm, v_hbm)):
            pltpu.make_async_copy(ref.at[p, 0], source.at[0, p, w], load_sem.at[m]).start()

    def load_wait(m):
        p = met(m)
        pltpu.make_async_copy(source.at[0, p], source.at[0, p], load_sem.at[m]).wait()

    def rest(c):
        return [
            pltpu.make_async_copy(ref.at[:, c], source.at[c, :, w], rest_sem.at[c, w])
            for w, ref in enumerate((k_hbm, v_hbm))
        ]

    side = [
        pltpu.make_async_copy(taps_hbm, taps_ref, side_sem.at[0]),
        pltpu.make_async_copy(filt_hbm, filt_ref, side_sem.at[1]),
        pltpu.make_async_copy(gain_hbm, gain_ref, side_sem.at[2]),
        pltpu.make_async_copy(there_hbm, there_ref, side_sem.at[3]),
        pltpu.make_async_copy(back_hbm, back_ref, side_sem.at[4]),
    ]
    load_q = pltpu.make_async_copy(q_hbm, q_ref, q_sem)

    for i, (a, b) in enumerate(order):
        load_start(jnp.int32(a))
        load_start(jnp.int32(b))
        if i == 0:
            side[0].start()
    for c in range(1, chunks):
        for copy in rest(c):
            copy.start()
    for i in (1, 3, 2, 4):
        side[i].start()
    load_q.start()

    size = eye.shape[0]
    row = lax.broadcasted_iota(jnp.int32, (size, size), 0)
    col = lax.broadcasted_iota(jnp.int32, (size, size), 1)
    eye[...] = (row == col).astype(F32).astype(BF16)
    pick_row = lax.broadcasted_iota(jnp.int32, (SLOT, LANES), 0) + (LANES - SLOT)
    pick = (pick_row == lax.broadcasted_iota(jnp.int32, (SLOT, LANES), 1)).astype(F32).astype(BF16)

    def peer_rows(peer, c):
        return pl.ds(pl.multiple_of((peer * chunks + c) * lanes, lanes), lanes)

    def chunk_lanes(c):
        return slice(c * lanes, (c + 1) * lanes)

    @pl.when(me == 0)
    def _():
        halo[...] = jnp.zeros_like(halo)
        q_halo[...] = jnp.zeros_like(q_halo)

    def halo_copy(which):
        mine, theirs = (tails.at[which], halo.at[which]) if which < chunks else (q_tails, q_halo)
        return pltpu.make_async_remote_copy(
            src_ref=mine, dst_ref=theirs, send_sem=halo_send.at[which], recv_sem=halo_recv.at[which],
            device_id={"ctx": lax.rem(me + 1, n)}, device_id_type=MESH,
        )

    def halo_start(which):
        @pl.when(me < n - 1)
        def _():
            halo_copy(which).start()

    def halo_wait(which):
        @pl.when(me < n - 1)
        def _():
            halo_copy(which).wait_send()

        @pl.when(me > 0)
        def _():
            halo_copy(which).wait_recv()

    def find_tails(c):
        def one(p, _):
            block = source[c, p].reshape(2 * lanes, tok)
            tails[c, p] = across(pick, block[:, tok - LANES :]).astype(BF16)
            return 0

        lax.fori_loop(0, n, one, 0, unroll=4)

    def find_q_tails():
        def one(p, _):
            block = q_ref[p].reshape(chunks * lanes, tok)
            q_tails[p] = across(pick, block[:, tok - LANES :]).astype(BF16)
            return 0

        lax.fori_loop(0, n, one, 0, unroll=4)

    def turn(c, m, turned):
        p = met(m)
        both = across(eye[:tok, :tok], source[c, p].reshape(2 * lanes, tok))
        for w in range(2):
            rows = both[:, w * lanes : (w + 1) * lanes]
            turned[w, SLOT:, :] = rows
            if c > 0:
                turned[w, :SLOT, :] = halo[c, p, :, w * lanes : (w + 1) * lanes].astype(F32)
            else:
                rim[w, p, SLOT:, :] = rows[:edge]

    def sums_of(ref, index, taps, start, count):
        total = None
        for j in range(reach):
            at = slice(SLOT - j + start, SLOT - j + start + count)
            term = taps[j : j + 1, :] * ref[(*index, at, slice(None))]
            total = term if total is None else total + term
        return total

    def spans(first):
        marks = [first] + list(range((first // part + 1) * part, tok, part)) + [tok]
        return list(zip(marks[:-1], marks[1:]))

    def gate(c, m, turned):
        p = met(m)
        k_taps, v_taps = (taps_ref[w, :, peer_rows(p, c)] for w in (1, 2))
        for start, stop in spans(0 if c else edge):
            count = stop - start
            product = sums_of(turned, (0,), k_taps, start, count) * sums_of(turned, (1,), v_taps, start, count)
            gated[c, p, start:stop, :] = product.astype(BF16)

    def in_start(c, m):
        peer = met(m)
        at = slice(0 if c else edge, tok)
        pltpu.make_async_remote_copy(
            src_ref=gated.at[c, peer, at, :], dst_ref=recv.at[c, me, at, :],
            send_sem=in_send, recv_sem=in_recv.at[c, lax.div(m, 2)],
            device_id={"ctx": peer}, device_id_type=MESH,
        ).start()

    def rim_start(m):
        peer = met(m)
        pltpu.make_async_remote_copy(
            src_ref=gated.at[0, peer, 0:edge, :], dst_ref=recv.at[0, me, 0:edge, :],
            send_sem=in_send, recv_sem=rim_recv.at[lax.div(m, 2)],
            device_id={"ctx": peer}, device_id_type=MESH,
        ).start()

    def own_in(c):
        return pltpu.make_async_copy(gated.at[c, me], recv.at[c, me], in_own.at[c])

    def out_copy(c, m):
        peer = met(m)
        return pltpu.make_async_remote_copy(
            src_ref=recv.at[c, peer], dst_ref=ret.at[c, me],
            send_sem=out_send, recv_sem=out_recv.at[c, m],
            device_id={"ctx": peer}, device_id_type=MESH,
        )

    def await_bytes(ref, sem):
        pltpu.make_async_copy(ref, ref, sem).wait()

    def gate_chunk(c):
        if c == 0:
            for m in (*order[0], order[1][0]):
                load_wait(jnp.int32(m))
            side[0].wait()
        turn(c, jnp.int32(order[0][0]), turned_a)

        def one(i, codes):
            a, b = lax.rem(codes[0], n), lax.rem(codes[1], n)
            codes = (lax.div(codes[0], n), lax.div(codes[1], n))
            after = lax.rem(codes[0], n)
            turn(c, b, turned_b)
            gate(c, a, turned_a)
            if c == 0:
                @pl.when(i == 0)
                def _():
                    pl.semaphore_wait(barrier, n - 1)

            in_start(c, a)
            turn(c, after, turned_a)
            gate(c, b, turned_b)

            @pl.when(i < pairs - 1)
            def _():
                in_start(c, b)

            if c == 0:
                @pl.when(i == 0)
                def _():
                    for m in (order[1][1], *(m for pair in order[2:] for m in pair)):
                        load_wait(jnp.int32(m))
                    find_tails(0)
                    halo_start(0)

                @pl.when(i == 1)
                def _():
                    for k in range(1, chunks):
                        for copy in rest(k):
                            copy.wait()
                        find_tails(k)
                        halo_start(k)

            return codes

        lax.fori_loop(0, pairs, one, (jnp.int32(first_code), jnp.int32(second_code)))

    def filter_range(first, last):
        for d in range(first, last):
            both = across(there_ref[...], filt_ref[:, d * tok : (d + 1) * tok])
            for c in range(chunks):
                filt_wave[c, d] = both[:, chunk_lanes(c)]

    def rim_step(p, _):
        sums = []
        for w in range(2):
            rim[w, p, :SLOT, :] = halo[0, p, :, w * lanes : (w + 1) * lanes].astype(F32)
            sums.append(sums_of(rim, (w, p), taps_ref[1 + w, :, peer_rows(p, 0)], 0, edge))
        gated[0, p, :edge, :] = (sums[0] * sums[1]).astype(BF16)
        return 0

    def sig_couple(c, first):
        both = jnp.concatenate([recv[c, first], recv[c, first + 1]], axis=1)
        both = jnp.dot(there_ref[...], both, preferred_element_type=F32)
        sig_wave[first] = both[:, :lanes]
        sig_wave[first + 1] = both[:, lanes:]

    def sig_chunk(c):
        at = slice(0 if c else edge, tok)
        own_in(c).wait()
        await_bytes(recv.at[c, met(jnp.int32(1)), at, :], in_recv.at[c, 0])
        if c == 0:
            await_bytes(recv.at[c, met(jnp.int32(1)), 0:edge, :], rim_recv.at[0])
        sig_couple(c, 2 * lax.div(me, 2))

        def one(x, _):
            first = 2 * lax.div(met(2 * x), 2)
            await_bytes(recv.at[c, pl.ds(first, 2), at, :], in_recv.at[c, x])
            if c == 0:
                await_bytes(recv.at[c, pl.ds(first, 2), 0:edge, :], rim_recv.at[x])
            sig_couple(c, first)
            return 0

        lax.fori_loop(1, pairs, one, 0)

    def blend(c):
        def one(r, _):
            done = []
            for part_of in range(2):
                start = r * step + part_of * half
                re_at = pl.ds(pl.multiple_of(start, half), half)
                im_at = pl.ds(pl.multiple_of(tok + start, half), half)
                f_re = [filt_wave[c, d, re_at, :] for d in range(n)]
                f_im = [filt_wave[c, d, im_at, :] for d in range(n)]
                s_re = [sig_wave[d, re_at, :] for d in range(n)]
                s_im = [sig_wave[d, im_at, :] for d in range(n)]
                rows, past = [], None
                for i in range(n):
                    re = im = None
                    for j in range(i + 1):
                        a, b, x, y = f_re[i - j], f_im[i - j], s_re[j], s_im[j]
                        re = a * x - b * y if re is None else re + a * x - b * y
                        im = a * y + b * x if im is None else im + a * y + b * x
                    if past is None:
                        rows.append((re, im))
                    elif part_of == 0:
                        rows.append((re + past[1], im - past[0]))
                    else:
                        rows.append((re - past[1], im + past[0]))
                    past = (re, im)
                done.append(rows)
            re_at = pl.ds(pl.multiple_of(r * step, step), step)
            im_at = pl.ds(pl.multiple_of(tok + r * step, step), step)
            for i in range(n):
                at = slice((i % 2) * lanes, (i % 2 + 1) * lanes)
                for which, rows_at in enumerate((re_at, im_at)):
                    whole = jnp.concatenate([done[0][i][which], done[1][i][which]], axis=0)
                    out_wave[i // 2, rows_at, at] = whole.astype(BF16)
            return 0

        lax.fori_loop(0, tok // step, one, 0)

    def return_chunk(c):
        gain = gain_ref[:, chunk_lanes(c)]

        def couple_of(x):
            return lax.div(met(2 * x), 2)

        def invert(x, slot):
            wave[slot] = jnp.dot(back_ref[...], out_wave[couple_of(x)], preferred_element_type=F32)

        def finish(x, slot):
            for k in range(2):
                p = 2 * couple_of(x) + k
                both = wave[slot, :, k * lanes : (k + 1) * lanes]
                recv[c, p] = (both + gain * recv[c, p].astype(F32)).astype(BF16)

        invert(jnp.int32(pairs - 1), 0)
        for i in range(pairs):
            x = jnp.int32(pairs - 1 - i)
            if i < pairs - 1:
                invert(x - 1, (i + 1) % 2)
            finish(x, i % 2)
            if i < pairs - 1:
                out_copy(c, 2 * x).start()
            out_copy(c, 2 * x + 1).start()

    def q_turn(p, turned):
        both = across(eye[:tok, :tok], q_ref[p].reshape(chunks * lanes, tok))
        for c in range(chunks):
            turned[c, SLOT:, :] = both[:, chunk_lanes(c)]
            turned[c, :SLOT, :] = q_halo[p, :, chunk_lanes(c)].astype(F32)

    def q_sums(p, turned):
        for c in range(chunks):
            taps = taps_ref[0, :, peer_rows(p, c)]
            for start in range(0, tok, part):
                q_rows[c, p, start : start + part, :] = sums_of(turned, (c,), taps, start, part).astype(BF16)

    def q_range(first, last):
        q_turn(first, turned_a)

        def one(i, _):
            p = first + 2 * i
            q_turn(p + 1, turned_b)
            q_sums(p, turned_a)
            q_turn(lax.rem(p + 2, n), turned_a)
            q_sums(p + 1, turned_b)
            return 0

        lax.fori_loop(0, (last - first) // 2, one, 0)

    def mix(ref, peer, c):
        mixed = (q_rows[c, peer].astype(F32) * ref[c, peer].astype(F32)).astype(BF16)
        out_ref[peer_rows(peer, c), :] = across(eye[:lanes, :lanes], mixed).astype(BF16)

    def mix_arrived(c, m):
        out_copy(c, m).wait_recv()
        mix(ret, met(m), c)

    def mix_chunk(c):
        mix(recv, me, c)
        mix_arrived(c, jnp.int32(1))

        def one(i, _):
            x = pairs - 1 - i
            mix_arrived(c, 2 * x)
            mix_arrived(c, 2 * x + 1)
            return 0

        lax.fori_loop(0, pairs - 1, one, 0)

    gate_chunk(0)
    for i in range(1, len(side)):
        side[i].wait()
    early = (3 * n) // 8
    filter_range(0, early)
    halo_wait(0)
    lax.fori_loop(0, n, rim_step, 0, unroll=2)

    def rim_starts(m, _):
        rim_start(m)
        return 0

    lax.fori_loop(1, n, rim_starts, 0)
    own_in(0).start()
    for c in range(1, chunks):
        halo_wait(c)
        gate_chunk(c)
        own_in(c).start()
    filter_range(early, n)
    load_q.wait()
    find_q_tails()
    halo_start(chunks)
    for c in range(chunks):
        sig_chunk(c)
        blend(c)
        return_chunk(c)
        if c == 0:
            halo_wait(chunks)
        q_range(c * n // chunks, (c + 1) * n // chunks)
    for c in range(chunks):
        mix_chunk(c)
    await_bytes(gated.at[:, 0 : n - 1], in_send)
    await_bytes(recv.at[:, 0 : n - 1], out_send)


def kernel(
    n, lanes,
    q_ref, k_ref, v_ref, taps_ref, filt_hbm, gain_ref, table_ref, twist_ref,
    out_hbm,
    out_ref, eye, tails, halo, turned, gated, recv, spec, h_spec, ret, filt_ref, filt_rows, twist,
    filt_sem, halo_sem, in_send, in_recv, in_own, out_send, out_recv, out_own, put,
):
    me = lax.axis_index("ctx")
    width, tok = q_ref.shape
    chan, length = filt_ref.shape
    chunks = chan // lanes
    rim = taps_ref.shape[-2]
    blocks = length // LANES
    tiles = tok // LANES
    sources = (q_ref, k_ref, v_ref)
    step = 16
    filt_copy = pltpu.make_async_copy(filt_hbm, filt_ref, filt_sem)
    filt_copy.start()

    barrier = pltpu.get_barrier_semaphore()
    for d in range(1, n):
        pl.semaphore_signal(barrier, inc=1, device_id={"ctx": lax.rem(me + d, n)}, device_id_type=MESH)

    side = eye.shape[0]
    row = lax.broadcasted_iota(jnp.int32, (side, side), 0)
    col = lax.broadcasted_iota(jnp.int32, (side, side), 1)
    eye[...] = (row == col).astype(F32).astype(BF16)

    pick_row = lax.broadcasted_iota(jnp.int32, (SLOT, LANES), 0) + (LANES - SLOT)
    pick = (pick_row == lax.broadcasted_iota(jnp.int32, (SLOT, LANES), 1)).astype(F32).astype(BF16)

    def tail_step(p, _):
        at = pl.ds(pl.multiple_of(p * chan, chan), chan)
        for w in range(3):
            tails[w, p] = across(pick, sources[w][at, tok - LANES :]).astype(BF16)
        return 0

    lax.fori_loop(0, n, tail_step, 0, unroll=4)

    pl.semaphore_wait(barrier, n - 1)
    halo_copy = pltpu.make_async_remote_copy(
        src_ref=tails, dst_ref=halo, send_sem=halo_sem.at[0], recv_sem=halo_sem.at[1],
        device_id={"ctx": lax.rem(me + 1, n)}, device_id_type=MESH,
    )

    halo_copy.start()
    if lanes < LANES:
        spec[...] = jnp.zeros_like(spec)

    filt_copy.wait()
    for a in range(blocks):
        filt_rows[a // tiles, (a % tiles) * LANES : (a % tiles + 1) * LANES, :] = across(
            eye[:LANES, :LANES], filt_ref[:, a * LANES : (a + 1) * LANES]
        ).astype(BF16)

    def chunk_lanes(c):
        return slice(c * lanes, (c + 1) * lanes)

    def leaf_lanes(leaf):
        return slice((leaf % 2) * LANES, (leaf % 2) * LANES + lanes)

    def short_stage(ref, c, first=False):
        at_lanes = chunk_lanes(c)

        def one(r, _):
            re_at = pl.ds(pl.multiple_of(r * step, step), step)
            im_at = pl.ds(pl.multiple_of(LANES + r * step, step), step)

            def emit(leaf, re, im):
                if first:
                    for which in range(2):
                        column = twist_ref[re_at, which * blocks + leaf : which * blocks + leaf + 1]
                        twist[leaf, which, re_at, :] = jnp.broadcast_to(column, (step, lanes))
                cos, sin = twist[leaf, 0, re_at, :], twist[leaf, 1, re_at, :]
                spec[leaf // 2, re_at, leaf_lanes(leaf)] = (re * cos - im * sin).astype(BF16)
                spec[leaf // 2, im_at, leaf_lanes(leaf)] = (re * sin + im * cos).astype(BF16)

            coefs = []
            for a in range(blocks):
                at = pl.ds(pl.multiple_of((a % tiles) * LANES + r * step, step), step)
                x, lean = ref[a // tiles, at, at_lanes].astype(F32), a * math.pi / (2 * blocks)
                coefs.append((x * math.cos(lean), x * math.sin(lean)))
            split_forward(coefs, 0.0, 0, emit)
            return 0

        lax.fori_loop(0, LANES // step, one, 0)

    def filter_chunk(c):
        short_stage(filt_rows, c, c == 0)

        def filt_pair(pair, _):
            h_spec[c, pair] = jnp.dot(table_ref[0], spec[pair], preferred_element_type=F32).astype(h_spec.dtype)
            return 0

        lax.fori_loop(0, blocks // 2, filt_pair, 0, unroll=2)

    filter_chunk(0)
    halo_copy.wait()

    def peer_rows(peer, c):
        return pl.ds(pl.multiple_of(peer * chan + c * lanes, lanes), lanes)

    def short(first, pair, c):
        block = jnp.concatenate([sources[w][peer_rows(peer, c), :] for w, peer in pair], axis=0)
        both = across(eye[:tok, :tok], block)
        taps = []
        for i, (w, peer) in enumerate(pair):
            turned[first + i, :SLOT, :] = jnp.where(me > 0, halo[w, peer, :, chunk_lanes(c)].astype(F32), 0.0)
            turned[first + i, SLOT:, :] = both[:, i * lanes : (i + 1) * lanes]
            if len(taps_ref.shape) == 3:
                taps.append(taps_ref[w, :, peer_rows(peer, c)])
            else:
                taps.append(taps_ref[peer, w, :, chunk_lanes(c)])
        return taps

    def sums_of(slot, taps, start, count):
        total = None
        for j in range(rim):
            term = taps[j : j + 1, :] * turned[slot, SLOT - j + start : SLOT - j + start + count, :]
            total = term if total is None else total + term
        return total

    part = 64

    def gate_pair(peers, c):
        taps = [short(2 * i, [(1, p), (2, p)], c) for i, p in enumerate(peers)]
        for i, p in enumerate(peers):
            for start in range(0, tok, part):
                product = sums_of(2 * i, taps[i][0], start, part) * sums_of(2 * i + 1, taps[i][1], start, part)
                gated[p, start : start + part, chunk_lanes(c)] = product.astype(BF16)

    def in_copy(c, d):
        peer = lax.rem(me + d, n)
        return pltpu.make_async_remote_copy(
            src_ref=gated.at[peer, :, chunk_lanes(c)], dst_ref=recv.at[me, :, chunk_lanes(c)],
            send_sem=in_send.at[c, d], recv_sem=in_recv.at[c, d],
            device_id={"ctx": peer}, device_id_type=MESH,
        )

    def own_in(c):
        return pltpu.make_async_copy(gated.at[me, :, chunk_lanes(c)], recv.at[me, :, chunk_lanes(c)], in_own.at[c])

    def out_copy(c, d):
        peer = lax.rem(me + d, n)
        return pltpu.make_async_remote_copy(
            src_ref=recv.at[peer, :, chunk_lanes(c)], dst_ref=ret.at[me, :, chunk_lanes(c)],
            send_sem=out_send.at[c, d], recv_sem=out_recv.at[c, d],
            device_id={"ctx": peer}, device_id_type=MESH,
        )

    def own_out(c):
        return pltpu.make_async_copy(recv.at[me, :, chunk_lanes(c)], ret.at[me, :, chunk_lanes(c)], out_own.at[c])

    for c in range(chunks):
        def send_step(i, _):
            gate_pair([lax.rem(me + 2 * i + 1, n), lax.rem(me + 2 * i + 2, n)], c)

            @pl.when(i > 0)
            def _():
                in_copy(c, 2 * i - 1).start()
                in_copy(c, 2 * i).start()

            return 0

        lax.fori_loop(0, n // 2, send_step, 0)
        in_copy(c, n - 1).start()
        own_in(c).start()

    for c in range(1, chunks):
        filter_chunk(c)

    for c in range(chunks):
        def wait_in(d, _):
            in_copy(c, d).wait()
            return 0

        lax.fori_loop(1, n, wait_in, 0)
        own_in(c).wait()
        at_lanes = chunk_lanes(c)
        short_stage(recv, c)

        def pair_step(pair, _):
            sig = jnp.dot(table_ref[0], spec[pair], preferred_element_type=F32)
            h_re, h_im = h_spec[c, pair, :LANES, :].astype(F32), h_spec[c, pair, LANES:, :].astype(F32)
            s_re, s_im = sig[:LANES], sig[LANES:]
            prod = jnp.concatenate([s_re * h_re - s_im * h_im, s_re * h_im + s_im * h_re], axis=0).astype(BF16)
            h_spec[c, pair] = jnp.dot(table_ref[1], prod, preferred_element_type=F32).astype(h_spec.dtype)
            return 0

        lax.fori_loop(0, blocks // 2, pair_step, 0, unroll=4)
        gain = gain_ref[:, at_lanes]

        def back_step(r, _):
            re_at = pl.ds(pl.multiple_of(r * step, step), step)
            im_at = pl.ds(pl.multiple_of(LANES + r * step, step), step)
            def fetch(leaf):
                re = h_spec[c, leaf // 2, re_at, leaf_lanes(leaf)].astype(F32)
                im = h_spec[c, leaf // 2, im_at, leaf_lanes(leaf)].astype(F32)
                cos, sin = twist[leaf, 0, re_at, :], twist[leaf, 1, re_at, :]
                return re * cos + im * sin, im * cos - re * sin

            parts = split_inverse(fetch, blocks, 0.0, 0)
            for a, (re, im) in enumerate(parts):
                lean = a * math.pi / (2 * blocks)
                cos, sin = math.cos(lean) / length, math.sin(lean) / length
                at = pl.ds(pl.multiple_of((a % tiles) * LANES + r * step, step), step)
                sig = recv[a // tiles, at, at_lanes].astype(F32)
                recv[a // tiles, at, at_lanes] = (cos * re + sin * im + gain * sig).astype(BF16)
            return 0

        lax.fori_loop(0, LANES // step, back_step, 0)

        def return_step(d, _):
            out_copy(c, d).start()
            return 0

        lax.fori_loop(1, n, return_step, 0)
        own_out(c).start()

    for c in range(chunks):
        def q_step(i, _):
            peers = (2 * i, 2 * i + 1)
            taps = short(0, [(0, p) for p in peers], c)
            for slot, p in enumerate(peers):
                parts = [sums_of(slot, taps[slot], start, part).astype(BF16) for start in range(0, tok, part)]
                out_ref[peer_rows(p, c), :] = across(eye[:lanes, :lanes], jnp.concatenate(parts, axis=0)).astype(BF16)
            return 0

        lax.fori_loop(0, n // 2, q_step, 0)

    def mix(peer, c):
        at = peer_rows(peer, c)
        long = across(eye[:lanes, :lanes], ret[peer, :, chunk_lanes(c)])
        out_ref[at, :] = (out_ref[at, :].astype(F32) * long).astype(BF16)
        put_copy(peer, c).start()

    def put_copy(peer, c):
        at = peer_rows(peer, c)
        return pltpu.make_async_copy(out_ref.at[at, :], out_hbm.at[at, :], put.at[c, peer])

    for c in range(chunks):
        own_out(c).wait()
        mix(me, c)

        def mix_step(d, _):
            out_copy(c, d).wait()
            mix(lax.rem(me + n - d, n), c)
            return 0

        lax.fori_loop(1, n, mix_step, 0)

    for c in range(chunks):
        def put_step(p, _):
            put_copy(p, c).wait()
            return 0

        lax.fori_loop(0, n, put_step, 0)


def wide_call(n, queries, keys, values, taps, filters, gain):
    width, tok = queries.shape
    chan, length = filters.shape
    chunks = chan // LANES
    reach = taps.shape[1]
    dma = pltpu.SemaphoreType.DMA
    there, back = wave_tables(tok)
    cut = [x.reshape(n, chunks, LANES, tok) for x in (queries, keys, values)]
    held = [
        pltpu.with_memory_space_constraint(x, pltpu.HBM)
        for x in (*cut, taps, filters, gain, jnp.asarray(there), jnp.asarray(back))
    ]
    return pl.pallas_call(
        functools.partial(wide_kernel, n),
        out_shape=pltpu.VMEM((width, tok), BF16),
        in_specs=[pl.BlockSpec(memory_space=pltpu.HBM)] * 8,
        out_specs=pl.BlockSpec(memory_space=pltpu.VMEM),
        scratch_shapes=[
            pltpu.VMEM((n, chunks, LANES, tok), BF16),
            pltpu.VMEM((chunks, n, 2, LANES, tok), BF16),
            pltpu.VMEM((3, reach, width), F32),
            pltpu.VMEM((chan, length), BF16),
            pltpu.VMEM((1, chan), F32),
            pltpu.VMEM(there.shape, BF16),
            pltpu.VMEM(back.shape, BF16),
            pltpu.VMEM((tok, tok), BF16),
            pltpu.VMEM((chunks, n, SLOT, 2 * LANES), BF16),
            pltpu.VMEM((chunks, n, SLOT, 2 * LANES), BF16),
            pltpu.VMEM((n, SLOT, chan), BF16),
            pltpu.VMEM((n, SLOT, chan), BF16),
            pltpu.VMEM((2, SLOT + tok, LANES), F32),
            pltpu.VMEM((2, SLOT + tok, LANES), F32),
            pltpu.VMEM((2, n, SLOT + 16, LANES), F32),
            pltpu.VMEM((chunks, n, tok, LANES), BF16),
            pltpu.VMEM((chunks, n, tok, LANES), BF16),
            pltpu.VMEM((chunks, n, tok, LANES), BF16),
            pltpu.VMEM((chunks, n, tok, LANES), BF16),
            pltpu.VMEM((2, tok, 2 * LANES), F32),
            pltpu.VMEM((chunks, n, 2 * tok, LANES), F32),
            pltpu.VMEM((n, 2 * tok, LANES), F32),
            pltpu.VMEM((n // 2, 2 * tok, 2 * LANES), BF16),
            dma((n,)),
            dma((chunks, 2)),
            dma,
            dma((5,)),
            dma((chunks + 1,)),
            dma((chunks + 1,)),
            dma((n // 2,)),
            dma,
            dma((chunks, n // 2)),
            dma((chunks,)),
            dma,
            dma((chunks, n)),
        ],
        compiler_params=pltpu.CompilerParams(
            collective_id=0, has_side_effects=True, vmem_limit_bytes=40 * 2**20
        ),
        name="hyena",
    )(*held)


def solution(mesh):
    n = mesh.shape["ctx"]

    def local(queries, keys, values, short_taps, long_filter, skip_gain):
        width, tok = queries.shape
        chan, length = long_filter.shape[1:]
        blocks = length // LANES
        lanes = min(chan, LANES)
        chunks = chan // lanes
        if n in (4, 8) and chan == 2 * LANES and tok == 2 * LANES and length == n * tok and width == n * chan:
            return wide_call(n, queries, keys, values, short_taps, long_filter[0], skip_gain)
        table = jnp.asarray(circle_tables())
        twist = jnp.asarray(twist_columns(blocks))
        dma = pltpu.SemaphoreType.DMA
        two = 2 * LANES
        small = blocks * two * max(chan, LANES) * 4 <= 8 * 2**20
        side = max(tok, LANES)
        any_space = pl.BlockSpec(memory_space=pl.ANY)
        taps = short_taps
        if lanes < LANES:
            taps = jnp.moveaxis(short_taps.reshape(3, -1, n, chan), 2, 0)
        return pl.pallas_call(
            functools.partial(kernel, n, lanes),
            out_shape=jax.ShapeDtypeStruct((width, tok), BF16),
            in_specs=[any_space if i == 4 else pl.BlockSpec(memory_space=pltpu.VMEM) for i in range(8)],
            out_specs=any_space,
            scratch_shapes=[
                pltpu.VMEM((width, tok), BF16),
                pltpu.VMEM((side, side), BF16),
                pltpu.VMEM((3, n, SLOT, chan), BF16),
                pltpu.VMEM((3, n, SLOT, chan), BF16),
                pltpu.VMEM((4, SLOT + tok, lanes), F32),
                pltpu.VMEM((n, tok, chan), BF16),
                pltpu.VMEM((n, tok, chan), BF16),
                pltpu.VMEM((blocks // 2, two, two), BF16),
                pltpu.VMEM((chunks, blocks // 2, two, two), F32 if small else BF16),
                pltpu.VMEM((n, tok, chan), BF16),
                pltpu.VMEM((chan, length), BF16),
                pltpu.VMEM((n, tok, chan), BF16),
                pltpu.VMEM((blocks, 2, LANES, lanes), F32),
                dma,
                dma((2,)),
                dma((chunks, n)),
                dma((chunks, n)),
                dma((chunks,)),
                dma((chunks, n)),
                dma((chunks, n)),
                dma((chunks,)),
                dma((chunks, n)),
            ],
            compiler_params=pltpu.CompilerParams(
                collective_id=0, has_side_effects=True, vmem_limit_bytes=67043328
            ),
            name="hyena",
        )(queries, keys, values, taps, long_filter[0], skip_gain, table, twist)

    placed = (
        P("ch", "ctx"),
        P("ch", "ctx"),
        P("ch", "ctx"),
        P(None, None, "ch"),
        P("ch", "ctx", None),
        P("ch", "ctx"),
    )
    return jax.shard_map(local, mesh=mesh, in_specs=placed, out_specs=P("ch", "ctx"), check_vma=False)
```

```python
import functools
import math

import jax
import jax.numpy as jnp
import ml_dtypes
import numpy as np
from jax import lax
from jax.experimental import pallas as pl
from jax.experimental.pallas import tpu as pltpu
from jax.sharding import PartitionSpec as P

MESH = pl.DeviceIdType.MESH
LANES = 128
SLOT = 8
F32 = jnp.float32
BF16 = jnp.bfloat16


def leaf_angles(count, theta):
    if count == 1:
        return [theta]
    return leaf_angles(count // 2, theta / 2) + leaf_angles(count // 2, theta / 2 + math.pi)


def circle_tables():
    place = np.arange(LANES, dtype=np.float64)
    angle = place[:, None] * place[None, :] * (2.0 * math.pi / LANES)
    cos, sin = np.cos(angle), np.sin(angle)
    there = np.block([[cos, -sin], [sin, cos]])
    return np.stack([there, there.T]).astype(ml_dtypes.bfloat16)


def twist_columns(count):
    roots = np.array(leaf_angles(count, 0.0)) + math.pi / (2 * count)
    angle = np.arange(LANES)[:, None] * roots[None, :] / LANES
    return np.concatenate([np.cos(angle), np.sin(angle)], axis=1).astype(np.float32)


def turn(re, im, angle):
    eighth = round(angle / (math.pi / 4))
    if abs(angle - eighth * math.pi / 4) > 1e-9:
        cos, sin = math.cos(angle), math.sin(angle)
        return cos * re - sin * im, cos * im + sin * re
    eighth %= 8
    if eighth % 2:
        re, im = math.sqrt(0.5) * (re - im), math.sqrt(0.5) * (re + im)
    return [(re, im), (-im, re), (-re, -im), (im, -re)][eighth // 2]


def split_forward(coefs, theta, first, emit):
    count = len(coefs)
    if count == 1:
        emit(first, *coefs[0])
        return
    half = count // 2
    plus, minus = [], []
    for (lo_re, lo_im), high in zip(coefs[:half], coefs[half:]):
        hi_re, hi_im = turn(*high, theta / 2)
        plus.append((lo_re + hi_re, lo_im + hi_im))
        minus.append((lo_re - hi_re, lo_im - hi_im))
    split_forward(plus, theta / 2, first, emit)
    split_forward(minus, theta / 2 + math.pi, first + half, emit)


def split_inverse(fetch, count, theta, first):
    if count == 1:
        return [fetch(first)]
    half = count // 2
    plus = split_inverse(fetch, half, theta / 2, first)
    minus = split_inverse(fetch, half, theta / 2 + math.pi, first + half)
    low, high = [], []
    for (p_re, p_im), (m_re, m_im) in zip(plus, minus):
        low.append((p_re + m_re, p_im + m_im))
        high.append(turn(p_re - m_re, p_im - m_im, -theta / 2))
    return low + high


def across(eye, block):
    return lax.dot_general(eye, block, (((1,), (1,)), ((), ())), preferred_element_type=F32)


def crossed(a, b, count):
    total, place = 0, 1
    while place < count:
        total = total + lax.rem(lax.div(a, place) + lax.div(b, place), 2) * place
        place *= 2
    return total


def wave_tables(tok):
    bins = np.arange(tok).reshape(-1, SLOT, 2).transpose(0, 2, 1).reshape(-1)
    angle = (2 * bins + 1)[:, None] * np.arange(tok)[None, :] * (math.pi / (2 * tok))
    there = np.concatenate([np.cos(angle), np.sin(angle)], axis=0)
    return there.astype(ml_dtypes.bfloat16), (there.T / tok).astype(ml_dtypes.bfloat16)


def send_order(n):
    pairs = [(m, m - 1) for m in range(n - 1, 0, -2)]
    return [(6, 7), (4, 2), (5, 3), (1, 0)] if n == 8 else pairs


def wide_kernel(
    n,
    q_hbm, k_hbm, v_hbm, taps_hbm, filt_hbm, gain_hbm, there_hbm, back_hbm,
    out_ref,
    q_ref, source, taps_ref, filt_ref, gain_ref, there_ref, back_ref,
    eye, tails, halo, q_tails, q_halo, turned_a, turned_b, rim, gated, recv, ret, sent,
    wave, filt_wave, sig_wave, out_wave,
    load_sem, rest_sem, q_sem, side_sem, halo_send, halo_recv,
    rim_recv, in_send, in_recv, in_own, out_send, out_recv,
):
    me = lax.axis_index("ctx")
    chunks, lanes, tok = q_hbm.shape[1:]
    reach = taps_hbm.shape[1]
    pairs = n // 2
    step = 16
    half = step // 2
    edge = 16
    part = 64
    order = send_order(n)
    couples = [2, 1, 3, 0] if n == 8 else list(range(pairs - 1, -1, -1))
    first_code = sum(a * n**i for i, (a, _) in enumerate(order))
    second_code = sum(b * n**i for i, (_, b) in enumerate(order))

    barrier = pltpu.get_barrier_semaphore()
    for d in range(1, n):
        pl.semaphore_signal(
            barrier, inc=1, device_id={"ctx": lax.rem(me + d, n)}, device_id_type=MESH
        )

    def met(m):
        return crossed(me, m, n)

    def load_start(m):
        p = met(m)
        for w, ref in enumerate((k_hbm, v_hbm)):
            pltpu.make_async_copy(ref.at[p, 0], source.at[0, p, w], load_sem.at[m]).start()

    def load_wait(m):
        p = met(m)
        pltpu.make_async_copy(source.at[0, p], source.at[0, p], load_sem.at[m]).wait()

    def rest(c):
        return [
            pltpu.make_async_copy(ref.at[:, c], source.at[c, :, w], rest_sem.at[c, w])
            for w, ref in enumerate((k_hbm, v_hbm))
        ]

    side = [
        pltpu.make_async_copy(taps_hbm, taps_ref, side_sem.at[0]),
        pltpu.make_async_copy(filt_hbm, filt_ref, side_sem.at[1]),
        pltpu.make_async_copy(gain_hbm, gain_ref, side_sem.at[2]),
        pltpu.make_async_copy(there_hbm, there_ref, side_sem.at[3]),
        pltpu.make_async_copy(back_hbm, back_ref, side_sem.at[4]),
    ]
    load_q = pltpu.make_async_copy(q_hbm, q_ref, q_sem)

    for i, (a, b) in enumerate(order):
        load_start(jnp.int32(a))
        load_start(jnp.int32(b))
        if i == 0:
            side[0].start()
    for c in range(1, chunks):
        for copy in rest(c):
            copy.start()
    for i in (1, 3, 2, 4):
        side[i].start()
    load_q.start()

    size = eye.shape[0]
    row = lax.broadcasted_iota(jnp.int32, (size, size), 0)
    col = lax.broadcasted_iota(jnp.int32, (size, size), 1)
    eye[...] = (row == col).astype(F32).astype(BF16)
    pick_row = lax.broadcasted_iota(jnp.int32, (SLOT, LANES), 0) + (LANES - SLOT)
    pick = (pick_row == lax.broadcasted_iota(jnp.int32, (SLOT, LANES), 1)).astype(F32).astype(BF16)

    def peer_rows(peer, c):
        return pl.ds(pl.multiple_of((peer * chunks + c) * lanes, lanes), lanes)

    def chunk_lanes(c):
        return slice(c * lanes, (c + 1) * lanes)

    @pl.when(me == 0)
    def _():
        halo[...] = jnp.zeros_like(halo)
        q_halo[...] = jnp.zeros_like(q_halo)

    def halo_copy(which):
        mine, theirs = (tails.at[which], halo.at[which]) if which < chunks else (q_tails, q_halo)
        return pltpu.make_async_remote_copy(
            src_ref=mine, dst_ref=theirs, send_sem=halo_send.at[which], recv_sem=halo_recv.at[which],
            device_id={"ctx": lax.rem(me + 1, n)}, device_id_type=MESH,
        )

    def halo_start(which):
        @pl.when(me < n - 1)
        def _():
            halo_copy(which).start()

    def halo_wait(which):
        @pl.when(me < n - 1)
        def _():
            halo_copy(which).wait_send()

        @pl.when(me > 0)
        def _():
            halo_copy(which).wait_recv()

    def find_tails(c):
        def one(p, _):
            block = source[c, p].reshape(2 * lanes, tok)
            tails[c, p] = across(pick, block[:, tok - LANES :]).astype(BF16)
            return 0

        lax.fori_loop(0, n, one, 0, unroll=4)

    def find_q_tails():
        def one(p, _):
            block = q_ref[p].reshape(chunks * lanes, tok)
            q_tails[p] = across(pick, block[:, tok - LANES :]).astype(BF16)
            return 0

        lax.fori_loop(0, n, one, 0, unroll=4)

    def turn(c, m, turned):
        p = met(m)
        both = across(eye[:tok, :tok], source[c, p].reshape(2 * lanes, tok))
        for w in range(2):
            rows = both[:, w * lanes : (w + 1) * lanes]
            turned[w, SLOT:, :] = rows
            if c > 0:
                turned[w, :SLOT, :] = halo[c, p, :, w * lanes : (w + 1) * lanes].astype(F32)
            else:
                rim[w, p, SLOT:, :] = rows[:edge]

    def sums_of(ref, index, taps, start, count):
        total = None
        for j in range(reach):
            at = slice(SLOT - j + start, SLOT - j + start + count)
            term = taps[j : j + 1, :] * ref[(*index, at, slice(None))]
            total = term if total is None else total + term
        return total

    def spans(first):
        marks = [first] + list(range((first // part + 1) * part, tok, part)) + [tok]
        return list(zip(marks[:-1], marks[1:]))

    def gate(c, m, turned):
        p = met(m)
        k_taps, v_taps = (taps_ref[w, :, peer_rows(p, c)] for w in (1, 2))
        for start, stop in spans(0 if c else edge):
            count = stop - start
            product = sums_of(turned, (0,), k_taps, start, count) * sums_of(turned, (1,), v_taps, start, count)
            gated[c, p, start:stop, :] = product.astype(BF16)

    def in_start(c, m):
        peer = met(m)
        at = slice(0 if c else edge, tok)
        pltpu.make_async_remote_copy(
            src_ref=gated.at[c, peer, at, :], dst_ref=recv.at[c, me, at, :],
            send_sem=in_send, recv_sem=in_recv.at[c, lax.div(m, 2)],
            device_id={"ctx": peer}, device_id_type=MESH,
        ).start()

    def rim_start(m):
        peer = met(m)
        pltpu.make_async_remote_copy(
            src_ref=gated.at[0, peer, 0:edge, :], dst_ref=recv.at[0, me, 0:edge, :],
            send_sem=in_send, recv_sem=rim_recv.at[lax.div(m, 2)],
            device_id={"ctx": peer}, device_id_type=MESH,
        ).start()

    def own_in(c):
        return pltpu.make_async_copy(gated.at[c, me], recv.at[c, me], in_own.at[c])

    def out_copy(c, m):
        peer = met(m)
        return pltpu.make_async_remote_copy(
            src_ref=sent.at[c, peer], dst_ref=ret.at[c, me],
            send_sem=out_send, recv_sem=out_recv.at[c, m],
            device_id={"ctx": peer}, device_id_type=MESH,
        )

    def await_bytes(ref, sem):
        pltpu.make_async_copy(ref, ref, sem).wait()

    def gate_chunk(c):
        if c == 0:
            for m in (*order[0], order[1][0]):
                load_wait(jnp.int32(m))
            side[0].wait()
        turn(c, jnp.int32(order[0][0]), turned_a)

        def one(i, codes):
            a, b = lax.rem(codes[0], n), lax.rem(codes[1], n)
            codes = (lax.div(codes[0], n), lax.div(codes[1], n))
            after = lax.rem(codes[0], n)
            turn(c, b, turned_b)
            gate(c, a, turned_a)
            if c == 0:
                @pl.when(i == 0)
                def _():
                    pl.semaphore_wait(barrier, n - 1)

            in_start(c, a)
            turn(c, after, turned_a)
            gate(c, b, turned_b)

            @pl.when(i < pairs - 1)
            def _():
                in_start(c, b)

            if c == 0:
                @pl.when(i == 0)
                def _():
                    for m in (order[1][1], *(m for pair in order[2:] for m in pair)):
                        load_wait(jnp.int32(m))
                    find_tails(0)
                    halo_start(0)

                @pl.when(i == 1)
                def _():
                    for k in range(1, chunks):
                        for copy in rest(k):
                            copy.wait()
                        find_tails(k)
                        halo_start(k)

            return codes

        lax.fori_loop(0, pairs, one, (jnp.int32(first_code), jnp.int32(second_code)))

    def filter_range(first, last):
        for d in range(first, last):
            both = across(there_ref[...], filt_ref[:, d * tok : (d + 1) * tok])
            for c in range(chunks):
                filt_wave[c, d] = both[:, chunk_lanes(c)]

    def rim_step(p, _):
        sums = []
        for w in range(2):
            rim[w, p, :SLOT, :] = halo[0, p, :, w * lanes : (w + 1) * lanes].astype(F32)
            sums.append(sums_of(rim, (w, p), taps_ref[1 + w, :, peer_rows(p, 0)], 0, edge))
        gated[0, p, :edge, :] = (sums[0] * sums[1]).astype(BF16)
        return 0

    def sig_couple(c, first):
        both = jnp.concatenate([recv[c, first], recv[c, first + 1]], axis=1)
        both = jnp.dot(there_ref[...], both, preferred_element_type=F32)
        sig_wave[first] = both[:, :lanes]
        sig_wave[first + 1] = both[:, lanes:]

    def sig_chunk(c):
        at = slice(0 if c else edge, tok)
        own_in(c).wait()
        await_bytes(recv.at[c, met(jnp.int32(1)), at, :], in_recv.at[c, 0])
        if c == 0:
            await_bytes(recv.at[c, met(jnp.int32(1)), 0:edge, :], rim_recv.at[0])
        sig_couple(c, 2 * lax.div(me, 2))

        def one(x, _):
            first = 2 * lax.div(met(2 * x), 2)
            await_bytes(recv.at[c, pl.ds(first, 2), at, :], in_recv.at[c, x])
            if c == 0:
                await_bytes(recv.at[c, pl.ds(first, 2), 0:edge, :], rim_recv.at[x])
            sig_couple(c, first)
            return 0

        lax.fori_loop(1, pairs, one, 0)

    def blend(c):
        def one(r, _):
            done = []
            for part_of in range(2):
                start = r * step + part_of * half
                re_at = pl.ds(pl.multiple_of(start, half), half)
                im_at = pl.ds(pl.multiple_of(tok + start, half), half)
                f_re = [filt_wave[c, d, re_at, :] for d in range(n)]
                f_im = [filt_wave[c, d, im_at, :] for d in range(n)]
                s_re = [sig_wave[d, re_at, :] for d in range(n)]
                s_im = [sig_wave[d, im_at, :] for d in range(n)]
                rows, past = [], None
                for i in range(n):
                    re = im = None
                    for j in range(i + 1):
                        a, b, x, y = f_re[i - j], f_im[i - j], s_re[j], s_im[j]
                        re = a * x - b * y if re is None else re + a * x - b * y
                        im = a * y + b * x if im is None else im + a * y + b * x
                    if past is None:
                        rows.append((re, im))
                    elif part_of == 0:
                        rows.append((re + past[1], im - past[0]))
                    else:
                        rows.append((re - past[1], im + past[0]))
                    past = (re, im)
                done.append(rows)
            re_at = pl.ds(pl.multiple_of(r * step, step), step)
            im_at = pl.ds(pl.multiple_of(tok + r * step, step), step)
            for i in range(n):
                at = slice((i % 2) * lanes, (i % 2 + 1) * lanes)
                for which, rows_at in enumerate((re_at, im_at)):
                    whole = jnp.concatenate([done[0][i][which], done[1][i][which]], axis=0)
                    out_wave[i // 2, rows_at, at] = whole.astype(BF16)
            return 0

        lax.fori_loop(0, tok // step, one, 0)

    def return_chunk(c):
        gain = gain_ref[:, chunk_lanes(c)]

        def couple_of(x):
            return lax.div(met(2 * x), 2)

        def invert(x, slot):
            wave[slot] = jnp.dot(back_ref[...], out_wave[couple_of(x)], preferred_element_type=F32)

        def finish(x, slot):
            for k in range(2):
                p = 2 * couple_of(x) + k
                both = wave[slot, :, k * lanes : (k + 1) * lanes]
                rows = (both + gain * recv[c, p].astype(F32)).astype(BF16)
                sent[c, p] = across(eye[:lanes, :lanes], rows).astype(BF16)

        invert(jnp.int32(couples[0]), 0)
        for i, x in enumerate(couples):
            if i < pairs - 1:
                invert(jnp.int32(couples[i + 1]), (i + 1) % 2)
            finish(jnp.int32(x), i % 2)
            if x > 0:
                out_copy(c, jnp.int32(2 * x)).start()
            out_copy(c, jnp.int32(2 * x + 1)).start()

    def q_turn(p, turned):
        both = across(eye[:tok, :tok], q_ref[p].reshape(chunks * lanes, tok))
        for c in range(chunks):
            turned[c, SLOT:, :] = both[:, chunk_lanes(c)]
            turned[c, :SLOT, :] = q_halo[p, :, chunk_lanes(c)].astype(F32)

    def q_sums(p, turned):
        for c in range(chunks):
            taps = taps_ref[0, :, peer_rows(p, c)]
            rows = [sums_of(turned, (c,), taps, start, part).astype(BF16) for start in range(0, tok, part)]
            out_ref[peer_rows(p, c), :] = across(eye[:lanes, :lanes], jnp.concatenate(rows, axis=0)).astype(BF16)

    def q_range(first, last):
        q_turn(first, turned_a)

        def one(i, _):
            p = first + 2 * i
            q_turn(p + 1, turned_b)
            q_sums(p, turned_a)
            q_turn(lax.rem(p + 2, n), turned_a)
            q_sums(p + 1, turned_b)
            return 0

        lax.fori_loop(0, (last - first) // 2, one, 0)

    def mix(ref, peer, c):
        at = peer_rows(peer, c)
        out_ref[at, :] = (out_ref[at, :].astype(F32) * ref[c, peer].astype(F32)).astype(BF16)

    def mix_arrived(c, m):
        out_copy(c, m).wait_recv()
        mix(ret, met(m), c)

    def mix_chunk(c):
        mix(sent, me, c)
        mix_arrived(c, jnp.int32(1))

        for x in couples:
            if x > 0:
                mix_arrived(c, jnp.int32(2 * x))
                mix_arrived(c, jnp.int32(2 * x + 1))

    gate_chunk(0)
    for i in range(1, len(side)):
        side[i].wait()
    early = (3 * n) // 8
    filter_range(0, early)
    halo_wait(0)
    lax.fori_loop(0, n, rim_step, 0, unroll=2)

    def rim_starts(m, _):
        rim_start(m)
        return 0

    lax.fori_loop(1, n, rim_starts, 0)
    own_in(0).start()
    for c in range(1, chunks):
        halo_wait(c)
        gate_chunk(c)
        own_in(c).start()
    filter_range(early, n)
    load_q.wait()
    find_q_tails()
    halo_start(chunks)
    for c in range(chunks):
        sig_chunk(c)
        blend(c)
        return_chunk(c)
        if c == 0:
            halo_wait(chunks)
        q_range(c * n // chunks, (c + 1) * n // chunks)
    for c in range(chunks):
        mix_chunk(c)
    await_bytes(gated.at[:, 0 : n - 1], in_send)
    await_bytes(sent.at[:, 0 : n - 1], out_send)


def kernel(
    n, lanes,
    q_ref, k_ref, v_ref, taps_ref, filt_hbm, gain_ref, table_ref, twist_ref,
    out_hbm,
    out_ref, eye, tails, halo, turned, gated, recv, spec, h_spec, ret, filt_ref, filt_rows, twist,
    filt_sem, halo_sem, in_send, in_recv, in_own, out_send, out_recv, out_own, put,
):
    me = lax.axis_index("ctx")
    width, tok = q_ref.shape
    chan, length = filt_ref.shape
    chunks = chan // lanes
    rim = taps_ref.shape[-2]
    blocks = length // LANES
    tiles = tok // LANES
    sources = (q_ref, k_ref, v_ref)
    step = 16
    filt_copy = pltpu.make_async_copy(filt_hbm, filt_ref, filt_sem)
    filt_copy.start()

    barrier = pltpu.get_barrier_semaphore()
    for d in range(1, n):
        pl.semaphore_signal(barrier, inc=1, device_id={"ctx": lax.rem(me + d, n)}, device_id_type=MESH)

    side = eye.shape[0]
    row = lax.broadcasted_iota(jnp.int32, (side, side), 0)
    col = lax.broadcasted_iota(jnp.int32, (side, side), 1)
    eye[...] = (row == col).astype(F32).astype(BF16)

    pick_row = lax.broadcasted_iota(jnp.int32, (SLOT, LANES), 0) + (LANES - SLOT)
    pick = (pick_row == lax.broadcasted_iota(jnp.int32, (SLOT, LANES), 1)).astype(F32).astype(BF16)

    def tail_step(p, _):
        at = pl.ds(pl.multiple_of(p * chan, chan), chan)
        for w in range(3):
            tails[w, p] = across(pick, sources[w][at, tok - LANES :]).astype(BF16)
        return 0

    lax.fori_loop(0, n, tail_step, 0, unroll=4)

    pl.semaphore_wait(barrier, n - 1)
    halo_copy = pltpu.make_async_remote_copy(
        src_ref=tails, dst_ref=halo, send_sem=halo_sem.at[0], recv_sem=halo_sem.at[1],
        device_id={"ctx": lax.rem(me + 1, n)}, device_id_type=MESH,
    )

    halo_copy.start()
    if lanes < LANES:
        spec[...] = jnp.zeros_like(spec)

    filt_copy.wait()
    for a in range(blocks):
        filt_rows[a // tiles, (a % tiles) * LANES : (a % tiles + 1) * LANES, :] = across(
            eye[:LANES, :LANES], filt_ref[:, a * LANES : (a + 1) * LANES]
        ).astype(BF16)

    def chunk_lanes(c):
        return slice(c * lanes, (c + 1) * lanes)

    def leaf_lanes(leaf):
        return slice((leaf % 2) * LANES, (leaf % 2) * LANES + lanes)

    def short_stage(ref, c, first=False):
        at_lanes = chunk_lanes(c)

        def one(r, _):
            re_at = pl.ds(pl.multiple_of(r * step, step), step)
            im_at = pl.ds(pl.multiple_of(LANES + r * step, step), step)

            def emit(leaf, re, im):
                if first:
                    for which in range(2):
                        column = twist_ref[re_at, which * blocks + leaf : which * blocks + leaf + 1]
                        twist[leaf, which, re_at, :] = jnp.broadcast_to(column, (step, lanes))
                cos, sin = twist[leaf, 0, re_at, :], twist[leaf, 1, re_at, :]
                spec[leaf // 2, re_at, leaf_lanes(leaf)] = (re * cos - im * sin).astype(BF16)
                spec[leaf // 2, im_at, leaf_lanes(leaf)] = (re * sin + im * cos).astype(BF16)

            coefs = []
            for a in range(blocks):
                at = pl.ds(pl.multiple_of((a % tiles) * LANES + r * step, step), step)
                x, lean = ref[a // tiles, at, at_lanes].astype(F32), a * math.pi / (2 * blocks)
                coefs.append((x * math.cos(lean), x * math.sin(lean)))
            split_forward(coefs, 0.0, 0, emit)
            return 0

        lax.fori_loop(0, LANES // step, one, 0)

    def filter_chunk(c):
        short_stage(filt_rows, c, c == 0)

        def filt_pair(pair, _):
            h_spec[c, pair] = jnp.dot(table_ref[0], spec[pair], preferred_element_type=F32).astype(h_spec.dtype)
            return 0

        lax.fori_loop(0, blocks // 2, filt_pair, 0, unroll=2)

    filter_chunk(0)
    halo_copy.wait()

    def peer_rows(peer, c):
        return pl.ds(pl.multiple_of(peer * chan + c * lanes, lanes), lanes)

    def short(first, pair, c):
        block = jnp.concatenate([sources[w][peer_rows(peer, c), :] for w, peer in pair], axis=0)
        both = across(eye[:tok, :tok], block)
        taps = []
        for i, (w, peer) in enumerate(pair):
            turned[first + i, :SLOT, :] = jnp.where(me > 0, halo[w, peer, :, chunk_lanes(c)].astype(F32), 0.0)
            turned[first + i, SLOT:, :] = both[:, i * lanes : (i + 1) * lanes]
            if len(taps_ref.shape) == 3:
                taps.append(taps_ref[w, :, peer_rows(peer, c)])
            else:
                taps.append(taps_ref[peer, w, :, chunk_lanes(c)])
        return taps

    def sums_of(slot, taps, start, count):
        total = None
        for j in range(rim):
            term = taps[j : j + 1, :] * turned[slot, SLOT - j + start : SLOT - j + start + count, :]
            total = term if total is None else total + term
        return total

    part = 64

    def gate_pair(peers, c):
        taps = [short(2 * i, [(1, p), (2, p)], c) for i, p in enumerate(peers)]
        for i, p in enumerate(peers):
            for start in range(0, tok, part):
                product = sums_of(2 * i, taps[i][0], start, part) * sums_of(2 * i + 1, taps[i][1], start, part)
                gated[p, start : start + part, chunk_lanes(c)] = product.astype(BF16)

    def in_copy(c, d):
        peer = lax.rem(me + d, n)
        return pltpu.make_async_remote_copy(
            src_ref=gated.at[peer, :, chunk_lanes(c)], dst_ref=recv.at[me, :, chunk_lanes(c)],
            send_sem=in_send.at[c, d], recv_sem=in_recv.at[c, d],
            device_id={"ctx": peer}, device_id_type=MESH,
        )

    def own_in(c):
        return pltpu.make_async_copy(gated.at[me, :, chunk_lanes(c)], recv.at[me, :, chunk_lanes(c)], in_own.at[c])

    def out_copy(c, d):
        peer = lax.rem(me + d, n)
        return pltpu.make_async_remote_copy(
            src_ref=recv.at[peer, :, chunk_lanes(c)], dst_ref=ret.at[me, :, chunk_lanes(c)],
            send_sem=out_send.at[c, d], recv_sem=out_recv.at[c, d],
            device_id={"ctx": peer}, device_id_type=MESH,
        )

    def own_out(c):
        return pltpu.make_async_copy(recv.at[me, :, chunk_lanes(c)], ret.at[me, :, chunk_lanes(c)], out_own.at[c])

    for c in range(chunks):
        def send_step(i, _):
            gate_pair([lax.rem(me + 2 * i + 1, n), lax.rem(me + 2 * i + 2, n)], c)

            @pl.when(i > 0)
            def _():
                in_copy(c, 2 * i - 1).start()
                in_copy(c, 2 * i).start()

            return 0

        lax.fori_loop(0, n // 2, send_step, 0)
        in_copy(c, n - 1).start()
        own_in(c).start()

    for c in range(1, chunks):
        filter_chunk(c)

    for c in range(chunks):
        def wait_in(d, _):
            in_copy(c, d).wait()
            return 0

        lax.fori_loop(1, n, wait_in, 0)
        own_in(c).wait()
        at_lanes = chunk_lanes(c)
        short_stage(recv, c)

        def pair_step(pair, _):
            sig = jnp.dot(table_ref[0], spec[pair], preferred_element_type=F32)
            h_re, h_im = h_spec[c, pair, :LANES, :].astype(F32), h_spec[c, pair, LANES:, :].astype(F32)
            s_re, s_im = sig[:LANES], sig[LANES:]
            prod = jnp.concatenate([s_re * h_re - s_im * h_im, s_re * h_im + s_im * h_re], axis=0).astype(BF16)
            h_spec[c, pair] = jnp.dot(table_ref[1], prod, preferred_element_type=F32).astype(h_spec.dtype)
            return 0

        lax.fori_loop(0, blocks // 2, pair_step, 0, unroll=4)
        gain = gain_ref[:, at_lanes]

        def back_step(r, _):
            re_at = pl.ds(pl.multiple_of(r * step, step), step)
            im_at = pl.ds(pl.multiple_of(LANES + r * step, step), step)
            def fetch(leaf):
                re = h_spec[c, leaf // 2, re_at, leaf_lanes(leaf)].astype(F32)
                im = h_spec[c, leaf // 2, im_at, leaf_lanes(leaf)].astype(F32)
                cos, sin = twist[leaf, 0, re_at, :], twist[leaf, 1, re_at, :]
                return re * cos + im * sin, im * cos - re * sin

            parts = split_inverse(fetch, blocks, 0.0, 0)
            for a, (re, im) in enumerate(parts):
                lean = a * math.pi / (2 * blocks)
                cos, sin = math.cos(lean) / length, math.sin(lean) / length
                at = pl.ds(pl.multiple_of((a % tiles) * LANES + r * step, step), step)
                sig = recv[a // tiles, at, at_lanes].astype(F32)
                recv[a // tiles, at, at_lanes] = (cos * re + sin * im + gain * sig).astype(BF16)
            return 0

        lax.fori_loop(0, LANES // step, back_step, 0)

        def return_step(d, _):
            out_copy(c, d).start()
            return 0

        lax.fori_loop(1, n, return_step, 0)
        own_out(c).start()

    for c in range(chunks):
        def q_step(i, _):
            peers = (2 * i, 2 * i + 1)
            taps = short(0, [(0, p) for p in peers], c)
            for slot, p in enumerate(peers):
                parts = [sums_of(slot, taps[slot], start, part).astype(BF16) for start in range(0, tok, part)]
                out_ref[peer_rows(p, c), :] = across(eye[:lanes, :lanes], jnp.concatenate(parts, axis=0)).astype(BF16)
            return 0

        lax.fori_loop(0, n // 2, q_step, 0)

    def mix(peer, c):
        at = peer_rows(peer, c)
        long = across(eye[:lanes, :lanes], ret[peer, :, chunk_lanes(c)])
        out_ref[at, :] = (out_ref[at, :].astype(F32) * long).astype(BF16)
        put_copy(peer, c).start()

    def put_copy(peer, c):
        at = peer_rows(peer, c)
        return pltpu.make_async_copy(out_ref.at[at, :], out_hbm.at[at, :], put.at[c, peer])

    for c in range(chunks):
        own_out(c).wait()
        mix(me, c)

        def mix_step(d, _):
            out_copy(c, d).wait()
            mix(lax.rem(me + n - d, n), c)
            return 0

        lax.fori_loop(1, n, mix_step, 0)

    for c in range(chunks):
        def put_step(p, _):
            put_copy(p, c).wait()
            return 0

        lax.fori_loop(0, n, put_step, 0)


def wide_call(n, queries, keys, values, taps, filters, gain):
    width, tok = queries.shape
    chan, length = filters.shape
    chunks = chan // LANES
    reach = taps.shape[1]
    dma = pltpu.SemaphoreType.DMA
    there, back = wave_tables(tok)
    cut = [x.reshape(n, chunks, LANES, tok) for x in (queries, keys, values)]
    held = [
        pltpu.with_memory_space_constraint(x, pltpu.HBM)
        for x in (*cut, taps, filters, gain, jnp.asarray(there), jnp.asarray(back))
    ]
    return pl.pallas_call(
        functools.partial(wide_kernel, n),
        out_shape=pltpu.VMEM((width, tok), BF16),
        in_specs=[pl.BlockSpec(memory_space=pltpu.HBM)] * 8,
        out_specs=pl.BlockSpec(memory_space=pltpu.VMEM),
        scratch_shapes=[
            pltpu.VMEM((n, chunks, LANES, tok), BF16),
            pltpu.VMEM((chunks, n, 2, LANES, tok), BF16),
            pltpu.VMEM((3, reach, width), F32),
            pltpu.VMEM((chan, length), BF16),
            pltpu.VMEM((1, chan), F32),
            pltpu.VMEM(there.shape, BF16),
            pltpu.VMEM(back.shape, BF16),
            pltpu.VMEM((tok, tok), BF16),
            pltpu.VMEM((chunks, n, SLOT, 2 * LANES), BF16),
            pltpu.VMEM((chunks, n, SLOT, 2 * LANES), BF16),
            pltpu.VMEM((n, SLOT, chan), BF16),
            pltpu.VMEM((n, SLOT, chan), BF16),
            pltpu.VMEM((2, SLOT + tok, LANES), F32),
            pltpu.VMEM((2, SLOT + tok, LANES), F32),
            pltpu.VMEM((2, n, SLOT + 16, LANES), F32),
            pltpu.VMEM((chunks, n, tok, LANES), BF16),
            pltpu.VMEM((chunks, n, tok, LANES), BF16),
            pltpu.VMEM((chunks, n, LANES, tok), BF16),
            pltpu.VMEM((chunks, n, LANES, tok), BF16),
            pltpu.VMEM((2, tok, 2 * LANES), F32),
            pltpu.VMEM((chunks, n, 2 * tok, LANES), F32),
            pltpu.VMEM((n, 2 * tok, LANES), F32),
            pltpu.VMEM((n // 2, 2 * tok, 2 * LANES), BF16),
            dma((n,)),
            dma((chunks, 2)),
            dma,
            dma((5,)),
            dma((chunks + 1,)),
            dma((chunks + 1,)),
            dma((n // 2,)),
            dma,
            dma((chunks, n // 2)),
            dma((chunks,)),
            dma,
            dma((chunks, n)),
        ],
        compiler_params=pltpu.CompilerParams(
            collective_id=0, has_side_effects=True, vmem_limit_bytes=40 * 2**20
        ),
        name="hyena",
    )(*held)


def solution(mesh):
    n = mesh.shape["ctx"]

    def local(queries, keys, values, short_taps, long_filter, skip_gain):
        width, tok = queries.shape
        chan, length = long_filter.shape[1:]
        blocks = length // LANES
        lanes = min(chan, LANES)
        chunks = chan // lanes
        if n in (4, 8) and chan == 2 * LANES and tok == 2 * LANES and length == n * tok and width == n * chan:
            return wide_call(n, queries, keys, values, short_taps, long_filter[0], skip_gain)
        table = jnp.asarray(circle_tables())
        twist = jnp.asarray(twist_columns(blocks))
        dma = pltpu.SemaphoreType.DMA
        two = 2 * LANES
        small = blocks * two * max(chan, LANES) * 4 <= 8 * 2**20
        side = max(tok, LANES)
        any_space = pl.BlockSpec(memory_space=pl.ANY)
        taps = short_taps
        if lanes < LANES:
            taps = jnp.moveaxis(short_taps.reshape(3, -1, n, chan), 2, 0)
        return pl.pallas_call(
            functools.partial(kernel, n, lanes),
            out_shape=jax.ShapeDtypeStruct((width, tok), BF16),
            in_specs=[any_space if i == 4 else pl.BlockSpec(memory_space=pltpu.VMEM) for i in range(8)],
            out_specs=any_space,
            scratch_shapes=[
                pltpu.VMEM((width, tok), BF16),
                pltpu.VMEM((side, side), BF16),
                pltpu.VMEM((3, n, SLOT, chan), BF16),
                pltpu.VMEM((3, n, SLOT, chan), BF16),
                pltpu.VMEM((4, SLOT + tok, lanes), F32),
                pltpu.VMEM((n, tok, chan), BF16),
                pltpu.VMEM((n, tok, chan), BF16),
                pltpu.VMEM((blocks // 2, two, two), BF16),
                pltpu.VMEM((chunks, blocks // 2, two, two), F32 if small else BF16),
                pltpu.VMEM((n, tok, chan), BF16),
                pltpu.VMEM((chan, length), BF16),
                pltpu.VMEM((n, tok, chan), BF16),
                pltpu.VMEM((blocks, 2, LANES, lanes), F32),
                dma,
                dma((2,)),
                dma((chunks, n)),
                dma((chunks, n)),
                dma((chunks,)),
                dma((chunks, n)),
                dma((chunks, n)),
                dma((chunks,)),
                dma((chunks, n)),
            ],
            compiler_params=pltpu.CompilerParams(
                collective_id=0, has_side_effects=True, vmem_limit_bytes=67043328
            ),
            name="hyena",
        )(queries, keys, values, taps, long_filter[0], skip_gain, table, twist)

    placed = (
        P("ch", "ctx"),
        P("ch", "ctx"),
        P("ch", "ctx"),
        P(None, None, "ch"),
        P("ch", "ctx", None),
        P("ch", "ctx"),
    )
    return jax.shard_map(local, mesh=mesh, in_specs=placed, out_specs=P("ch", "ctx"), check_vma=False)
```

```python
import functools
import math

import jax
import jax.numpy as jnp
import ml_dtypes
import numpy as np
from jax import lax
from jax.experimental import pallas as pl
from jax.experimental.pallas import tpu as pltpu
from jax.sharding import PartitionSpec as P

MESH = pl.DeviceIdType.MESH
LANES = 128
SLOT = 8
F32 = jnp.float32
BF16 = jnp.bfloat16


def leaf_angles(count, theta):
    if count == 1:
        return [theta]
    return leaf_angles(count // 2, theta / 2) + leaf_angles(count // 2, theta / 2 + math.pi)


def circle_tables():
    place = np.arange(LANES, dtype=np.float64)
    angle = place[:, None] * place[None, :] * (2.0 * math.pi / LANES)
    cos, sin = np.cos(angle), np.sin(angle)
    there = np.block([[cos, -sin], [sin, cos]])
    return np.stack([there, there.T]).astype(ml_dtypes.bfloat16)


def twist_columns(count):
    roots = np.array(leaf_angles(count, 0.0)) + math.pi / (2 * count)
    angle = np.arange(LANES)[:, None] * roots[None, :] / LANES
    return np.concatenate([np.cos(angle), np.sin(angle)], axis=1).astype(np.float32)


def turn(re, im, angle):
    eighth = round(angle / (math.pi / 4))
    if abs(angle - eighth * math.pi / 4) > 1e-9:
        cos, sin = math.cos(angle), math.sin(angle)
        return cos * re - sin * im, cos * im + sin * re
    eighth %= 8
    if eighth % 2:
        re, im = math.sqrt(0.5) * (re - im), math.sqrt(0.5) * (re + im)
    return [(re, im), (-im, re), (-re, -im), (im, -re)][eighth // 2]


def split_forward(coefs, theta, first, emit):
    count = len(coefs)
    if count == 1:
        emit(first, *coefs[0])
        return
    half = count // 2
    plus, minus = [], []
    for (lo_re, lo_im), high in zip(coefs[:half], coefs[half:]):
        hi_re, hi_im = turn(*high, theta / 2)
        plus.append((lo_re + hi_re, lo_im + hi_im))
        minus.append((lo_re - hi_re, lo_im - hi_im))
    split_forward(plus, theta / 2, first, emit)
    split_forward(minus, theta / 2 + math.pi, first + half, emit)


def split_inverse(fetch, count, theta, first):
    if count == 1:
        return [fetch(first)]
    half = count // 2
    plus = split_inverse(fetch, half, theta / 2, first)
    minus = split_inverse(fetch, half, theta / 2 + math.pi, first + half)
    low, high = [], []
    for (p_re, p_im), (m_re, m_im) in zip(plus, minus):
        low.append((p_re + m_re, p_im + m_im))
        high.append(turn(p_re - m_re, p_im - m_im, -theta / 2))
    return low + high


def across(eye, block):
    return lax.dot_general(eye, block, (((1,), (1,)), ((), ())), preferred_element_type=F32)


def crossed(a, b, count):
    total, place = 0, 1
    while place < count:
        total = total + lax.rem(lax.div(a, place) + lax.div(b, place), 2) * place
        place *= 2
    return total


def wave_tables(tok):
    bins = np.arange(tok).reshape(-1, SLOT, 2).transpose(0, 2, 1).reshape(-1)
    angle = (2 * bins + 1)[:, None] * np.arange(tok)[None, :] * (math.pi / (2 * tok))
    there = np.concatenate([np.cos(angle), np.sin(angle)], axis=0)
    return there.astype(ml_dtypes.bfloat16), (there.T / tok).astype(ml_dtypes.bfloat16)


def send_order(n):
    pairs = [(m, m - 1) for m in range(n - 1, 0, -2)]
    return [(6, 7), (4, 2), (5, 3), (1, 0)] if n == 8 else pairs


def wide_kernel(
    n,
    q_hbm, k_hbm, v_hbm, taps_hbm, filt_hbm, gain_hbm, there_hbm, back_hbm,
    out_ref,
    q_ref, source, taps_ref, filt_ref, gain_ref, there_ref, back_ref,
    eye, tails, halo, q_tails, q_halo, turned_a, turned_b, rim, gated, recv, ret, sent,
    wave, filt_wave, sig_wave, out_wave,
    load_sem, rest_sem, q_sem, side_sem, halo_send, halo_recv,
    rim_recv, in_send, in_recv, in_own, out_send, out_recv,
):
    me = lax.axis_index("ctx")
    chunks, lanes, tok = q_hbm.shape[1:]
    reach = taps_hbm.shape[1]
    pairs = n // 2
    step = 16
    half = step // 2
    edge = 16
    part = 64
    order = send_order(n)
    couples = [2, 1, 3, 0] if n == 8 else list(range(pairs - 1, -1, -1))
    first_code = sum(a * n**i for i, (a, _) in enumerate(order))
    second_code = sum(b * n**i for i, (_, b) in enumerate(order))

    barrier = pltpu.get_barrier_semaphore()
    beside = me + 1 - 2 * lax.rem(me, 2)
    pair = me - lax.rem(me, 2)
    for peer in (n - 1 - me, n - 1 - beside):
        pl.semaphore_signal(barrier, inc=1, device_id={"ctx": peer}, device_id_type=MESH)
    for x in range(2, n - 2, 2):
        for peer in (crossed(me, jnp.int32(x), n), crossed(beside, jnp.int32(x), n)):
            pl.semaphore_signal(barrier, inc=1, device_id={"ctx": peer}, device_id_type=MESH)
    pl.semaphore_signal(barrier, inc=1, device_id={"ctx": beside}, device_id_type=MESH)

    def met(m):
        return crossed(me, m, n)

    needed = [m for pair in order for m in pair]

    def load_start(m, slot):
        p = met(jnp.int32(m))
        for w, ref in enumerate((k_hbm, v_hbm)):
            pltpu.make_async_copy(ref.at[p, 0], source.at[0, p, w], load_sem.at[slot]).start()

    def load_wait(m, slot):
        p = met(jnp.int32(m))
        pltpu.make_async_copy(source.at[0, p], source.at[0, p], load_sem.at[slot]).wait()

    def rest(c):
        return [
            pltpu.make_async_copy(ref.at[:, c], source.at[c, :, w], rest_sem.at[c, w])
            for w, ref in enumerate((k_hbm, v_hbm))
        ]

    side = [
        pltpu.make_async_copy(taps_hbm, taps_ref, side_sem.at[0]),
        pltpu.make_async_copy(filt_hbm, filt_ref, side_sem.at[1]),
        pltpu.make_async_copy(gain_hbm, gain_ref, side_sem.at[2]),
        pltpu.make_async_copy(there_hbm, there_ref, side_sem.at[3]),
        pltpu.make_async_copy(back_hbm, back_ref, side_sem.at[4]),
    ]
    load_q = pltpu.make_async_copy(q_hbm, q_ref, q_sem)

    for i, m in enumerate(needed):
        load_start(m, min(i, 3))
        if i == 1:
            side[0].start()
    for c in range(1, chunks):
        for copy in rest(c):
            copy.start()
    for i in (1, 3, 2, 4):
        side[i].start()
    load_q.start()

    size = eye.shape[0]
    row = lax.broadcasted_iota(jnp.int32, (size, size), 0)
    col = lax.broadcasted_iota(jnp.int32, (size, size), 1)
    eye[...] = (row == col).astype(F32).astype(BF16)
    pick_row = lax.broadcasted_iota(jnp.int32, (SLOT, LANES), 0) + (LANES - SLOT)
    pick = (pick_row == lax.broadcasted_iota(jnp.int32, (SLOT, LANES), 1)).astype(F32).astype(BF16)

    def peer_rows(peer, c):
        return pl.ds(pl.multiple_of((peer * chunks + c) * lanes, lanes), lanes)

    def chunk_lanes(c):
        return slice(c * lanes, (c + 1) * lanes)

    @pl.when(me == 0)
    def _():
        halo[...] = jnp.zeros_like(halo)
        q_halo[...] = jnp.zeros_like(q_halo)

    def halo_copy(which):
        mine, theirs = (tails.at[which], halo.at[which]) if which < chunks else (q_tails, q_halo)
        return pltpu.make_async_remote_copy(
            src_ref=mine, dst_ref=theirs, send_sem=halo_send.at[which], recv_sem=halo_recv.at[which],
            device_id={"ctx": lax.rem(me + 1, n)}, device_id_type=MESH,
        )

    def halo_start(which):
        @pl.when(me < n - 1)
        def _():
            halo_copy(which).start()

    def halo_wait(which):
        @pl.when(me < n - 1)
        def _():
            halo_copy(which).wait_send()

        @pl.when(me > 0)
        def _():
            halo_copy(which).wait_recv()

    def find_tails(c):
        def one(p, _):
            block = source[c, p].reshape(2 * lanes, tok)
            tails[c, p] = across(pick, block[:, tok - LANES :]).astype(BF16)
            return 0

        lax.fori_loop(0, n, one, 0, unroll=4)

    def find_q_tails():
        def one(p, _):
            block = q_ref[p].reshape(chunks * lanes, tok)
            q_tails[p] = across(pick, block[:, tok - LANES :]).astype(BF16)
            return 0

        lax.fori_loop(0, n, one, 0, unroll=4)

    def turn(c, m, turned):
        p = met(m)
        both = across(eye[:tok, :tok], source[c, p].reshape(2 * lanes, tok))
        for w in range(2):
            rows = both[:, w * lanes : (w + 1) * lanes]
            turned[w, SLOT:, :] = rows
            if c > 0:
                turned[w, :SLOT, :] = halo[c, p, :, w * lanes : (w + 1) * lanes].astype(F32)
            else:
                rim[w, p, SLOT:, :] = rows[:edge]

    def sums_of(ref, index, taps, start, count):
        total = None
        for j in range(reach):
            at = slice(SLOT - j + start, SLOT - j + start + count)
            term = taps[j : j + 1, :] * ref[(*index, at, slice(None))]
            total = term if total is None else total + term
        return total

    def spans(first):
        marks = [first] + list(range((first // part + 1) * part, tok, part)) + [tok]
        return list(zip(marks[:-1], marks[1:]))

    def gate(c, m, turned):
        p = met(m)
        k_taps, v_taps = (taps_ref[w, :, peer_rows(p, c)] for w in (1, 2))
        for start, stop in spans(0 if c else edge):
            count = stop - start
            product = sums_of(turned, (0,), k_taps, start, count) * sums_of(turned, (1,), v_taps, start, count)
            gated[c, p, start:stop, :] = product.astype(BF16)

    def in_start(c, m):
        peer = met(m)
        at = slice(0 if c else edge, tok)
        pltpu.make_async_remote_copy(
            src_ref=gated.at[c, peer, at, :], dst_ref=recv.at[c, me, at, :],
            send_sem=in_send, recv_sem=in_recv.at[c, lax.div(m, 2)],
            device_id={"ctx": peer}, device_id_type=MESH,
        ).start()

    def rim_start(m):
        peer = met(m)
        pltpu.make_async_remote_copy(
            src_ref=gated.at[0, peer, 0:edge, :], dst_ref=recv.at[0, me, 0:edge, :],
            send_sem=in_send, recv_sem=rim_recv.at[lax.div(m, 2)],
            device_id={"ctx": peer}, device_id_type=MESH,
        ).start()

    def own_in(c):
        return pltpu.make_async_copy(gated.at[c, me], recv.at[c, me], in_own.at[c])

    def out_copy(c, m):
        peer = met(m)
        return pltpu.make_async_remote_copy(
            src_ref=sent.at[c, peer], dst_ref=ret.at[c, me],
            send_sem=out_send, recv_sem=out_recv.at[0 if c == 0 else (c - 1) * (n - 1) + m],
            device_id={"ctx": peer}, device_id_type=MESH,
        )

    def await_bytes(ref, sem):
        pltpu.make_async_copy(ref, ref, sem).wait()

    def gate_chunk(c):
        if c == 0:
            for i, m in enumerate(needed[:3]):
                load_wait(m, i)
            side[0].wait()
        turn(c, jnp.int32(order[0][0]), turned_a)

        def one(i, codes):
            a, b = lax.rem(codes[0], n), lax.rem(codes[1], n)
            codes = (lax.div(codes[0], n), lax.div(codes[1], n))
            after = lax.rem(codes[0], n)
            turn(c, b, turned_b)
            gate(c, a, turned_a)
            if c == 0:
                @pl.when(i == 0)
                def _():
                    pl.semaphore_wait(barrier, n - 1)

            in_start(c, a)
            turn(c, after, turned_a)
            gate(c, b, turned_b)

            @pl.when(i < pairs - 1)
            def _():
                in_start(c, b)

            if c == 0:
                @pl.when(i == 0)
                def _():
                    await_bytes(source.at[0, 0 : n - 3], load_sem.at[3])
                    find_tails(0)
                    halo_start(0)

                @pl.when(i == 1)
                def _():
                    for k in range(1, chunks):
                        for copy in rest(k):
                            copy.wait()
                        find_tails(k)
                        halo_start(k)

            return codes

        lax.fori_loop(0, pairs, one, (jnp.int32(first_code), jnp.int32(second_code)))

    def filter_range(first, last):
        for d in range(first, last):
            both = across(there_ref[...], filt_ref[:, d * tok : (d + 1) * tok])
            for c in range(chunks):
                filt_wave[c, d] = both[:, chunk_lanes(c)]

    def rim_step(p, _):
        sums = []
        for w in range(2):
            rim[w, p, :SLOT, :] = halo[0, p, :, w * lanes : (w + 1) * lanes].astype(F32)
            sums.append(sums_of(rim, (w, p), taps_ref[1 + w, :, peer_rows(p, 0)], 0, edge))
        gated[0, p, :edge, :] = (sums[0] * sums[1]).astype(BF16)
        return 0

    def sig_couple(c, first):
        both = jnp.concatenate([recv[c, first], recv[c, first + 1]], axis=1)
        both = jnp.dot(there_ref[...], both, preferred_element_type=F32)
        sig_wave[first] = both[:, :lanes]
        sig_wave[first + 1] = both[:, lanes:]

    def sig_chunk(c):
        at = slice(0 if c else edge, tok)
        own_in(c).wait()
        await_bytes(recv.at[c, met(jnp.int32(1)), at, :], in_recv.at[c, 0])
        if c == 0:
            await_bytes(recv.at[c, met(jnp.int32(1)), 0:edge, :], rim_recv.at[0])
        sig_couple(c, 2 * lax.div(me, 2))

        def one(x, _):
            first = 2 * lax.div(met(2 * x), 2)
            await_bytes(recv.at[c, pl.ds(first, 2), at, :], in_recv.at[c, x])
            if c == 0:
                await_bytes(recv.at[c, pl.ds(first, 2), 0:edge, :], rim_recv.at[x])
            sig_couple(c, first)
            return 0

        lax.fori_loop(1, pairs, one, 0)

    def blend(c):
        def one(r, _):
            done = []
            for part_of in range(2):
                start = r * step + part_of * half
                re_at = pl.ds(pl.multiple_of(start, half), half)
                im_at = pl.ds(pl.multiple_of(tok + start, half), half)
                f_re = [filt_wave[c, d, re_at, :] for d in range(n)]
                f_im = [filt_wave[c, d, im_at, :] for d in range(n)]
                s_re = [sig_wave[d, re_at, :] for d in range(n)]
                s_im = [sig_wave[d, im_at, :] for d in range(n)]
                rows, past = [], None
                for i in range(n):
                    re = im = None
                    for j in range(i + 1):
                        a, b, x, y = f_re[i - j], f_im[i - j], s_re[j], s_im[j]
                        re = a * x - b * y if re is None else re + a * x - b * y
                        im = a * y + b * x if im is None else im + a * y + b * x
                    if past is None:
                        rows.append((re, im))
                    elif part_of == 0:
                        rows.append((re + past[1], im - past[0]))
                    else:
                        rows.append((re - past[1], im + past[0]))
                    past = (re, im)
                done.append(rows)
            re_at = pl.ds(pl.multiple_of(r * step, step), step)
            im_at = pl.ds(pl.multiple_of(tok + r * step, step), step)
            for i in range(n):
                at = slice((i % 2) * lanes, (i % 2 + 1) * lanes)
                for which, rows_at in enumerate((re_at, im_at)):
                    whole = jnp.concatenate([done[0][i][which], done[1][i][which]], axis=0)
                    out_wave[i // 2, rows_at, at] = whole.astype(BF16)
            return 0

        lax.fori_loop(0, tok // step, one, 0)

    def return_chunk(c):
        gain = gain_ref[:, chunk_lanes(c)]

        def couple_of(x):
            return lax.div(met(2 * x), 2)

        def invert(x, slot):
            wave[slot] = jnp.dot(back_ref[...], out_wave[couple_of(x)], preferred_element_type=F32)

        def finish(x, slot):
            for k in range(2):
                p = 2 * couple_of(x) + k
                both = wave[slot, :, k * lanes : (k + 1) * lanes]
                rows = (both + gain * recv[c, p].astype(F32)).astype(BF16)
                sent[c, p] = across(eye[:lanes, :lanes], rows).astype(BF16)

        invert(jnp.int32(couples[0]), 0)
        for i, x in enumerate(couples):
            if i < pairs - 1:
                invert(jnp.int32(couples[i + 1]), (i + 1) % 2)
            finish(jnp.int32(x), i % 2)
            if x > 0:
                out_copy(c, jnp.int32(2 * x)).start()
            out_copy(c, jnp.int32(2 * x + 1)).start()

    def q_turn(p, turned):
        both = across(eye[:tok, :tok], q_ref[p].reshape(chunks * lanes, tok))
        for c in range(chunks):
            turned[c, SLOT:, :] = both[:, chunk_lanes(c)]
            turned[c, :SLOT, :] = q_halo[p, :, chunk_lanes(c)].astype(F32)

    def q_sums(p, turned):
        for c in range(chunks):
            taps = taps_ref[0, :, peer_rows(p, c)]
            rows = [sums_of(turned, (c,), taps, start, part).astype(BF16) for start in range(0, tok, part)]
            out_ref[peer_rows(p, c), :] = across(eye[:lanes, :lanes], jnp.concatenate(rows, axis=0)).astype(BF16)

    def q_range(first, last):
        q_turn(first, turned_a)

        def one(i, _):
            p = first + 2 * i
            q_turn(p + 1, turned_b)
            q_sums(p, turned_a)
            q_turn(lax.rem(p + 2, n), turned_a)
            q_sums(p + 1, turned_b)
            return 0

        lax.fori_loop(0, (last - first) // 2, one, 0)

    def mix(ref, peer, c):
        at = peer_rows(peer, c)
        out_ref[at, :] = (out_ref[at, :].astype(F32) * ref[c, peer].astype(F32)).astype(BF16)

    def mix_arrived(c, m):
        if c > 0:
            out_copy(c, m).wait_recv()
        mix(ret, met(m), c)

    def mix_chunk(c):
        mix(sent, me, c)
        if c == 0:
            await_bytes(ret.at[0, 0 : n - 1], out_recv.at[0])
        mix_arrived(c, jnp.int32(1))

        for x in couples:
            if x > 0:
                mix_arrived(c, jnp.int32(2 * x))
                mix_arrived(c, jnp.int32(2 * x + 1))

    gate_chunk(0)
    for i in range(1, len(side)):
        side[i].wait()
    early = (3 * n) // 8
    filter_range(0, early)
    halo_wait(0)
    lax.fori_loop(0, n, rim_step, 0, unroll=2)

    def rim_starts(m, _):
        rim_start(m)
        return 0

    lax.fori_loop(1, n, rim_starts, 0)
    own_in(0).start()
    for c in range(1, chunks):
        halo_wait(c)
        gate_chunk(c)
        own_in(c).start()
    filter_range(early, n)
    load_q.wait()
    find_q_tails()
    halo_start(chunks)
    for c in range(chunks):
        sig_chunk(c)
        blend(c)
        return_chunk(c)
        if c == 0:
            halo_wait(chunks)
        q_range(c * n // chunks, (c + 1) * n // chunks)
    for c in range(chunks):
        mix_chunk(c)
    await_bytes(gated.at[:, 0 : n - 1], in_send)
    await_bytes(sent.at[:, 0 : n - 1], out_send)


def kernel(
    n, lanes,
    q_ref, k_ref, v_ref, taps_ref, filt_hbm, gain_ref, table_ref, twist_ref,
    out_hbm,
    out_ref, eye, tails, halo, turned, gated, recv, spec, h_spec, ret, filt_ref, filt_rows, twist,
    filt_sem, halo_sem, in_send, in_recv, in_own, out_send, out_recv, out_own, put,
):
    me = lax.axis_index("ctx")
    width, tok = q_ref.shape
    chan, length = filt_ref.shape
    chunks = chan // lanes
    rim = taps_ref.shape[-2]
    blocks = length // LANES
    tiles = tok // LANES
    sources = (q_ref, k_ref, v_ref)
    step = 16
    filt_copy = pltpu.make_async_copy(filt_hbm, filt_ref, filt_sem)
    filt_copy.start()

    barrier = pltpu.get_barrier_semaphore()
    for d in range(1, n):
        pl.semaphore_signal(barrier, inc=1, device_id={"ctx": lax.rem(me + d, n)}, device_id_type=MESH)

    side = eye.shape[0]
    row = lax.broadcasted_iota(jnp.int32, (side, side), 0)
    col = lax.broadcasted_iota(jnp.int32, (side, side), 1)
    eye[...] = (row == col).astype(F32).astype(BF16)

    pick_row = lax.broadcasted_iota(jnp.int32, (SLOT, LANES), 0) + (LANES - SLOT)
    pick = (pick_row == lax.broadcasted_iota(jnp.int32, (SLOT, LANES), 1)).astype(F32).astype(BF16)

    def tail_step(p, _):
        at = pl.ds(pl.multiple_of(p * chan, chan), chan)
        for w in range(3):
            tails[w, p] = across(pick, sources[w][at, tok - LANES :]).astype(BF16)
        return 0

    lax.fori_loop(0, n, tail_step, 0, unroll=4)

    pl.semaphore_wait(barrier, n - 1)
    halo_copy = pltpu.make_async_remote_copy(
        src_ref=tails, dst_ref=halo, send_sem=halo_sem.at[0], recv_sem=halo_sem.at[1],
        device_id={"ctx": lax.rem(me + 1, n)}, device_id_type=MESH,
    )

    halo_copy.start()
    if lanes < LANES:
        spec[...] = jnp.zeros_like(spec)

    filt_copy.wait()
    for a in range(blocks):
        filt_rows[a // tiles, (a % tiles) * LANES : (a % tiles + 1) * LANES, :] = across(
            eye[:LANES, :LANES], filt_ref[:, a * LANES : (a + 1) * LANES]
        ).astype(BF16)

    def chunk_lanes(c):
        return slice(c * lanes, (c + 1) * lanes)

    def leaf_lanes(leaf):
        return slice((leaf % 2) * LANES, (leaf % 2) * LANES + lanes)

    def short_stage(ref, c, first=False):
        at_lanes = chunk_lanes(c)

        def one(r, _):
            re_at = pl.ds(pl.multiple_of(r * step, step), step)
            im_at = pl.ds(pl.multiple_of(LANES + r * step, step), step)

            def emit(leaf, re, im):
                if first:
                    for which in range(2):
                        column = twist_ref[re_at, which * blocks + leaf : which * blocks + leaf + 1]
                        twist[leaf, which, re_at, :] = jnp.broadcast_to(column, (step, lanes))
                cos, sin = twist[leaf, 0, re_at, :], twist[leaf, 1, re_at, :]
                spec[leaf // 2, re_at, leaf_lanes(leaf)] = (re * cos - im * sin).astype(BF16)
                spec[leaf // 2, im_at, leaf_lanes(leaf)] = (re * sin + im * cos).astype(BF16)

            coefs = []
            for a in range(blocks):
                at = pl.ds(pl.multiple_of((a % tiles) * LANES + r * step, step), step)
                x, lean = ref[a // tiles, at, at_lanes].astype(F32), a * math.pi / (2 * blocks)
                coefs.append((x * math.cos(lean), x * math.sin(lean)))
            split_forward(coefs, 0.0, 0, emit)
            return 0

        lax.fori_loop(0, LANES // step, one, 0)

    def filter_chunk(c):
        short_stage(filt_rows, c, c == 0)

        def filt_pair(pair, _):
            h_spec[c, pair] = jnp.dot(table_ref[0], spec[pair], preferred_element_type=F32).astype(h_spec.dtype)
            return 0

        lax.fori_loop(0, blocks // 2, filt_pair, 0, unroll=2)

    filter_chunk(0)
    halo_copy.wait()

    def peer_rows(peer, c):
        return pl.ds(pl.multiple_of(peer * chan + c * lanes, lanes), lanes)

    def short(first, pair, c):
        block = jnp.concatenate([sources[w][peer_rows(peer, c), :] for w, peer in pair], axis=0)
        both = across(eye[:tok, :tok], block)
        taps = []
        for i, (w, peer) in enumerate(pair):
            turned[first + i, :SLOT, :] = jnp.where(me > 0, halo[w, peer, :, chunk_lanes(c)].astype(F32), 0.0)
            turned[first + i, SLOT:, :] = both[:, i * lanes : (i + 1) * lanes]
            if len(taps_ref.shape) == 3:
                taps.append(taps_ref[w, :, peer_rows(peer, c)])
            else:
                taps.append(taps_ref[peer, w, :, chunk_lanes(c)])
        return taps

    def sums_of(slot, taps, start, count):
        total = None
        for j in range(rim):
            term = taps[j : j + 1, :] * turned[slot, SLOT - j + start : SLOT - j + start + count, :]
            total = term if total is None else total + term
        return total

    part = 64

    def gate_pair(peers, c):
        taps = [short(2 * i, [(1, p), (2, p)], c) for i, p in enumerate(peers)]
        for i, p in enumerate(peers):
            for start in range(0, tok, part):
                product = sums_of(2 * i, taps[i][0], start, part) * sums_of(2 * i + 1, taps[i][1], start, part)
                gated[p, start : start + part, chunk_lanes(c)] = product.astype(BF16)

    def in_copy(c, d):
        peer = lax.rem(me + d, n)
        return pltpu.make_async_remote_copy(
            src_ref=gated.at[peer, :, chunk_lanes(c)], dst_ref=recv.at[me, :, chunk_lanes(c)],
            send_sem=in_send.at[c, d], recv_sem=in_recv.at[c, d],
            device_id={"ctx": peer}, device_id_type=MESH,
        )

    def own_in(c):
        return pltpu.make_async_copy(gated.at[me, :, chunk_lanes(c)], recv.at[me, :, chunk_lanes(c)], in_own.at[c])

    def out_copy(c, d):
        peer = lax.rem(me + d, n)
        return pltpu.make_async_remote_copy(
            src_ref=recv.at[peer, :, chunk_lanes(c)], dst_ref=ret.at[me, :, chunk_lanes(c)],
            send_sem=out_send.at[c, d], recv_sem=out_recv.at[c, d],
            device_id={"ctx": peer}, device_id_type=MESH,
        )

    def own_out(c):
        return pltpu.make_async_copy(recv.at[me, :, chunk_lanes(c)], ret.at[me, :, chunk_lanes(c)], out_own.at[c])

    for c in range(chunks):
        def send_step(i, _):
            gate_pair([lax.rem(me + 2 * i + 1, n), lax.rem(me + 2 * i + 2, n)], c)

            @pl.when(i > 0)
            def _():
                in_copy(c, 2 * i - 1).start()
                in_copy(c, 2 * i).start()

            return 0

        lax.fori_loop(0, n // 2, send_step, 0)
        in_copy(c, n - 1).start()
        own_in(c).start()

    for c in range(1, chunks):
        filter_chunk(c)

    for c in range(chunks):
        def wait_in(d, _):
            in_copy(c, d).wait()
            return 0

        lax.fori_loop(1, n, wait_in, 0)
        own_in(c).wait()
        at_lanes = chunk_lanes(c)
        short_stage(recv, c)

        def pair_step(pair, _):
            sig = jnp.dot(table_ref[0], spec[pair], preferred_element_type=F32)
            h_re, h_im = h_spec[c, pair, :LANES, :].astype(F32), h_spec[c, pair, LANES:, :].astype(F32)
            s_re, s_im = sig[:LANES], sig[LANES:]
            prod = jnp.concatenate([s_re * h_re - s_im * h_im, s_re * h_im + s_im * h_re], axis=0).astype(BF16)
            h_spec[c, pair] = jnp.dot(table_ref[1], prod, preferred_element_type=F32).astype(h_spec.dtype)
            return 0

        lax.fori_loop(0, blocks // 2, pair_step, 0, unroll=4)
        gain = gain_ref[:, at_lanes]

        def back_step(r, _):
            re_at = pl.ds(pl.multiple_of(r * step, step), step)
            im_at = pl.ds(pl.multiple_of(LANES + r * step, step), step)
            def fetch(leaf):
                re = h_spec[c, leaf // 2, re_at, leaf_lanes(leaf)].astype(F32)
                im = h_spec[c, leaf // 2, im_at, leaf_lanes(leaf)].astype(F32)
                cos, sin = twist[leaf, 0, re_at, :], twist[leaf, 1, re_at, :]
                return re * cos + im * sin, im * cos - re * sin

            parts = split_inverse(fetch, blocks, 0.0, 0)
            for a, (re, im) in enumerate(parts):
                lean = a * math.pi / (2 * blocks)
                cos, sin = math.cos(lean) / length, math.sin(lean) / length
                at = pl.ds(pl.multiple_of((a % tiles) * LANES + r * step, step), step)
                sig = recv[a // tiles, at, at_lanes].astype(F32)
                recv[a // tiles, at, at_lanes] = (cos * re + sin * im + gain * sig).astype(BF16)
            return 0

        lax.fori_loop(0, LANES // step, back_step, 0)

        def return_step(d, _):
            out_copy(c, d).start()
            return 0

        lax.fori_loop(1, n, return_step, 0)
        own_out(c).start()

    for c in range(chunks):
        def q_step(i, _):
            peers = (2 * i, 2 * i + 1)
            taps = short(0, [(0, p) for p in peers], c)
            for slot, p in enumerate(peers):
                parts = [sums_of(slot, taps[slot], start, part).astype(BF16) for start in range(0, tok, part)]
                out_ref[peer_rows(p, c), :] = across(eye[:lanes, :lanes], jnp.concatenate(parts, axis=0)).astype(BF16)
            return 0

        lax.fori_loop(0, n // 2, q_step, 0)

    def mix(peer, c):
        at = peer_rows(peer, c)
        long = across(eye[:lanes, :lanes], ret[peer, :, chunk_lanes(c)])
        out_ref[at, :] = (out_ref[at, :].astype(F32) * long).astype(BF16)
        put_copy(peer, c).start()

    def put_copy(peer, c):
        at = peer_rows(peer, c)
        return pltpu.make_async_copy(out_ref.at[at, :], out_hbm.at[at, :], put.at[c, peer])

    for c in range(chunks):
        own_out(c).wait()
        mix(me, c)

        def mix_step(d, _):
            out_copy(c, d).wait()
            mix(lax.rem(me + n - d, n), c)
            return 0

        lax.fori_loop(1, n, mix_step, 0)

    for c in range(chunks):
        def put_step(p, _):
            put_copy(p, c).wait()
            return 0

        lax.fori_loop(0, n, put_step, 0)


def wide_call(n, queries, keys, values, taps, filters, gain):
    width, tok = queries.shape
    chan, length = filters.shape
    chunks = chan // LANES
    reach = taps.shape[1]
    dma = pltpu.SemaphoreType.DMA
    there, back = wave_tables(tok)
    cut = [x.reshape(n, chunks, LANES, tok) for x in (queries, keys, values)]
    held = [
        pltpu.with_memory_space_constraint(x, pltpu.HBM)
        for x in (*cut, taps, filters, gain, jnp.asarray(there), jnp.asarray(back))
    ]
    return pl.pallas_call(
        functools.partial(wide_kernel, n),
        out_shape=pltpu.VMEM((width, tok), BF16),
        in_specs=[pl.BlockSpec(memory_space=pltpu.HBM)] * 8,
        out_specs=pl.BlockSpec(memory_space=pltpu.VMEM),
        scratch_shapes=[
            pltpu.VMEM((n, chunks, LANES, tok), BF16),
            pltpu.VMEM((chunks, n, 2, LANES, tok), BF16),
            pltpu.VMEM((3, reach, width), F32),
            pltpu.VMEM((chan, length), BF16),
            pltpu.VMEM((1, chan), F32),
            pltpu.VMEM(there.shape, BF16),
            pltpu.VMEM(back.shape, BF16),
            pltpu.VMEM((tok, tok), BF16),
            pltpu.VMEM((chunks, n, SLOT, 2 * LANES), BF16),
            pltpu.VMEM((chunks, n, SLOT, 2 * LANES), BF16),
            pltpu.VMEM((n, SLOT, chan), BF16),
            pltpu.VMEM((n, SLOT, chan), BF16),
            pltpu.VMEM((2, SLOT + tok, LANES), F32),
            pltpu.VMEM((2, SLOT + tok, LANES), F32),
            pltpu.VMEM((2, n, SLOT + 16, LANES), F32),
            pltpu.VMEM((chunks, n, tok, LANES), BF16),
            pltpu.VMEM((chunks, n, tok, LANES), BF16),
            pltpu.VMEM((chunks, n, LANES, tok), BF16),
            pltpu.VMEM((chunks, n, LANES, tok), BF16),
            pltpu.VMEM((2, tok, 2 * LANES), F32),
            pltpu.VMEM((chunks, n, 2 * tok, LANES), F32),
            pltpu.VMEM((n, 2 * tok, LANES), F32),
            pltpu.VMEM((n // 2, 2 * tok, 2 * LANES), BF16),
            dma((4,)),
            dma((chunks, 2)),
            dma,
            dma((5,)),
            dma((chunks + 1,)),
            dma((chunks + 1,)),
            dma((n // 2,)),
            dma,
            dma((chunks, n // 2)),
            dma((chunks,)),
            dma,
            dma(((chunks - 1) * (n - 1) + 1,)),
        ],
        compiler_params=pltpu.CompilerParams(
            collective_id=0, has_side_effects=True, vmem_limit_bytes=40 * 2**20
        ),
        name="hyena",
    )(*held)


def solution(mesh):
    n = mesh.shape["ctx"]

    def local(queries, keys, values, short_taps, long_filter, skip_gain):
        width, tok = queries.shape
        chan, length = long_filter.shape[1:]
        blocks = length // LANES
        lanes = min(chan, LANES)
        chunks = chan // lanes
        if n in (4, 8) and chan == 2 * LANES and tok == 2 * LANES and length == n * tok and width == n * chan:
            return wide_call(n, queries, keys, values, short_taps, long_filter[0], skip_gain)
        table = jnp.asarray(circle_tables())
        twist = jnp.asarray(twist_columns(blocks))
        dma = pltpu.SemaphoreType.DMA
        two = 2 * LANES
        small = blocks * two * max(chan, LANES) * 4 <= 8 * 2**20
        side = max(tok, LANES)
        any_space = pl.BlockSpec(memory_space=pl.ANY)
        taps = short_taps
        if lanes < LANES:
            taps = jnp.moveaxis(short_taps.reshape(3, -1, n, chan), 2, 0)
        return pl.pallas_call(
            functools.partial(kernel, n, lanes),
            out_shape=jax.ShapeDtypeStruct((width, tok), BF16),
            in_specs=[any_space if i == 4 else pl.BlockSpec(memory_space=pltpu.VMEM) for i in range(8)],
            out_specs=any_space,
            scratch_shapes=[
                pltpu.VMEM((width, tok), BF16),
                pltpu.VMEM((side, side), BF16),
                pltpu.VMEM((3, n, SLOT, chan), BF16),
                pltpu.VMEM((3, n, SLOT, chan), BF16),
                pltpu.VMEM((4, SLOT + tok, lanes), F32),
                pltpu.VMEM((n, tok, chan), BF16),
                pltpu.VMEM((n, tok, chan), BF16),
                pltpu.VMEM((blocks // 2, two, two), BF16),
                pltpu.VMEM((chunks, blocks // 2, two, two), F32 if small else BF16),
                pltpu.VMEM((n, tok, chan), BF16),
                pltpu.VMEM((chan, length), BF16),
                pltpu.VMEM((n, tok, chan), BF16),
                pltpu.VMEM((blocks, 2, LANES, lanes), F32),
                dma,
                dma((2,)),
                dma((chunks, n)),
                dma((chunks, n)),
                dma((chunks,)),
                dma((chunks, n)),
                dma((chunks, n)),
                dma((chunks,)),
                dma((chunks, n)),
            ],
            compiler_params=pltpu.CompilerParams(
                collective_id=0, has_side_effects=True, vmem_limit_bytes=67043328
            ),
            name="hyena",
        )(queries, keys, values, taps, long_filter[0], skip_gain, table, twist)

    placed = (
        P("ch", "ctx"),
        P("ch", "ctx"),
        P("ch", "ctx"),
        P(None, None, "ch"),
        P("ch", "ctx", None),
        P("ch", "ctx"),
    )
    return jax.shard_map(local, mesh=mesh, in_specs=placed, out_specs=P("ch", "ctx"), check_vma=False)
```

```python
import functools
import math

import jax
import jax.numpy as jnp
import ml_dtypes
import numpy as np
from jax import lax
from jax.experimental import pallas as pl
from jax.experimental.pallas import tpu as pltpu
from jax.sharding import PartitionSpec as P

MESH = pl.DeviceIdType.MESH
LANES = 128
SLOT = 8
F32 = jnp.float32
BF16 = jnp.bfloat16


def leaf_angles(count, theta):
    if count == 1:
        return [theta]
    return leaf_angles(count // 2, theta / 2) + leaf_angles(count // 2, theta / 2 + math.pi)


def circle_tables():
    place = np.arange(LANES, dtype=np.float64)
    angle = place[:, None] * place[None, :] * (2.0 * math.pi / LANES)
    cos, sin = np.cos(angle), np.sin(angle)
    there = np.block([[cos, -sin], [sin, cos]])
    return np.stack([there, there.T]).astype(ml_dtypes.bfloat16)


def twist_columns(count):
    roots = np.array(leaf_angles(count, 0.0)) + math.pi / (2 * count)
    angle = np.arange(LANES)[:, None] * roots[None, :] / LANES
    return np.concatenate([np.cos(angle), np.sin(angle)], axis=1).astype(np.float32)


def turn(re, im, angle):
    eighth = round(angle / (math.pi / 4))
    if abs(angle - eighth * math.pi / 4) > 1e-9:
        cos, sin = math.cos(angle), math.sin(angle)
        return cos * re - sin * im, cos * im + sin * re
    eighth %= 8
    if eighth % 2:
        re, im = math.sqrt(0.5) * (re - im), math.sqrt(0.5) * (re + im)
    return [(re, im), (-im, re), (-re, -im), (im, -re)][eighth // 2]


def split_forward(coefs, theta, first, emit):
    count = len(coefs)
    if count == 1:
        emit(first, *coefs[0])
        return
    half = count // 2
    plus, minus = [], []
    for (lo_re, lo_im), high in zip(coefs[:half], coefs[half:]):
        hi_re, hi_im = turn(*high, theta / 2)
        plus.append((lo_re + hi_re, lo_im + hi_im))
        minus.append((lo_re - hi_re, lo_im - hi_im))
    split_forward(plus, theta / 2, first, emit)
    split_forward(minus, theta / 2 + math.pi, first + half, emit)


def split_inverse(fetch, count, theta, first):
    if count == 1:
        return [fetch(first)]
    half = count // 2
    plus = split_inverse(fetch, half, theta / 2, first)
    minus = split_inverse(fetch, half, theta / 2 + math.pi, first + half)
    low, high = [], []
    for (p_re, p_im), (m_re, m_im) in zip(plus, minus):
        low.append((p_re + m_re, p_im + m_im))
        high.append(turn(p_re - m_re, p_im - m_im, -theta / 2))
    return low + high


def across(eye, block):
    return lax.dot_general(eye, block, (((1,), (1,)), ((), ())), preferred_element_type=F32)


def crossed(a, b, count):
    total, place = 0, 1
    while place < count:
        total = total + lax.rem(lax.div(a, place) + lax.div(b, place), 2) * place
        place *= 2
    return total


def wave_tables(tok):
    bins = np.arange(tok).reshape(-1, SLOT, 2).transpose(0, 2, 1).reshape(-1)
    angle = (2 * bins + 1)[:, None] * np.arange(tok)[None, :] * (math.pi / (2 * tok))
    there = np.concatenate([np.cos(angle), np.sin(angle)], axis=0)
    return there.astype(ml_dtypes.bfloat16), (there.T / tok).astype(ml_dtypes.bfloat16)


def send_order(n):
    pairs = [(m, m - 1) for m in range(n - 1, 0, -2)]
    return [(6, 7), (4, 2), (5, 3), (1, 0)] if n == 8 else pairs


def wide_kernel(
    n,
    q_hbm, k_hbm, v_hbm, taps_hbm, filt_hbm, gain_hbm, there_hbm, back_hbm,
    out_ref,
    q_ref, source, taps_ref, filt_ref, gain_ref, there_ref, back_ref,
    eye, tails, halo, q_tails, q_halo, turned_a, turned_b, rim, gated, recv, ret, sent,
    wave, filt_wave, sig_wave, out_wave,
    load_sem, rest_sem, q_sem, side_sem, halo_send, halo_recv,
    rim_recv, in_send, in_recv, in_own, out_send, out_recv,
):
    me = lax.axis_index("ctx")
    chunks, lanes, tok = q_hbm.shape[1:]
    reach = taps_hbm.shape[1]
    pairs = n // 2
    step = 16
    half = step // 2
    edge = 16
    part = 64
    order = send_order(n)
    couples = [2, 1, 3, 0] if n == 8 else list(range(pairs - 1, -1, -1))
    later = [(4, 2), (5, 3), (6, 7), (1, 0)] if n == 8 else order

    def code_of(pairs_of, k):
        return jnp.int32(sum(pair[k] * n**i for i, pair in enumerate(pairs_of)))

    barrier = pltpu.get_barrier_semaphore()
    beside = me + 1 - 2 * lax.rem(me, 2)
    pair = me - lax.rem(me, 2)
    for peer in (n - 1 - me, n - 1 - beside):
        pl.semaphore_signal(barrier, inc=1, device_id={"ctx": peer}, device_id_type=MESH)
    for x in range(2, n - 2, 2):
        for peer in (crossed(me, jnp.int32(x), n), crossed(beside, jnp.int32(x), n)):
            pl.semaphore_signal(barrier, inc=1, device_id={"ctx": peer}, device_id_type=MESH)
    pl.semaphore_signal(barrier, inc=1, device_id={"ctx": beside}, device_id_type=MESH)

    def met(m):
        return crossed(me, m, n)

    needed = [m for pair in order for m in pair]

    def load_start(m, slot):
        p = met(jnp.int32(m))
        for w, ref in enumerate((k_hbm, v_hbm)):
            pltpu.make_async_copy(ref.at[p, 0], source.at[0, p, w], load_sem.at[slot]).start()

    def load_wait(m, slot):
        p = met(jnp.int32(m))
        pltpu.make_async_copy(source.at[0, p], source.at[0, p], load_sem.at[slot]).wait()

    def rest(c):
        return [
            pltpu.make_async_copy(ref.at[:, c], source.at[c, :, w], rest_sem.at[c, w])
            for w, ref in enumerate((k_hbm, v_hbm))
        ]

    side = [
        pltpu.make_async_copy(taps_hbm, taps_ref, side_sem.at[0]),
        pltpu.make_async_copy(filt_hbm, filt_ref, side_sem.at[1]),
        pltpu.make_async_copy(gain_hbm, gain_ref, side_sem.at[2]),
        pltpu.make_async_copy(there_hbm, there_ref, side_sem.at[3]),
        pltpu.make_async_copy(back_hbm, back_ref, side_sem.at[4]),
    ]
    load_q = pltpu.make_async_copy(q_hbm, q_ref, q_sem)

    for i, m in enumerate(needed):
        load_start(m, min(i, 3))
        if i == 1:
            side[0].start()
    for c in range(1, chunks):
        for copy in rest(c):
            copy.start()
    for i in (1, 3, 2, 4):
        side[i].start()
    load_q.start()

    size = eye.shape[0]
    row = lax.broadcasted_iota(jnp.int32, (size, size), 0)
    col = lax.broadcasted_iota(jnp.int32, (size, size), 1)
    eye[...] = (row == col).astype(F32).astype(BF16)
    pick_row = lax.broadcasted_iota(jnp.int32, (SLOT, LANES), 0) + (LANES - SLOT)
    pick = (pick_row == lax.broadcasted_iota(jnp.int32, (SLOT, LANES), 1)).astype(F32).astype(BF16)

    def peer_rows(peer, c):
        return pl.ds(pl.multiple_of((peer * chunks + c) * lanes, lanes), lanes)

    def chunk_lanes(c):
        return slice(c * lanes, (c + 1) * lanes)

    @pl.when(me == 0)
    def _():
        halo[...] = jnp.zeros_like(halo)
        q_halo[...] = jnp.zeros_like(q_halo)

    def halo_copy(which):
        mine, theirs = (tails.at[which], halo.at[which]) if which < chunks else (q_tails, q_halo)
        return pltpu.make_async_remote_copy(
            src_ref=mine, dst_ref=theirs, send_sem=halo_send.at[which], recv_sem=halo_recv.at[which],
            device_id={"ctx": lax.rem(me + 1, n)}, device_id_type=MESH,
        )

    def halo_start(which):
        @pl.when(me < n - 1)
        def _():
            halo_copy(which).start()

    def halo_wait(which):
        @pl.when(me < n - 1)
        def _():
            halo_copy(which).wait_send()

        @pl.when(me > 0)
        def _():
            halo_copy(which).wait_recv()

    def find_tails(c):
        def one(p, _):
            block = source[c, p].reshape(2 * lanes, tok)
            tails[c, p] = across(pick, block[:, tok - LANES :]).astype(BF16)
            return 0

        lax.fori_loop(0, n, one, 0, unroll=4)

    def find_q_tails():
        def one(p, _):
            block = q_ref[p].reshape(chunks * lanes, tok)
            q_tails[p] = across(pick, block[:, tok - LANES :]).astype(BF16)
            return 0

        lax.fori_loop(0, n, one, 0, unroll=4)

    def turn(c, m, turned):
        p = met(m)
        both = across(eye[:tok, :tok], source[c, p].reshape(2 * lanes, tok))
        for w in range(2):
            rows = both[:, w * lanes : (w + 1) * lanes]
            turned[w, SLOT:, :] = rows
            if c > 0:
                turned[w, :SLOT, :] = halo[c, p, :, w * lanes : (w + 1) * lanes].astype(F32)
            else:
                rim[w, p, SLOT:, :] = rows[:edge]

    def sums_of(ref, index, taps, start, count):
        total = None
        for j in range(reach):
            at = slice(SLOT - j + start, SLOT - j + start + count)
            term = taps[j : j + 1, :] * ref[(*index, at, slice(None))]
            total = term if total is None else total + term
        return total

    def spans(first):
        marks = [first] + list(range((first // part + 1) * part, tok, part)) + [tok]
        return list(zip(marks[:-1], marks[1:]))

    def gate(c, m, turned):
        p = met(m)
        k_taps, v_taps = (taps_ref[w, :, peer_rows(p, c)] for w in (1, 2))
        for start, stop in spans(0 if c else edge):
            count = stop - start
            product = sums_of(turned, (0,), k_taps, start, count) * sums_of(turned, (1,), v_taps, start, count)
            gated[c, p, start:stop, :] = product.astype(BF16)

    def in_start(c, m):
        peer = met(m)
        at = slice(0 if c else edge, tok)
        pltpu.make_async_remote_copy(
            src_ref=gated.at[c, peer, at, :], dst_ref=recv.at[c, me, at, :],
            send_sem=in_send, recv_sem=in_recv.at[c, lax.div(m, 2)],
            device_id={"ctx": peer}, device_id_type=MESH,
        ).start()

    def rim_start(m):
        peer = met(m)
        pltpu.make_async_remote_copy(
            src_ref=gated.at[0, peer, 0:edge, :], dst_ref=recv.at[0, me, 0:edge, :],
            send_sem=in_send, recv_sem=rim_recv.at[lax.div(m, 2)],
            device_id={"ctx": peer}, device_id_type=MESH,
        ).start()

    def own_in(c):
        return pltpu.make_async_copy(gated.at[c, me], recv.at[c, me], in_own.at[c])

    def out_copy(c, m):
        peer = met(m)
        return pltpu.make_async_remote_copy(
            src_ref=sent.at[c, peer], dst_ref=ret.at[c, me],
            send_sem=out_send, recv_sem=out_recv.at[0 if c == 0 else (c - 1) * (n - 1) + m],
            device_id={"ctx": peer}, device_id_type=MESH,
        )

    def await_bytes(ref, sem):
        pltpu.make_async_copy(ref, ref, sem).wait()

    def gate_chunk(c):
        if c == 0:
            for i, m in enumerate(needed[:3]):
                load_wait(m, i)
            side[0].wait()
        turn(c, jnp.int32((later if c else order)[0][0]), turned_a)

        def one(i, codes):
            a, b = lax.rem(codes[0], n), lax.rem(codes[1], n)
            codes = (lax.div(codes[0], n), lax.div(codes[1], n))
            after = lax.rem(codes[0], n)
            turn(c, b, turned_b)
            gate(c, a, turned_a)
            if c == 0:
                @pl.when(i == 0)
                def _():
                    pl.semaphore_wait(barrier, n - 1)

            in_start(c, a)
            turn(c, after, turned_a)
            gate(c, b, turned_b)

            @pl.when(i < pairs - 1)
            def _():
                in_start(c, b)

            if c == 0:
                @pl.when(i == 0)
                def _():
                    await_bytes(source.at[0, 0 : n - 3], load_sem.at[3])
                    find_tails(0)
                    halo_start(0)

                @pl.when(i == 1)
                def _():
                    for k in range(1, chunks):
                        for copy in rest(k):
                            copy.wait()
                        find_tails(k)
                        halo_start(k)

            return codes

        lax.fori_loop(0, pairs, one, (code_of(later if c else order, 0), code_of(later if c else order, 1)))

    def filter_range(first, last):
        for d in range(first, last):
            both = across(there_ref[...], filt_ref[:, d * tok : (d + 1) * tok])
            for c in range(chunks):
                filt_wave[c, d] = both[:, chunk_lanes(c)]

    def rim_step(p, _):
        sums = []
        for w in range(2):
            rim[w, p, :SLOT, :] = halo[0, p, :, w * lanes : (w + 1) * lanes].astype(F32)
            sums.append(sums_of(rim, (w, p), taps_ref[1 + w, :, peer_rows(p, 0)], 0, edge))
        gated[0, p, :edge, :] = (sums[0] * sums[1]).astype(BF16)
        return 0

    def sig_couple(c, first):
        both = jnp.concatenate([recv[c, first], recv[c, first + 1]], axis=1)
        both = jnp.dot(there_ref[...], both, preferred_element_type=F32)
        sig_wave[first] = both[:, :lanes]
        sig_wave[first + 1] = both[:, lanes:]

    def sig_chunk(c):
        at = slice(0 if c else edge, tok)
        own_in(c).wait()
        await_bytes(recv.at[c, met(jnp.int32(1)), at, :], in_recv.at[c, 0])
        if c == 0:
            await_bytes(recv.at[c, met(jnp.int32(1)), 0:edge, :], rim_recv.at[0])
        sig_couple(c, 2 * lax.div(me, 2))

        def one(x, _):
            first = 2 * lax.div(met(2 * x), 2)
            await_bytes(recv.at[c, pl.ds(first, 2), at, :], in_recv.at[c, x])
            if c == 0:
                await_bytes(recv.at[c, pl.ds(first, 2), 0:edge, :], rim_recv.at[x])
            sig_couple(c, first)
            return 0

        lax.fori_loop(1, pairs, one, 0)

    def blend(c):
        def one(r, _):
            done = []
            for part_of in range(2):
                start = r * step + part_of * half
                re_at = pl.ds(pl.multiple_of(start, half), half)
                im_at = pl.ds(pl.multiple_of(tok + start, half), half)
                f_re = [filt_wave[c, d, re_at, :] for d in range(n)]
                f_im = [filt_wave[c, d, im_at, :] for d in range(n)]
                s_re = [sig_wave[d, re_at, :] for d in range(n)]
                s_im = [sig_wave[d, im_at, :] for d in range(n)]
                rows, past = [], None
                for i in range(n):
                    re = im = None
                    for j in range(i + 1):
                        a, b, x, y = f_re[i - j], f_im[i - j], s_re[j], s_im[j]
                        re = a * x - b * y if re is None else re + a * x - b * y
                        im = a * y + b * x if im is None else im + a * y + b * x
                    if past is None:
                        rows.append((re, im))
                    elif part_of == 0:
                        rows.append((re + past[1], im - past[0]))
                    else:
                        rows.append((re - past[1], im + past[0]))
                    past = (re, im)
                done.append(rows)
            re_at = pl.ds(pl.multiple_of(r * step, step), step)
            im_at = pl.ds(pl.multiple_of(tok + r * step, step), step)
            for i in range(n):
                at = slice((i % 2) * lanes, (i % 2 + 1) * lanes)
                for which, rows_at in enumerate((re_at, im_at)):
                    whole = jnp.concatenate([done[0][i][which], done[1][i][which]], axis=0)
                    out_wave[i // 2, rows_at, at] = whole.astype(BF16)
            return 0

        lax.fori_loop(0, tok // step, one, 0)

    def return_chunk(c):
        gain = gain_ref[:, chunk_lanes(c)]

        def couple_of(x):
            return lax.div(met(2 * x), 2)

        def invert(x, slot):
            wave[slot] = jnp.dot(back_ref[...], out_wave[couple_of(x)], preferred_element_type=F32)

        def finish(x, slot):
            for k in range(2):
                p = 2 * couple_of(x) + k
                both = wave[slot, :, k * lanes : (k + 1) * lanes]
                rows = (both + gain * recv[c, p].astype(F32)).astype(BF16)
                sent[c, p] = across(eye[:lanes, :lanes], rows).astype(BF16)

        invert(jnp.int32(couples[0]), 0)
        for i, x in enumerate(couples):
            if i < pairs - 1:
                invert(jnp.int32(couples[i + 1]), (i + 1) % 2)
            finish(jnp.int32(x), i % 2)
            if x > 0:
                out_copy(c, jnp.int32(2 * x)).start()
            out_copy(c, jnp.int32(2 * x + 1)).start()

    def q_turn(p, turned):
        both = across(eye[:tok, :tok], q_ref[p].reshape(chunks * lanes, tok))
        for c in range(chunks):
            turned[c, SLOT:, :] = both[:, chunk_lanes(c)]
            turned[c, :SLOT, :] = q_halo[p, :, chunk_lanes(c)].astype(F32)

    def q_sums(p, turned):
        for c in range(chunks):
            taps = taps_ref[0, :, peer_rows(p, c)]
            rows = [sums_of(turned, (c,), taps, start, part).astype(BF16) for start in range(0, tok, part)]
            out_ref[peer_rows(p, c), :] = across(eye[:lanes, :lanes], jnp.concatenate(rows, axis=0)).astype(BF16)

    def q_range(first, last):
        q_turn(first, turned_a)

        def one(i, _):
            p = first + 2 * i
            q_turn(p + 1, turned_b)
            q_sums(p, turned_a)
            q_turn(lax.rem(p + 2, n), turned_a)
            q_sums(p + 1, turned_b)
            return 0

        lax.fori_loop(0, (last - first) // 2, one, 0)

    def mix(ref, peer, c):
        at = peer_rows(peer, c)
        out_ref[at, :] = (out_ref[at, :].astype(F32) * ref[c, peer].astype(F32)).astype(BF16)

    def mix_arrived(c, m):
        if c > 0:
            out_copy(c, m).wait_recv()
        mix(ret, met(m), c)

    def mix_chunk(c):
        mix(sent, me, c)
        if c == 0:
            await_bytes(ret.at[0, 0 : n - 1], out_recv.at[0])
        mix_arrived(c, jnp.int32(1))

        for x in couples:
            if x > 0:
                mix_arrived(c, jnp.int32(2 * x))
                mix_arrived(c, jnp.int32(2 * x + 1))

    gate_chunk(0)
    for i in range(1, len(side)):
        side[i].wait()
    early = (3 * n) // 8
    filter_range(0, early)
    halo_wait(0)
    lax.fori_loop(0, n, rim_step, 0, unroll=2)

    def rim_starts(m, _):
        rim_start(m)
        return 0

    lax.fori_loop(1, n, rim_starts, 0)
    own_in(0).start()
    for c in range(1, chunks):
        halo_wait(c)
        gate_chunk(c)
        own_in(c).start()
    filter_range(early, n)
    load_q.wait()
    find_q_tails()
    halo_start(chunks)
    for c in range(chunks):
        sig_chunk(c)
        blend(c)
        return_chunk(c)
        if c == 0:
            halo_wait(chunks)
        q_range(c * n // chunks, (c + 1) * n // chunks)
    await_bytes(gated.at[:, 0 : n - 1], in_send)
    for c in range(chunks):
        mix_chunk(c)
    await_bytes(sent.at[:, 0 : n - 1], out_send)


def kernel(
    n, lanes,
    q_ref, k_ref, v_ref, taps_ref, filt_hbm, gain_ref, table_ref, twist_ref,
    out_hbm,
    out_ref, eye, tails, halo, turned, gated, recv, spec, h_spec, ret, filt_ref, filt_rows, twist,
    filt_sem, halo_sem, in_send, in_recv, in_own, out_send, out_recv, out_own, put,
):
    me = lax.axis_index("ctx")
    width, tok = q_ref.shape
    chan, length = filt_ref.shape
    chunks = chan // lanes
    rim = taps_ref.shape[-2]
    blocks = length // LANES
    tiles = tok // LANES
    sources = (q_ref, k_ref, v_ref)
    step = 16
    filt_copy = pltpu.make_async_copy(filt_hbm, filt_ref, filt_sem)
    filt_copy.start()

    barrier = pltpu.get_barrier_semaphore()
    for d in range(1, n):
        pl.semaphore_signal(barrier, inc=1, device_id={"ctx": lax.rem(me + d, n)}, device_id_type=MESH)

    side = eye.shape[0]
    row = lax.broadcasted_iota(jnp.int32, (side, side), 0)
    col = lax.broadcasted_iota(jnp.int32, (side, side), 1)
    eye[...] = (row == col).astype(F32).astype(BF16)

    pick_row = lax.broadcasted_iota(jnp.int32, (SLOT, LANES), 0) + (LANES - SLOT)
    pick = (pick_row == lax.broadcasted_iota(jnp.int32, (SLOT, LANES), 1)).astype(F32).astype(BF16)

    def tail_step(p, _):
        at = pl.ds(pl.multiple_of(p * chan, chan), chan)
        for w in range(3):
            tails[w, p] = across(pick, sources[w][at, tok - LANES :]).astype(BF16)
        return 0

    lax.fori_loop(0, n, tail_step, 0, unroll=4)

    pl.semaphore_wait(barrier, n - 1)
    halo_copy = pltpu.make_async_remote_copy(
        src_ref=tails, dst_ref=halo, send_sem=halo_sem.at[0], recv_sem=halo_sem.at[1],
        device_id={"ctx": lax.rem(me + 1, n)}, device_id_type=MESH,
    )

    halo_copy.start()
    if lanes < LANES:
        spec[...] = jnp.zeros_like(spec)

    filt_copy.wait()
    for a in range(blocks):
        filt_rows[a // tiles, (a % tiles) * LANES : (a % tiles + 1) * LANES, :] = across(
            eye[:LANES, :LANES], filt_ref[:, a * LANES : (a + 1) * LANES]
        ).astype(BF16)

    def chunk_lanes(c):
        return slice(c * lanes, (c + 1) * lanes)

    def leaf_lanes(leaf):
        return slice((leaf % 2) * LANES, (leaf % 2) * LANES + lanes)

    def short_stage(ref, c, first=False):
        at_lanes = chunk_lanes(c)

        def one(r, _):
            re_at = pl.ds(pl.multiple_of(r * step, step), step)
            im_at = pl.ds(pl.multiple_of(LANES + r * step, step), step)

            def emit(leaf, re, im):
                if first:
                    for which in range(2):
                        column = twist_ref[re_at, which * blocks + leaf : which * blocks + leaf + 1]
                        twist[leaf, which, re_at, :] = jnp.broadcast_to(column, (step, lanes))
                cos, sin = twist[leaf, 0, re_at, :], twist[leaf, 1, re_at, :]
                spec[leaf // 2, re_at, leaf_lanes(leaf)] = (re * cos - im * sin).astype(BF16)
                spec[leaf // 2, im_at, leaf_lanes(leaf)] = (re * sin + im * cos).astype(BF16)

            coefs = []
            for a in range(blocks):
                at = pl.ds(pl.multiple_of((a % tiles) * LANES + r * step, step), step)
                x, lean = ref[a // tiles, at, at_lanes].astype(F32), a * math.pi / (2 * blocks)
                coefs.append((x * math.cos(lean), x * math.sin(lean)))
            split_forward(coefs, 0.0, 0, emit)
            return 0

        lax.fori_loop(0, LANES // step, one, 0)

    def filter_chunk(c):
        short_stage(filt_rows, c, c == 0)

        def filt_pair(pair, _):
            h_spec[c, pair] = jnp.dot(table_ref[0], spec[pair], preferred_element_type=F32).astype(h_spec.dtype)
            return 0

        lax.fori_loop(0, blocks // 2, filt_pair, 0, unroll=2)

    filter_chunk(0)
    halo_copy.wait()

    def peer_rows(peer, c):
        return pl.ds(pl.multiple_of(peer * chan + c * lanes, lanes), lanes)

    def short(first, pair, c):
        block = jnp.concatenate([sources[w][peer_rows(peer, c), :] for w, peer in pair], axis=0)
        both = across(eye[:tok, :tok], block)
        taps = []
        for i, (w, peer) in enumerate(pair):
            turned[first + i, :SLOT, :] = jnp.where(me > 0, halo[w, peer, :, chunk_lanes(c)].astype(F32), 0.0)
            turned[first + i, SLOT:, :] = both[:, i * lanes : (i + 1) * lanes]
            if len(taps_ref.shape) == 3:
                taps.append(taps_ref[w, :, peer_rows(peer, c)])
            else:
                taps.append(taps_ref[peer, w, :, chunk_lanes(c)])
        return taps

    def sums_of(slot, taps, start, count):
        total = None
        for j in range(rim):
            term = taps[j : j + 1, :] * turned[slot, SLOT - j + start : SLOT - j + start + count, :]
            total = term if total is None else total + term
        return total

    part = 64

    def gate_pair(peers, c):
        taps = [short(2 * i, [(1, p), (2, p)], c) for i, p in enumerate(peers)]
        for i, p in enumerate(peers):
            for start in range(0, tok, part):
                product = sums_of(2 * i, taps[i][0], start, part) * sums_of(2 * i + 1, taps[i][1], start, part)
                gated[p, start : start + part, chunk_lanes(c)] = product.astype(BF16)

    def in_copy(c, d):
        peer = lax.rem(me + d, n)
        return pltpu.make_async_remote_copy(
            src_ref=gated.at[peer, :, chunk_lanes(c)], dst_ref=recv.at[me, :, chunk_lanes(c)],
            send_sem=in_send.at[c, d], recv_sem=in_recv.at[c, d],
            device_id={"ctx": peer}, device_id_type=MESH,
        )

    def own_in(c):
        return pltpu.make_async_copy(gated.at[me, :, chunk_lanes(c)], recv.at[me, :, chunk_lanes(c)], in_own.at[c])

    def out_copy(c, d):
        peer = lax.rem(me + d, n)
        return pltpu.make_async_remote_copy(
            src_ref=recv.at[peer, :, chunk_lanes(c)], dst_ref=ret.at[me, :, chunk_lanes(c)],
            send_sem=out_send.at[c, d], recv_sem=out_recv.at[c, d],
            device_id={"ctx": peer}, device_id_type=MESH,
        )

    def own_out(c):
        return pltpu.make_async_copy(recv.at[me, :, chunk_lanes(c)], ret.at[me, :, chunk_lanes(c)], out_own.at[c])

    for c in range(chunks):
        def send_step(i, _):
            gate_pair([lax.rem(me + 2 * i + 1, n), lax.rem(me + 2 * i + 2, n)], c)

            @pl.when(i > 0)
            def _():
                in_copy(c, 2 * i - 1).start()
                in_copy(c, 2 * i).start()

            return 0

        lax.fori_loop(0, n // 2, send_step, 0)
        in_copy(c, n - 1).start()
        own_in(c).start()

    for c in range(1, chunks):
        filter_chunk(c)

    for c in range(chunks):
        def wait_in(d, _):
            in_copy(c, d).wait()
            return 0

        lax.fori_loop(1, n, wait_in, 0)
        own_in(c).wait()
        at_lanes = chunk_lanes(c)
        short_stage(recv, c)

        def pair_step(pair, _):
            sig = jnp.dot(table_ref[0], spec[pair], preferred_element_type=F32)
            h_re, h_im = h_spec[c, pair, :LANES, :].astype(F32), h_spec[c, pair, LANES:, :].astype(F32)
            s_re, s_im = sig[:LANES], sig[LANES:]
            prod = jnp.concatenate([s_re * h_re - s_im * h_im, s_re * h_im + s_im * h_re], axis=0).astype(BF16)
            h_spec[c, pair] = jnp.dot(table_ref[1], prod, preferred_element_type=F32).astype(h_spec.dtype)
            return 0

        lax.fori_loop(0, blocks // 2, pair_step, 0, unroll=4)
        gain = gain_ref[:, at_lanes]

        def back_step(r, _):
            re_at = pl.ds(pl.multiple_of(r * step, step), step)
            im_at = pl.ds(pl.multiple_of(LANES + r * step, step), step)
            def fetch(leaf):
                re = h_spec[c, leaf // 2, re_at, leaf_lanes(leaf)].astype(F32)
                im = h_spec[c, leaf // 2, im_at, leaf_lanes(leaf)].astype(F32)
                cos, sin = twist[leaf, 0, re_at, :], twist[leaf, 1, re_at, :]
                return re * cos + im * sin, im * cos - re * sin

            parts = split_inverse(fetch, blocks, 0.0, 0)
            for a, (re, im) in enumerate(parts):
                lean = a * math.pi / (2 * blocks)
                cos, sin = math.cos(lean) / length, math.sin(lean) / length
                at = pl.ds(pl.multiple_of((a % tiles) * LANES + r * step, step), step)
                sig = recv[a // tiles, at, at_lanes].astype(F32)
                recv[a // tiles, at, at_lanes] = (cos * re + sin * im + gain * sig).astype(BF16)
            return 0

        lax.fori_loop(0, LANES // step, back_step, 0)

        def return_step(d, _):
            out_copy(c, d).start()
            return 0

        lax.fori_loop(1, n, return_step, 0)
        own_out(c).start()

    for c in range(chunks):
        def q_step(i, _):
            peers = (2 * i, 2 * i + 1)
            taps = short(0, [(0, p) for p in peers], c)
            for slot, p in enumerate(peers):
                parts = [sums_of(slot, taps[slot], start, part).astype(BF16) for start in range(0, tok, part)]
                out_ref[peer_rows(p, c), :] = across(eye[:lanes, :lanes], jnp.concatenate(parts, axis=0)).astype(BF16)
            return 0

        lax.fori_loop(0, n // 2, q_step, 0)

    def mix(peer, c):
        at = peer_rows(peer, c)
        long = across(eye[:lanes, :lanes], ret[peer, :, chunk_lanes(c)])
        out_ref[at, :] = (out_ref[at, :].astype(F32) * long).astype(BF16)
        put_copy(peer, c).start()

    def put_copy(peer, c):
        at = peer_rows(peer, c)
        return pltpu.make_async_copy(out_ref.at[at, :], out_hbm.at[at, :], put.at[c, peer])

    for c in range(chunks):
        own_out(c).wait()
        mix(me, c)

        def mix_step(d, _):
            out_copy(c, d).wait()
            mix(lax.rem(me + n - d, n), c)
            return 0

        lax.fori_loop(1, n, mix_step, 0)

    for c in range(chunks):
        def put_step(p, _):
            put_copy(p, c).wait()
            return 0

        lax.fori_loop(0, n, put_step, 0)


def wide_call(n, queries, keys, values, taps, filters, gain):
    width, tok = queries.shape
    chan, length = filters.shape
    chunks = chan // LANES
    reach = taps.shape[1]
    dma = pltpu.SemaphoreType.DMA
    there, back = wave_tables(tok)
    cut = [x.reshape(n, chunks, LANES, tok) for x in (queries, keys, values)]
    held = [
        pltpu.with_memory_space_constraint(x, pltpu.HBM)
        for x in (*cut, taps, filters, gain, jnp.asarray(there), jnp.asarray(back))
    ]
    return pl.pallas_call(
        functools.partial(wide_kernel, n),
        out_shape=pltpu.VMEM((width, tok), BF16),
        in_specs=[pl.BlockSpec(memory_space=pltpu.HBM)] * 8,
        out_specs=pl.BlockSpec(memory_space=pltpu.VMEM),
        scratch_shapes=[
            pltpu.VMEM((n, chunks, LANES, tok), BF16),
            pltpu.VMEM((chunks, n, 2, LANES, tok), BF16),
            pltpu.VMEM((3, reach, width), F32),
            pltpu.VMEM((chan, length), BF16),
            pltpu.VMEM((1, chan), F32),
            pltpu.VMEM(there.shape, BF16),
            pltpu.VMEM(back.shape, BF16),
            pltpu.VMEM((tok, tok), BF16),
            pltpu.VMEM((chunks, n, SLOT, 2 * LANES), BF16),
            pltpu.VMEM((chunks, n, SLOT, 2 * LANES), BF16),
            pltpu.VMEM((n, SLOT, chan), BF16),
            pltpu.VMEM((n, SLOT, chan), BF16),
            pltpu.VMEM((2, SLOT + tok, LANES), F32),
            pltpu.VMEM((2, SLOT + tok, LANES), F32),
            pltpu.VMEM((2, n, SLOT + 16, LANES), F32),
            pltpu.VMEM((chunks, n, tok, LANES), BF16),
            pltpu.VMEM((chunks, n, tok, LANES), BF16),
            pltpu.VMEM((chunks, n, LANES, tok), BF16),
            pltpu.VMEM((chunks, n, LANES, tok), BF16),
            pltpu.VMEM((2, tok, 2 * LANES), F32),
            pltpu.VMEM((chunks, n, 2 * tok, LANES), F32),
            pltpu.VMEM((n, 2 * tok, LANES), F32),
            pltpu.VMEM((n // 2, 2 * tok, 2 * LANES), BF16),
            dma((4,)),
            dma((chunks, 2)),
            dma,
            dma((5,)),
            dma((chunks + 1,)),
            dma((chunks + 1,)),
            dma((n // 2,)),
            dma,
            dma((chunks, n // 2)),
            dma((chunks,)),
            dma,
            dma(((chunks - 1) * (n - 1) + 1,)),
        ],
        compiler_params=pltpu.CompilerParams(
            collective_id=0, has_side_effects=True, vmem_limit_bytes=40 * 2**20
        ),
        name="hyena",
    )(*held)


def solution(mesh):
    n = mesh.shape["ctx"]

    def local(queries, keys, values, short_taps, long_filter, skip_gain):
        width, tok = queries.shape
        chan, length = long_filter.shape[1:]
        blocks = length // LANES
        lanes = min(chan, LANES)
        chunks = chan // lanes
        if n in (4, 8) and chan == 2 * LANES and tok == 2 * LANES and length == n * tok and width == n * chan:
            return wide_call(n, queries, keys, values, short_taps, long_filter[0], skip_gain)
        table = jnp.asarray(circle_tables())
        twist = jnp.asarray(twist_columns(blocks))
        dma = pltpu.SemaphoreType.DMA
        two = 2 * LANES
        small = blocks * two * max(chan, LANES) * 4 <= 8 * 2**20
        side = max(tok, LANES)
        any_space = pl.BlockSpec(memory_space=pl.ANY)
        taps = short_taps
        if lanes < LANES:
            taps = jnp.moveaxis(short_taps.reshape(3, -1, n, chan), 2, 0)
        return pl.pallas_call(
            functools.partial(kernel, n, lanes),
            out_shape=jax.ShapeDtypeStruct((width, tok), BF16),
            in_specs=[any_space if i == 4 else pl.BlockSpec(memory_space=pltpu.VMEM) for i in range(8)],
            out_specs=any_space,
            scratch_shapes=[
                pltpu.VMEM((width, tok), BF16),
                pltpu.VMEM((side, side), BF16),
                pltpu.VMEM((3, n, SLOT, chan), BF16),
                pltpu.VMEM((3, n, SLOT, chan), BF16),
                pltpu.VMEM((4, SLOT + tok, lanes), F32),
                pltpu.VMEM((n, tok, chan), BF16),
                pltpu.VMEM((n, tok, chan), BF16),
                pltpu.VMEM((blocks // 2, two, two), BF16),
                pltpu.VMEM((chunks, blocks // 2, two, two), F32 if small else BF16),
                pltpu.VMEM((n, tok, chan), BF16),
                pltpu.VMEM((chan, length), BF16),
                pltpu.VMEM((n, tok, chan), BF16),
                pltpu.VMEM((blocks, 2, LANES, lanes), F32),
                dma,
                dma((2,)),
                dma((chunks, n)),
                dma((chunks, n)),
                dma((chunks,)),
                dma((chunks, n)),
                dma((chunks, n)),
                dma((chunks,)),
                dma((chunks, n)),
            ],
            compiler_params=pltpu.CompilerParams(
                collective_id=0, has_side_effects=True, vmem_limit_bytes=67043328
            ),
            name="hyena",
        )(queries, keys, values, taps, long_filter[0], skip_gain, table, twist)

    placed = (
        P("ch", "ctx"),
        P("ch", "ctx"),
        P("ch", "ctx"),
        P(None, None, "ch"),
        P("ch", "ctx", None),
        P("ch", "ctx"),
    )
    return jax.shard_map(local, mesh=mesh, in_specs=placed, out_specs=P("ch", "ctx"), check_vma=False)
```
